32 devices in a mesh: fx: 2 (over y), fy: 4 (over x, core), st: 4 (over z).
Axes of the slice: x: 2, y: 2, z: 4, core: 2. Of those that a mesh axis runs over, the one named last changes fastest.
Arguments:
- tangent_rhs: bfloat16 [4, 6, 64, 2, 4, 128], P('st', None, None, 'fx', 'fy'), may hold values from -6 to 6
- adjoint_rhs: bfloat16 [4, 6, 64, 2, 4, 128], P('st', None, None, 'fx', 'fy'), may hold values from -6 to 6
- jacobians: bfloat16 [3, 6, 6, 2, 4, 128], P(None, None, None, 'fx', 'fy'), may hold values from -0.75 to 0.75
- deriv: bfloat16 [3, 64, 64], replicated, may hold values from -0.75 to 0.75
- penalty: float32 [6], replicated, may hold values from 0.1 to 0.4
- second_order: float32 [6, 2, 4, 128], P(None, 'fx', 'fy'), may hold values from -4 to 4
- coupling: bfloat16 [6, 384], replicated, may hold values from -2.5 to 2.5
- shell_inverse: bfloat16 [16, 384, 384], P('st')
- shell_load: float32 [4, 16, 384], P(None, 'st'), may hold values from -6 to 6
- shell_adjoint_rhs: float32 [4, 16, 384], P(None, 'st'), may hold values from -6 to 6
- iface_elem: int32 [8, 128], P(('fx', 'fy')), may hold values from 0 to 127
- iface_node: int32 [8, 128], P(('fx', 'fy')), may hold values from 0 to 1023
- iface_weight: float32 [8, 128], P(('fx', 'fy')), may hold values from 0.5 to 2
- iface_count: int32 [8], P(('fx', 'fy')), may hold values from 0 to 128, as said below
Outputs:
- tangent_flow: bfloat16 [4, 6, 64, 2, 4, 128], P('st', None, None, 'fx', 'fy')
- adjoint_flow: bfloat16 [4, 6, 64, 2, 4, 128], P('st', None, None, 'fx', 'fy')
- shell_tangent: float32 [4, 16, 384], P(None, 'st')
- shell_adjoint: float32 [4, 16, 384], P(None, 'st')
The draws below stay inside these ranges and needn't reach their ends.
Inputs may be any that keep to these rules, and one draw needn't show every extreme that they name: `iface_count`: at most 128 live slots in one flow block; some block has exactly 128.
All inputs are finite; a program needn't handle non-finite values.
Results may differ from the reference program's by a relative error of at most 0.0069.
Values may be sent and summed in bfloat16 or wider, within the bound.
No kernel may reach another device: no remote copies, remote signals or barrier semaphores. Data moves between devices by JAX's collectives and lax.ppermute only.
A program may use at most 64 MiB of HBM per device.

```python
import math
import jax
import jax.numpy as jnp
from jax import lax

NV = 6
NP = 64
NDIR = 4
SDOF = 6
PN = 64
BX = 1
BY = 1
BZ = 128
CAP = 128
FSWEEP = 3
ROUNDS = 2
NBX = 2
NBY = 4
NPAN = 16
NSHELL = 1024
NFLOW = 8
N_FY = 4


def draw_shell_inverse(key, part):
    panel_width = SDOF * PN
    perturbation = jax.random.normal(key, (NPAN, panel_width, panel_width), jnp.float32) * (0.5 / math.sqrt(panel_width))
    return (jnp.eye(panel_width, dtype=jnp.float32)[None] + perturbation).astype(jnp.bfloat16)


def draw_iface_count(key, part):
    first_key, second_key = jax.random.split(jax.random.fold_in(key, 17))
    counts = jax.random.randint(first_key, (NFLOW,), 0, CAP + 1, dtype=jnp.int32)
    busiest = jax.random.randint(second_key, (), 0, NFLOW, dtype=jnp.int32)
    return counts.at[busiest].set(CAP)


def touch_ends(values, stream_key, low, largest):
    dims = values.shape
    place = [jax.random.randint(jax.random.fold_in(stream_key, axis), (), 0, dims[axis]) for axis in range(len(dims))]
    values = values.at[tuple(place)].set(low)
    longest = dims.index(max(dims))
    place[longest] = (place[longest] + 1) % dims[longest]
    return values.at[tuple(place)].set(largest)


def levels(stream_key, dims, pieces, low, largest):
    loudness = 1.0
    for position, shards_of in pieces:
        draws = jax.random.uniform(jax.random.fold_in(jax.random.fold_in(stream_key, 6), position), (shards_of,), jnp.float32, low / len(pieces), largest / len(pieces))
        loudness = loudness * jnp.repeat(jnp.exp(draws), dims[position] // shards_of).reshape((-1,) + (1,) * (len(dims) - 1 - position))
    return loudness


def centred(stream_key, dims, spread, most, cuts=(), held_as=jnp.bfloat16):
    gain = levels(stream_key, dims, cuts, -0.22, 0.18) if cuts else 1.0
    values = jax.random.normal(stream_key, dims, jnp.float32) * spread * gain
    return jnp.minimum(jnp.maximum(values, -most), most).astype(held_as)


def setup_inputs(seed: int = 0) -> dict:
    keys = jax.random.split(jax.random.key(seed), 15)
    tangent_rhs = centred(keys[0], (NDIR, NV, NP, NBX, NBY, BZ), 1.0, 6.0, ((0, 4), (3, 2), (4, 4)))
    adjoint_rhs = centred(keys[1], (NDIR, NV, NP, NBX, NBY, BZ), 1.0, 6.0, ((0, 4), (3, 2), (4, 4)))
    jacobians = centred(keys[2], (3, NV, NV, NBX, NBY, BZ), (12 * NV) ** -0.5, 0.75, ((3, 2), (4, 4)))
    deriv = centred(keys[3], (3, NP, NP), NP ** -0.5, 0.75)
    penalty = jnp.clip(jnp.exp(jax.random.uniform(keys[4], (NV,), jnp.float32, math.log(0.1), math.log(0.4))), 0.1, 0.4)
    second_order = centred(keys[5], (NV, NBX, NBY, BZ), 0.5, 4.0, ((1, 2), (2, 4)), jnp.float32)
    coupling = centred(keys[6], (SDOF, NV * NP), SDOF ** -0.5, 2.5)
    shell_inverse = draw_shell_inverse(jax.random.fold_in(keys[14], 71), 0)
    shell_load = centred(keys[8], (NDIR, NPAN, SDOF * PN), 1.0, 6.0, ((1, 4),), jnp.float32)
    shell_adjoint_rhs = centred(keys[9], (NDIR, NPAN, SDOF * PN), 1.0, 6.0, ((1, 4),), jnp.float32)
    iface_elem = touch_ends(jax.random.randint(keys[10], (NFLOW, CAP), 0, BX * BY * BZ), jax.random.fold_in(keys[10], 1), 0, (BX * BY * BZ) - 1).astype(jnp.int32)
    iface_node = touch_ends(jax.random.randint(keys[11], (NFLOW, CAP), 0, NSHELL), jax.random.fold_in(keys[11], 1), 0, NSHELL - 1).astype(jnp.int32)
    iface_weight = jnp.clip(jnp.exp(math.log(2.0) - 1.3862944 * jax.random.uniform(keys[12], (NFLOW, CAP), jnp.float32) ** levels(keys[12], (NFLOW, CAP), ((0, 8),), -0.2, 0.2)), 0.5, 2.0)
    iface_count = draw_iface_count(jax.random.fold_in(keys[14], 71), 0)
    return {"tangent_rhs": tangent_rhs, "adjoint_rhs": adjoint_rhs, "jacobians": jacobians, "deriv": deriv, "penalty": penalty, "second_order": second_order, "coupling": coupling, "shell_inverse": shell_inverse, "shell_load": shell_load, "shell_adjoint_rhs": shell_adjoint_rhs, "iface_elem": iface_elem, "iface_node": iface_node, "iface_weight": iface_weight, "iface_count": iface_count}


SIGMA = 0.5
HIGHEST = lax.Precision.HIGHEST


def face_pair(lower_face, upper_face, below, above, axis):
    length = lower_face.shape[axis]
    beyond_upper = jnp.concatenate([lax.slice_in_dim(lower_face, 1, length, axis=axis), above], axis=axis)
    beyond_lower = jnp.concatenate([below, lax.slice_in_dim(upper_face, 0, length - 1, axis=axis)], axis=axis)
    return lower_face - beyond_lower, upper_face - beyond_upper


def place_faces(jump_low, jump_high, axis):
    middle_shape = list(jump_low.shape)
    middle_shape.insert(axis, 2)
    middle = jnp.zeros(middle_shape, jump_low.dtype)
    return jnp.concatenate([jnp.expand_dims(jump_low, axis), middle, jnp.expand_dims(jump_high, axis)], axis=axis)


def flow_jumps(values):
    members, variables, points, size_x, size_y, size_z = values.shape
    cube = values.reshape(members, variables, 4, 4, 4, size_x, size_y, size_z)
    result = jnp.zeros(cube.shape, values.dtype)
    for node_axis in (2, 3, 4):
        elem_axis = node_axis + 2
        lower_face = jnp.take(cube, 0, axis=node_axis)
        upper_face = jnp.take(cube, 3, axis=node_axis)
        border = jnp.zeros_like(lax.slice_in_dim(lower_face, 0, 1, axis=elem_axis))
        jump_low, jump_high = face_pair(lower_face, upper_face, border, border, elem_axis)
        result = result + place_faces(jump_low, jump_high, node_axis)
    return result.reshape(values.shape)


def volume(values, deriv_mats, jac_mats):
    result = jnp.zeros(values.shape, jnp.float32)
    for axis_index in range(3):
        grads = jnp.einsum('pq,vqxyz->vpxyz', deriv_mats[axis_index].astype(jnp.float32),
                           values.astype(jnp.float32), precision=HIGHEST)
        for variable in range(values.shape[0]):
            result = result + jac_mats[axis_index][:, variable, None] * grads[variable][None]
    return result


def operator(state, deriv_mats, jac_mats, penalty):
    values = lax.optimization_barrier(state.astype(jnp.bfloat16))
    jumps = flow_jumps(values.astype(jnp.float32)[None])[0]
    return state + volume(values, deriv_mats, jac_mats) + penalty[:, None, None, None, None] * jumps


def shell_solve(shell_inverse, rhs):
    rounded = lax.optimization_barrier(rhs.astype(jnp.bfloat16))
    return jnp.einsum('pab,dpb->dpa', shell_inverse.astype(jnp.float32), rounded.astype(jnp.float32),
                      precision=HIGHEST)


def reference(tangent_rhs, adjoint_rhs, jacobians, deriv, penalty, second_order, coupling, shell_inverse,
              shell_load, shell_adjoint_rhs, iface_elem, iface_node, iface_weight, iface_count):
    flow_count, slots = iface_elem.shape
    slot_index = jnp.arange(slots, dtype=jnp.int32)
    live = (slot_index[None, :] < iface_count[:, None]).astype(jnp.float32)
    weights = (iface_weight * live).reshape(-1)
    block = jnp.arange(flow_count, dtype=jnp.int32)[:, None]
    block_x = block // N_FY
    block_y = block % N_FY
    local_x = iface_elem // (BY * BZ)
    local_y = (iface_elem // BZ) % BY
    local_z = iface_elem % BZ
    global_elem = (((block_x * BX + local_x) * NBY + block_y * BY + local_y) * BZ + local_z).reshape(-1).astype(jnp.int32)
    dof_rows = jnp.arange(SDOF, dtype=jnp.int32)[:, None]
    nodes = iface_node.reshape(-1)[None, :]
    columns = ((nodes // PN) * (SDOF * PN) + dof_rows * PN + nodes % PN).astype(jnp.int32)
    field_shape = tangent_rhs.shape[1:]
    elements = NBX * NBY * BZ
    coupling32 = coupling.astype(jnp.float32)
    forward_deriv = deriv
    backward_deriv = jnp.swapaxes(deriv, 1, 2)
    forward_jac = jacobians.astype(jnp.float32)
    backward_jac = jnp.swapaxes(forward_jac, 1, 2)

    shell_tangent = shell_solve(shell_inverse, shell_load)
    tangent = [jnp.zeros(field_shape, jnp.float32) for direction in range(NDIR)]
    adjoint = [jnp.zeros(field_shape, jnp.float32) for direction in range(NDIR)]
    shell_adjoint = jnp.zeros(shell_load.shape, jnp.float32)
    for round_index in range(ROUNDS):
        shell_b = lax.optimization_barrier(shell_tangent.astype(jnp.bfloat16)).reshape(NDIR, -1)
        new_tangent = []
        new_adjoint = []
        load_rows = []
        for direction in range(NDIR):
            picked = shell_b[direction][columns].astype(jnp.float32)
            pushed_cols = jnp.einsum('jc,js->cs', coupling32, picked, precision=HIGHEST) * weights[None, :]
            pushed = jnp.zeros((NV * NP, elements), jnp.float32).at[:, global_elem].add(pushed_cols)
            force = tangent_rhs[direction].astype(jnp.float32) - pushed.reshape(field_shape)
            source = adjoint_rhs[direction].astype(jnp.float32) + second_order[:, None] * tangent[direction]
            state = tangent[direction]
            for sweep in range(FSWEEP):
                state = state + SIGMA * (force - operator(state, forward_deriv, forward_jac, penalty))
            new_tangent.append(state)
            state = adjoint[direction]
            for sweep in range(FSWEEP):
                state = state + SIGMA * (source - operator(state, backward_deriv, backward_jac, penalty))
            new_adjoint.append(state)
            rounded = lax.optimization_barrier(state.astype(jnp.bfloat16)).reshape(NV * NP, elements)
            gathered = rounded[:, global_elem].astype(jnp.float32)
            loads = jnp.einsum('jc,cs->js', coupling32, gathered, precision=HIGHEST) * weights[None, :]
            load_rows.append(jnp.zeros((NPAN * SDOF * PN,), jnp.float32).at[columns].add(loads))
        tangent = new_tangent
        adjoint = new_adjoint
        summed = jnp.stack(load_rows).reshape(shell_load.shape)
        shell_adjoint = shell_solve(shell_inverse, shell_adjoint_rhs - summed)
        shell_tangent = shell_solve(shell_inverse, shell_load + shell_adjoint)
    tangent_flow = jnp.stack(tangent).astype(jnp.bfloat16)
    adjoint_flow = jnp.stack(adjoint).astype(jnp.bfloat16)
    return (tangent_flow, adjoint_flow, shell_tangent, shell_adjoint)
```

```python
import functools

import jax
import jax.numpy as jnp
from jax import lax
from jax.experimental import pallas as pl
from jax.experimental.pallas import tpu as pltpu
from jax.sharding import PartitionSpec as P

SDOF = 6
PN = 64
NP = 64
FSWEEP = 3
ROUNDS = 2
LANES = 128
KERNEL_VMEM = 32 * 1024 * 1024
F32 = jnp.float32
BF16 = jnp.bfloat16


SIGMA = 0.5


def with_halo(value, sides, width):
    for axis, dim in sides:
        peers, length = (lax.axis_size(axis), value.shape[dim])
        up = [(i, (i + 1) % peers) for i in range(peers - 1)]
        down = [(j, i) for i, j in up]
        last = lax.slice_in_dim(value, length - width, length, axis=dim)
        initial = lax.slice_in_dim(value, 0, width, axis=dim)
        before = lax.ppermute(last, axis, up)
        after = lax.ppermute(initial, axis, down)
        value = jnp.concatenate([before, value, after], axis=dim)
    return value


def face_pair(lower_face, upper_face, below, above, axis):
    length = lower_face.shape[axis]
    beyond_upper = jnp.concatenate(
        [lax.slice_in_dim(lower_face, 1, length, axis=axis), above], axis=axis
    )
    beyond_lower = jnp.concatenate(
        [below, lax.slice_in_dim(upper_face, 0, length - 1, axis=axis)], axis=axis
    )
    return (lower_face - beyond_lower, upper_face - beyond_upper)


def place_faces(jump_low, jump_high, axis):
    middle_shape = list(jump_low.shape)
    middle_shape.insert(axis, 2)
    middle = jnp.zeros(middle_shape, jump_low.dtype)
    return jnp.concatenate(
        [jnp.expand_dims(jump_low, axis), middle, jnp.expand_dims(jump_high, axis)], axis=axis
    )


def as_cube(values):
    members, variables, points, size_x, size_y, size_z = values.shape
    return values.reshape(members, variables, 4, 4, 4, size_x, size_y, size_z)


def face_edges(values):
    cube = as_cube(values)
    received = []
    for node_axis in (2, 3):
        elem_axis = node_axis + 2
        lower_face = jnp.take(cube, 0, axis=node_axis)
        upper_face = jnp.take(cube, 3, axis=node_axis)
        edges = jnp.concatenate([lower_face, upper_face], axis=elem_axis)
        if node_axis == 2:
            extended = with_halo(edges, (("fx", 4),), 1)
        else:
            extended = with_halo(edges, (("fy", 5),), 1)
        below = lax.slice_in_dim(extended, 0, 1, axis=elem_axis)
        above = lax.slice_in_dim(extended, 3, 4, axis=elem_axis)
        received.append((below, above))
    return received


def flow_jumps(values, received):
    cube = as_cube(values)
    result = jnp.zeros(cube.shape, jnp.float32)
    for node_axis in (2, 3, 4):
        elem_axis = node_axis + 2
        lower_face = jnp.take(cube, 0, axis=node_axis).astype(jnp.float32)
        upper_face = jnp.take(cube, 3, axis=node_axis).astype(jnp.float32)
        if received is None or node_axis == 4:
            below = jnp.zeros_like(lax.slice_in_dim(lower_face, 0, 1, axis=elem_axis))
            above = below
        else:
            below = received[node_axis - 2][0].astype(jnp.float32)
            above = received[node_axis - 2][1].astype(jnp.float32)
        jump_low, jump_high = face_pair(lower_face, upper_face, below, above, elem_axis)
        result = result + place_faces(jump_low, jump_high, node_axis)
    return result.reshape(values.shape)


def volume(values, deriv_mats, jac_mats):
    grads = jnp.einsum("kpq,vqxyz->kvpxyz", deriv_mats, values, preferred_element_type=jnp.float32)
    result = jnp.sum(jac_mats[0][:, :, None] * grads[0][None], axis=1)
    for axis_index in (1, 2):
        result = result + jnp.sum(
            jac_mats[axis_index][:, :, None] * grads[axis_index][None], axis=1
        )
    return result


def operator(states, operator_kinds, penalty):
    values = lax.optimization_barrier(states.astype(jnp.bfloat16))
    received = face_edges(values)
    jumps = flow_jumps(values, received)
    volumes = jnp.stack(
        [
            volume(values[member], operator_kinds[member][0], operator_kinds[member][1])
            for member in range(len(operator_kinds))
        ]
    )
    return states + volumes + penalty[None, :, None, None, None, None] * jumps


def halo_body(
    tangent_rhs,
    adjoint_rhs,
    jacobians,
    deriv,
    penalty,
    second_order,
    coupling,
    shell_inverse,
    shell_load,
    shell_adjoint_rhs,
    iface_elem,
    iface_node,
    iface_weight,
    iface_count,
):
    state_shape = tangent_rhs.shape
    variables = state_shape[1]
    points = state_shape[2]
    elements = state_shape[3] * state_shape[4] * state_shape[5]
    slots = iface_elem.shape[1]
    live = (jnp.arange(slots, dtype=jnp.int32) < iface_count[0]).astype(jnp.float32)
    weights = iface_weight[0] * live
    elem_index = iface_elem[0]
    node_index = iface_node[0]
    dof_rows = jnp.arange(SDOF, dtype=jnp.int32)[:, None]
    columns = (node_index // PN)[None, :] * (SDOF * PN) + dof_rows * PN + (node_index % PN)[None, :]
    forward_jac = jacobians.astype(jnp.float32)
    forward_kind = (deriv, forward_jac)
    backward_kind = (jnp.swapaxes(deriv, 1, 2), jnp.swapaxes(forward_jac, 1, 2))
    coupling_cols = coupling.T

    def shell_solve(rhs):
        return jnp.einsum(
            "pab,dpb->dpa",
            shell_inverse,
            rhs.astype(jnp.bfloat16),
            preferred_element_type=jnp.float32,
        )

    shell_tangent = shell_solve(shell_load)
    shell_adjoint = jnp.zeros(shell_load.shape, jnp.float32)
    tangent = jnp.zeros(state_shape, jnp.float32)
    adjoint = jnp.zeros(state_shape, jnp.float32)
    for round_index in range(ROUNDS):
        received = lax.all_to_all(
            shell_tangent.astype(jnp.bfloat16), "st", split_axis=0, concat_axis=1, tiled=True
        )
        picked = received.reshape(-1)[columns]
        pushed_cols = (
            jnp.dot(coupling_cols, picked, preferred_element_type=jnp.float32) * weights[None, :]
        )
        pushed = (
            jnp.zeros((variables * points, elements), jnp.float32)
            .at[:, elem_index]
            .add(pushed_cols)
        )
        force = tangent_rhs.astype(jnp.float32) - pushed.reshape(state_shape)
        adjoint_source = adjoint_rhs.astype(jnp.float32) + second_order[None, :, None] * tangent
        paired = jnp.concatenate([tangent, adjoint])
        sources = jnp.concatenate([force, adjoint_source])
        for sweep in range(FSWEEP):
            paired = paired + SIGMA * (
                sources - operator(paired, (forward_kind, backward_kind), penalty)
            )
        tangent = paired[:1]
        adjoint = paired[1:]
        adjoint_values = adjoint.astype(jnp.bfloat16).reshape(variables * points, elements)
        gathered = adjoint_values[:, elem_index]
        loads = jnp.dot(coupling, gathered, preferred_element_type=jnp.float32) * weights[None, :]
        panels = received.shape[1]
        partial_loads = jnp.zeros((panels * SDOF * PN,), jnp.float32).at[columns].add(loads)
        partial_loads = partial_loads.reshape(1, panels, SDOF * PN)
        summed = lax.psum(partial_loads, ("fx", "fy"))
        owned = lax.all_to_all(summed, "st", split_axis=1, concat_axis=0, tiled=True)
        shell_adjoint = shell_solve(shell_adjoint_rhs - owned)
        shell_tangent = shell_solve(shell_load + shell_adjoint)
    return (
        tangent.astype(jnp.bfloat16),
        adjoint.astype(jnp.bfloat16),
        shell_tangent,
        shell_adjoint,
    )


def _iota(shape, dim):
    return lax.broadcasted_iota(jnp.int32, shape, dim)


def _flag(cond):
    return jnp.where(cond, 1.0, 0.0)


def _nt(a, b):
    return lax.dot_general(a, b, (((1,), (1,)), ((), ())), preferred_element_type=F32)


def _nn(a, b):
    return lax.dot_general(a, b, (((1,), (0,)), ((), ())), preferred_element_type=F32)


def _tn(a, b):
    return lax.dot_general(a, b, (((0,), (0,)), ((), ())), preferred_element_type=F32)


def _split(x):
    high = x.astype(BF16)
    low = (x - high.astype(F32)).astype(BF16)
    return jnp.concatenate([high, low], axis=0)


def _fold(x):
    half = x.shape[0] // 2
    return x[:half] + x[half:]


def _roll(x, shift):
    shift = shift % LANES
    return x if shift == 0 else pltpu.roll(x, shift, 1)


class Plan:
    def __init__(self, nx, ny, ns, nv, span, panels, width):
        self.nx, self.ny, self.ns, self.nv = nx, ny, ns, nv
        self.span, self.panels, self.width = span, panels, width
        self.groups = nx * ny
        self.own = span // self.groups
        self.window = LANES // ny
        self.halo = (self.window - self.own) // 2
        self.held = panels // ns
        self.nodes = panels * PN
        self.tiles = width // LANES
        self.narrow = LANES // self.groups
        self.deps = 3 * nv * nv
        self.granules = 3 * nv + 1
        self.per = -(-self.granules // 4)
        self.field_rows = nv * 16
        self.rows = 2 * self.field_rows + self.per * 8 + 8
        self.depth = 7 * NP + 32
        self.slots = ny * LANES

    def rank(self):
        return lax.axis_index("fx") * self.ny + lax.axis_index("fy")


def fits(nx, ny, ns, local_shape, slots, panels, width):
    members, nv, points, size_x, size_y, span = local_shape
    groups = nx * ny
    if members != 1 or (size_x, size_y) != (1, 1) or points != NP or nv > 8 or nv % 2:
        return False
    if span != LANES or slots != LANES or span % groups or LANES % ny or LANES % groups:
        return False
    own, window = span // groups, LANES // ny
    if window * 4 != LANES or (window - own) % 2 or (window - own) // 2 < ROUNDS * FSWEEP - 1:
        return False
    if own * 8 != LANES or width != SDOF * PN or width % LANES or SDOF > 8:
        return False
    held = panels // ns
    if panels % ns or panels != 16 or groups % held or ns > 4:
        return False
    return (held + 1) * (width // LANES) <= 16 and 8 % held == 0


def shell_solve_rows(plan, rhs, inverse_ref):
    rows = rhs.shape[0]
    rounded = rhs.astype(BF16)
    member = _iota((rows, plan.width), 0) % plan.held
    result = jnp.zeros((rows, plan.width), F32)
    for panel in range(plan.held):
        result = jnp.where(member == panel, _nt(rounded, inverse_ref[panel]), result)
    return result


def stacked(ref, count):
    return jnp.concatenate([ref[d] for d in range(count)], axis=0)


def pack_kernel(plan, trhs, arhs, jac, second, elem, node, weight, count, out, scr):
    nv, window = plan.nv, plan.window
    lane = _iota((1, LANES), 1)
    masks = []
    for dest in range(plan.groups):
        start = plan.own * dest - plan.halo
        row = []
        for k in range(4):
            z = start + lane % window
            row.append(_flag((lane // window == k) & (z >= 0) & (z < plan.span)))
        masks.append(row)

    def window_of(parts, dest, dtype):
        start = plan.own * dest - plan.halo
        total = None
        for k in range(4):
            term = _roll(parts[k], window * k - start) * masks[dest][k].astype(dtype)
            total = term if total is None else total + term
        return total

    for f, ref in enumerate((trhs, arhs)):
        for a in range(nv):
            parts = [ref[a, pl.ds(16 * k, 16), :] for k in range(4)]
            for dest in range(plan.groups):
                out[dest, pl.ds((f * nv + a) * 16, 16), :] = window_of(parts, dest, BF16)

    scr[...] = jnp.zeros(scr.shape, F32)
    for k in range(3):
        for a in range(nv):
            scr[k * nv + a, 0:nv, :] = jac[k, a].astype(F32)
    for a in range(nv):
        scr[3 * nv, a : a + 1, :] = second[a]
    quarter = [
        scr[pl.ds(plan.per * k, plan.per)].reshape(plan.per * 8, LANES) for k in range(4)
    ]
    live = _flag(lane < count[0])
    scaled = weight[...] * live
    coarse = scaled.astype(BF16).astype(F32)
    panel = node[...] // PN
    upper = jnp.where(panel >= 8, 1, 0)
    table = [
        elem[...].astype(F32),
        (panel - 8 * upper).astype(F32),
        (node[...] - panel * PN + PN * upper).astype(F32),
        coarse,
        scaled - coarse,
        jnp.zeros((3, LANES), F32),
    ]
    table = jnp.concatenate(table, axis=0)
    for dest in range(plan.groups):
        block = jnp.concatenate([window_of(quarter, dest, F32), table], axis=0)
        first = 2 * plan.field_rows
        out[dest, pl.ds(first, plan.rows - first), :] = block.astype(BF16)


def coefficients(plan, penalty, coef, rank):
    point = _iota((NP, LANES), 0)
    ends = [point // 16, (point // 4) % 4, point % 4]
    faces = sum(_flag((e == 0) | (e == 3)) for e in ends)
    lane = _iota((1, LANES), 1)
    z = plan.own * rank - plan.halo + lane % plan.window
    inside = _flag((z >= 0) & (z < plan.span))
    rows = []
    for a in range(plan.nv):
        coef[a] = 0.5 - (0.5 * penalty[a]) * faces
        rows.append((penalty[a] * inside).astype(BF16))
    return rows


def sweeps(plan, count, state, rounded, source, table, matrix, transposed, coef, rows):
    nv, nx, window = plan.nv, plan.nx, plan.window
    lane = _iota((1, LANES), 1)
    not_last = _flag(lane < LANES - window).astype(BF16)
    not_first = _flag(lane >= window).astype(BF16)
    for s in range(count):
        now, later = s % 2, (s + 1) % 2
        for h in range(nx):
            own = [rounded[now, h, b].reshape(4, 16, LANES) for b in range(nv)]
            for a0 in range(0, nv, 2):
                stacks = []
                for a in (a0, a0 + 1):
                    parts = []
                    for k in range(3):
                        total = None
                        for b in range(nv):
                            r = (k * nv + b) * nv + a if transposed else (k * nv + a) * nv + b
                            term = own[b] * table[h, r][None]
                            total = term if total is None else total + term
                        parts.append(total.reshape(NP, LANES))
                    scaled = own[a].reshape(NP, LANES) * rows[a]
                    parts.append(_roll(scaled, -window) * not_last)
                    parts.append(_roll(scaled, window) * not_first)
                    parts.append(_roll(scaled, -1))
                    parts.append(_roll(scaled, 1))
                    none = jnp.zeros((16, LANES), BF16)
                    above = rounded[now, h + 1, a, 0:16, :] * rows[a] if h + 1 < nx else none
                    below = rounded[now, h - 1, a, 48:64, :] * rows[a] if h > 0 else none
                    parts += [above, below]
                    stacks.append(jnp.concatenate(parts, axis=0))
                product = _nn(matrix, jnp.concatenate(stacks, axis=1))
                for i, a in enumerate((a0, a0 + 1)):
                    value = coef[a] * state[h, a] + source[h, a]
                    value = value + product[:, LANES * i : LANES * (i + 1)]
                    state[h, a] = value
                    rounded[later, h, a] = value.astype(BF16)
    return count % 2


def couple_rows(coupling):
    wide = coupling[...].astype(F32)
    pad = jnp.zeros((8 - SDOF, wide.shape[1]), F32)
    return jnp.concatenate([wide, pad], axis=0).astype(BF16)


def node_loads(plan, couple, values, incidence, places, weights, scr):
    lane = _iota((1, LANES), 1)
    place = lane % plan.window
    owned = _flag((place >= plan.halo) & (place < plan.halo + plan.own))
    picked = []
    for h in range(plan.nx):
        flow = _nn(couple, values[h]) * owned
        picked.append(_fold(_nn(_split(flow), places[h])) * weights[h])
    nodal = _fold(_nt(_split(jnp.concatenate(picked, axis=1)), incidence[...]))
    for j in range(8):
        scr[:, j, :] = nodal[:, LANES * j : LANES * (j + 1)]
    left = _iota((8, LANES), 1) < PN
    low, high = [], []
    for t in range(plan.tiles):
        even, odd = scr[2 * t], scr[2 * t + 1]
        low.append(jnp.where(left, even, _roll(odd, PN)))
        high.append(jnp.where(left, _roll(even, PN), odd))
    return low, high


def write_exchange(plan, low, high, solved, solved_scr, out, rank):
    solved_scr[...] = solved
    mine = rank // (plan.groups // plan.held)
    for dest in range(plan.ns):
        rows = []
        first = dest * plan.held
        for t in range(plan.tiles):
            part = low[t] if first < 8 else high[t]
            rows.append(part[first % 8 : first % 8 + plan.held])
        line = solved_scr[pl.ds(dest * plan.held + mine, 1), :]
        for t in range(plan.tiles):
            rows.append(line[:, LANES * t : LANES * (t + 1)])
        used = (plan.held + 1) * plan.tiles
        if used < 16:
            rows.append(jnp.zeros((16 - used, LANES), F32))
        block = jnp.concatenate(rows, axis=0).astype(BF16)
        for g in range(plan.groups):
            out[g * plan.ns + dest] = block


def read_loads(plan, received):
    totals = []
    for d in range(plan.ns):
        total = received[d].astype(F32)
        for g in range(1, plan.groups):
            total = total + received[g * plan.ns + d].astype(F32)
        totals.append(total)
    tiles = []
    for t in range(plan.tiles):
        rows = [x[plan.held * t : plan.held * (t + 1)] for x in totals]
        tiles.append(jnp.concatenate(rows, axis=0))
    return jnp.concatenate(tiles, axis=1)


def push_force(plan, received, incidence, places, weights, couple, rhs, shell_scr, scr, source):
    span = plan.groups // plan.held
    for s in range(plan.ns):
        for panel in range(plan.held):
            block = received[panel * span * plan.ns + s].astype(F32)
            q = s * plan.held + panel
            for t in range(plan.tiles):
                r = plan.held * plan.tiles + t
                shell_scr[q : q + 1, LANES * t : LANES * (t + 1)] = block[r : r + 1]
    left = _iota((8, LANES), 1) < PN
    for t in range(plan.tiles):
        upper = shell_scr[0:8, LANES * t : LANES * (t + 1)]
        lower = shell_scr[8:16, LANES * t : LANES * (t + 1)]
        scr[2 * t] = jnp.where(left, upper, _roll(lower, PN))
        scr[2 * t + 1] = jnp.where(left, _roll(upper, PN), lower)
    for c in range(2 * plan.tiles, 8):
        scr[c] = jnp.zeros((8, LANES), F32)
    nodal = jnp.concatenate([scr[:, j, :] for j in range(8)], axis=1).astype(BF16)
    picked = _nn(nodal, incidence[...])
    twice = jnp.concatenate([couple, couple], axis=0)
    for h in range(plan.nx):
        part = picked[:, plan.slots * h : plan.slots * (h + 1)] * weights[h]
        dofs = _fold(_nt(_split(part), places[h]))
        push = _tn(twice, _split(dofs))
        for a in range(plan.nv):
            value = rhs[0, h, a].astype(F32) - push[NP * a : NP * (a + 1)]
            source[h, a] = 0.5 * value


def first_kernel(
    plan, received, deriv, penalty, coupling, load, inverse,
    adjoint, rhs, table, second, incidence, places, weights, forward, backward, out,
    source, rounded, coef, scr, solved_scr,
):
    nv, window, nx, ny = plan.nv, plan.window, plan.nx, plan.ny
    rank = plan.rank()
    lane = _iota((1, LANES), 1)
    group = [_flag(lane // window == y) for y in range(ny)]

    def regroup(parts, k, dtype):
        total = None
        for y in range(ny):
            term = _roll(parts[y], window * (y - k)) * group[y].astype(dtype)
            total = term if total is None else total + term
        return total

    for h in range(nx):
        for f in range(2):
            for a in range(nv):
                first = (f * nv + a) * 16
                parts = [received[h * ny + y, pl.ds(first, 16), :] for y in range(ny)]
                for k in range(4):
                    rhs[f, h, a, pl.ds(16 * k, 16), :] = regroup(parts, k, BF16)
        first = 2 * plan.field_rows
        tails = [
            received[h * ny + y, pl.ds(first, plan.rows - first), :].astype(F32)
            for y in range(ny)
        ]
        for k in range(4):
            block = regroup([x[: plan.per * 8] for x in tails], k, F32)
            for i in range(plan.per):
                granule = k * plan.per + i
                part = block[8 * i : 8 * (i + 1)]
                if granule < 3 * nv:
                    for b in range(nv):
                        row = jnp.broadcast_to(part[b : b + 1], (16, LANES))
                        table[h, granule * nv + b] = row.astype(BF16)
                elif granule == 3 * nv:
                    second[h] = part
        info = [x[plan.per * 8 :] for x in tails]
        place = _iota((LANES, LANES), 0)
        spot = _iota((plan.nodes, LANES), 0)
        for y in range(ny):
            at = info[y]
            where = (at[0:1] - (plan.own * rank - plan.halo).astype(F32)).astype(jnp.int32)
            within = (where >= 0) & (where < window)
            target = jnp.where(within, where + y * window, -1)
            columns = pl.ds(LANES * y, LANES)
            places[h, :, columns] = _flag(place == target).astype(BF16)
            weights[h, :, columns] = at[3:4] + at[4:5]
            position = (at[1:2] * LANES + at[2:3]).astype(jnp.int32)
            columns = pl.ds(plan.slots * h + LANES * y, LANES)
            incidence[:, columns] = _flag(spot == position).astype(BF16)

    p, c = _iota((NP, plan.depth), 0), _iota((NP, plan.depth), 1)
    j, l = (p // 4) % 4, p % 4

    def block(n, ok, shift):
        return ok & (c - (3 + n) * NP == p + shift)

    links = block(0, j == 3, -12) | block(1, j == 0, 12)
    links = links | block(2, l == 3, -3) | block(3, l == 0, 3)
    links = links | ((p >= 48) & (c - 7 * NP == p - 48))
    links = links | ((p < 16) & (c - 7 * NP - 16 == p))
    base = (0.5 * _flag(links)).astype(BF16)
    forward[...] = base
    backward[...] = base
    for k in range(3):
        part = -0.5 * deriv[k].astype(F32)
        forward[:, NP * k : NP * (k + 1)] = part.astype(BF16)
        backward[:, NP * k : NP * (k + 1)] = part.T.astype(BF16)

    rows = coefficients(plan, penalty, coef, rank)
    for h in range(nx):
        for a in range(nv):
            value = 0.5 * rhs[1, h, a].astype(F32)
            source[h, a] = value
            adjoint[h, a] = value
            rounded[0, h, a] = value.astype(BF16)
    last = sweeps(
        plan, FSWEEP - 1, adjoint, rounded, source, table, backward[...], True, coef, rows
    )
    values = [rounded[last, h].reshape(nv * NP, LANES) for h in range(nx)]
    low, high = node_loads(plan, couple_rows(coupling), values, incidence, places, weights, scr)
    solved = shell_solve_rows(plan, stacked(load, plan.ns), inverse)
    write_exchange(plan, low, high, solved, solved_scr, out, rank)


def second_kernel(
    plan, received, penalty, coupling, load, shell_rhs, inverse, adjoint_in, rhs, table, second,
    incidence, places, weights, forward, backward,
    tangent, adjoint_rounded, out,
    adjoint, source, rounded, coef, scr, solved_scr, shell_scr,
):
    nv, nx = plan.nv, plan.nx
    rank = plan.rank()
    rows = coefficients(plan, penalty, coef, rank)
    couple = couple_rows(coupling)
    push_force(
        plan, received, incidence, places, weights, couple, rhs, shell_scr, scr, source
    )
    for h in range(nx):
        for a in range(nv):
            value = source[h, a]
            tangent[h, a] = value
            rounded[0, h, a] = value.astype(BF16)
    sweeps(plan, FSWEEP - 1, tangent, rounded, source, table, forward[...], False, coef, rows)
    for h in range(nx):
        for a in range(nv):
            extra = second[h, a : a + 1, :] * tangent[h, a]
            source[h, a] = 0.5 * (rhs[1, h, a].astype(F32) + extra)
            value = adjoint_in[h, a]
            adjoint[h, a] = value
            rounded[0, h, a] = value.astype(BF16)
    last = sweeps(
        plan, FSWEEP, adjoint, rounded, source, table, backward[...], True, coef, rows
    )
    adjoint_rounded[...] = rounded[last]
    values = [rounded[last, h].reshape(nv * NP, LANES) for h in range(nx)]
    low, high = node_loads(plan, couple, values, incidence, places, weights, scr)
    shell = stacked(shell_rhs, plan.ns) - read_loads(plan, received)
    shell = shell_solve_rows(plan, shell, inverse)
    solved = shell_solve_rows(plan, stacked(load, plan.ns) + shell, inverse)
    write_exchange(plan, low, high, solved, solved_scr, out, rank)


def third_kernel(
    plan, received, penalty, coupling, load, shell_rhs, inverse, tangent_in, adjoint_rounded,
    rhs, table, incidence, places, weights, forward,
    out, shell_tangent, shell_adjoint,
    tangent, source, rounded, coef, scr, shell_scr,
):
    nv, nx, ny, ns = plan.nv, plan.nx, plan.ny, plan.ns
    rank = plan.rank()
    rows = coefficients(plan, penalty, coef, rank)
    couple = couple_rows(coupling)
    push_force(
        plan, received, incidence, places, weights, couple, rhs, shell_scr, scr, source
    )
    for h in range(nx):
        for a in range(nv):
            value = tangent_in[h, a]
            tangent[h, a] = value
            rounded[0, h, a] = value.astype(BF16)
    last = sweeps(
        plan, FSWEEP, tangent, rounded, source, table, forward[...], False, coef, rows
    )
    lane = _iota((1, LANES), 1)
    narrow = plan.narrow
    group = [_flag(lane // narrow == n).astype(BF16) for n in range(8)]
    for h in range(nx):
        for a in range(nv):
            parts = []
            for ref in (rounded.at[last], adjoint_rounded):
                parts += [ref[h, a, pl.ds(16 * i, 16), :] for i in range(4)]
            for y in range(ny):
                total = None
                for n in range(8):
                    shift = narrow * n - plan.window * y - plan.halo
                    term = _roll(parts[n], shift) * group[n]
                    total = term if total is None else total + term
                out[h * ny + y, pl.ds(16 * a, 16), :] = total
    shell = stacked(shell_rhs, ns) - read_loads(plan, received)
    shell = shell_solve_rows(plan, shell, inverse)
    solved = shell_solve_rows(plan, stacked(load, ns) + shell, inverse)
    for d in range(ns):
        shell_adjoint[d] = shell[plan.held * d : plan.held * (d + 1)]
        shell_tangent[d] = solved[plan.held * d : plan.held * (d + 1)]


def last_kernel(plan, received, tangent, adjoint):
    lane = _iota((1, LANES), 1)
    narrow = plan.narrow
    group = [_flag(lane // narrow == g).astype(BF16) for g in range(plan.groups)]
    for a in range(plan.nv):
        parts = [received[g, pl.ds(16 * a, 16), :] for g in range(plan.groups)]
        for f, ref in enumerate((tangent, adjoint)):
            for i in range(4):
                total = None
                for g in range(plan.groups):
                    term = _roll(parts[g], narrow * (g - 4 * f - i)) * group[g]
                    total = term if total is None else total + term
                ref[a, pl.ds(16 * i, 16), :] = total


def call(kernel, plan, out_shape, scratch, scalars, args):
    vmem = pl.BlockSpec(memory_space=pltpu.VMEM)
    smem = pl.BlockSpec(memory_space=pltpu.SMEM)
    specs = [smem if i in scalars else vmem for i in range(len(args))]
    return pl.pallas_call(
        functools.partial(kernel, plan),
        out_shape=[jax.ShapeDtypeStruct(s, d) for s, d in out_shape],
        in_specs=specs,
        out_specs=[vmem] * len(out_shape),
        scratch_shapes=[pltpu.VMEM(s, d) for s, d in scratch],
        compiler_params=pltpu.CompilerParams(vmem_limit_bytes=KERNEL_VMEM),
    )(*args)


def slab_body(
    plan, tangent_rhs, adjoint_rhs, jacobians, deriv, penalty, second_order, coupling,
    shell_inverse, shell_load, shell_adjoint_rhs, iface_elem, iface_node, iface_weight,
    iface_count,
):
    nv, nx, ny, ns, groups = plan.nv, plan.nx, plan.ny, plan.ns, plan.groups
    flow, everyone = ("fx", "fy"), ("fx", "fy", "st")
    state = (nx, nv, NP, LANES)
    rounded = ((2,) + state, BF16)
    coef = ((nv, NP, LANES), F32)
    scr = ((8, 8, LANES), F32)
    shell_rows = ((plan.panels, plan.width), F32)
    solved_rows = ((ns * plan.held, plan.width), F32)
    trhs = tangent_rhs.reshape(nv, NP, LANES)
    arhs = adjoint_rhs.reshape(nv, NP, LANES)
    jac = jacobians.reshape(3, nv, nv, LANES)
    second_rows = second_order.reshape(nv, 1, LANES)

    (packed,) = call(
        pack_kernel, plan, [((groups, plan.rows, LANES), BF16)],
        [((4 * plan.per, 8, LANES), F32)], (7,),
        (trhs, arhs, jac, second_rows, iface_elem, iface_node, iface_weight, iface_count),
    )
    slab = lax.all_to_all(packed, flow, split_axis=0, concat_axis=0, tiled=True)
    exchange = ((groups * ns, 16, LANES), BF16)
    adjoint, rhs, table, second, incidence, places, weights, forward, backward, sent = call(
        first_kernel, plan,
        [
            (state, F32), ((2,) + state, BF16), ((nx, plan.deps, 16, LANES), BF16),
            ((nx, 8, LANES), F32), ((plan.nodes, nx * plan.slots), BF16),
            ((nx, LANES, plan.slots), BF16), ((nx, 1, plan.slots), F32),
            ((NP, plan.depth), BF16), ((NP, plan.depth), BF16), exchange,
        ],
        [(state, F32), rounded, coef, scr, solved_rows], (2,),
        (slab, deriv, penalty, coupling, shell_load, shell_inverse),
    )
    received = lax.all_to_all(sent, everyone, split_axis=0, concat_axis=0, tiled=True)
    tangent, adjoint_rounded, sent = call(
        second_kernel, plan, [(state, F32), (state, BF16), exchange],
        [(state, F32), (state, F32), rounded, coef, scr, solved_rows, shell_rows], (1,),
        (
            received, penalty, coupling, shell_load, shell_adjoint_rhs, shell_inverse, adjoint,
            rhs, table, second, incidence, places, weights, forward, backward,
        ),
    )
    received = lax.all_to_all(sent, everyone, split_axis=0, concat_axis=0, tiled=True)
    shell_shape = (shell_load.shape, F32)
    sent, shell_tangent, shell_adjoint = call(
        third_kernel, plan,
        [((groups, plan.field_rows, LANES), BF16), shell_shape, shell_shape],
        [(state, F32), (state, F32), rounded, coef, scr, shell_rows], (1,),
        (
            received, penalty, coupling, shell_load, shell_adjoint_rhs, shell_inverse, tangent,
            adjoint_rounded, rhs, table, incidence, places, weights, forward,
        ),
    )
    received = lax.all_to_all(sent, flow, split_axis=0, concat_axis=0, tiled=True)
    tangent, adjoint = call(
        last_kernel, plan, [((nv, NP, LANES), BF16)] * 2, [], (), (received,)
    )
    return (
        tangent.reshape(tangent_rhs.shape), adjoint.reshape(adjoint_rhs.shape),
        shell_tangent, shell_adjoint,
    )


def body(*args):
    tangent_rhs, shell_inverse, shell_load, iface_elem = args[0], args[7], args[8], args[10]
    nx, ny, ns = (lax.axis_size(name) for name in ("fx", "fy", "st"))
    panels, width = shell_inverse.shape[0] * ns, shell_load.shape[2]
    if fits(nx, ny, ns, tangent_rhs.shape, iface_elem.shape[1], panels, width):
        plan = Plan(nx, ny, ns, tangent_rhs.shape[1], tangent_rhs.shape[5], panels, width)
        return slab_body(plan, *args)
    return halo_body(*args)


def solution(mesh):
    in_specs = (
        P("st", None, None, "fx", "fy", None),
        P("st", None, None, "fx", "fy", None),
        P(None, None, None, "fx", "fy", None),
        P(),
        P(),
        P(None, "fx", "fy", None),
        P(),
        P("st", None, None),
        P(None, "st", None),
        P(None, "st", None),
        P(("fx", "fy"), None),
        P(("fx", "fy"), None),
        P(("fx", "fy"), None),
        P(("fx", "fy")),
    )
    out_specs = (
        P("st", None, None, "fx", "fy", None),
        P("st", None, None, "fx", "fy", None),
        P(None, "st", None),
        P(None, "st", None),
    )
    return jax.shard_map(body, mesh=mesh, in_specs=in_specs, out_specs=out_specs, check_vma=False)
```

```python
import functools

import jax
import jax.numpy as jnp
from jax import lax
from jax.experimental import pallas as pl
from jax.experimental.pallas import tpu as pltpu
from jax.sharding import PartitionSpec as P

SDOF = 6
PN = 64
NP = 64
FSWEEP = 3
ROUNDS = 2
LANES = 128
KERNEL_VMEM = 32 * 1024 * 1024
F32 = jnp.float32
BF16 = jnp.bfloat16


SIGMA = 0.5


def with_halo(value, sides, width):
    for axis, dim in sides:
        peers, length = (lax.axis_size(axis), value.shape[dim])
        up = [(i, (i + 1) % peers) for i in range(peers - 1)]
        down = [(j, i) for i, j in up]
        last = lax.slice_in_dim(value, length - width, length, axis=dim)
        initial = lax.slice_in_dim(value, 0, width, axis=dim)
        before = lax.ppermute(last, axis, up)
        after = lax.ppermute(initial, axis, down)
        value = jnp.concatenate([before, value, after], axis=dim)
    return value


def face_pair(lower_face, upper_face, below, above, axis):
    length = lower_face.shape[axis]
    beyond_upper = jnp.concatenate(
        [lax.slice_in_dim(lower_face, 1, length, axis=axis), above], axis=axis
    )
    beyond_lower = jnp.concatenate(
        [below, lax.slice_in_dim(upper_face, 0, length - 1, axis=axis)], axis=axis
    )
    return (lower_face - beyond_lower, upper_face - beyond_upper)


def place_faces(jump_low, jump_high, axis):
    middle_shape = list(jump_low.shape)
    middle_shape.insert(axis, 2)
    middle = jnp.zeros(middle_shape, jump_low.dtype)
    return jnp.concatenate(
        [jnp.expand_dims(jump_low, axis), middle, jnp.expand_dims(jump_high, axis)], axis=axis
    )


def as_cube(values):
    members, variables, points, size_x, size_y, size_z = values.shape
    return values.reshape(members, variables, 4, 4, 4, size_x, size_y, size_z)


def face_edges(values):
    cube = as_cube(values)
    received = []
    for node_axis in (2, 3):
        elem_axis = node_axis + 2
        lower_face = jnp.take(cube, 0, axis=node_axis)
        upper_face = jnp.take(cube, 3, axis=node_axis)
        edges = jnp.concatenate([lower_face, upper_face], axis=elem_axis)
        if node_axis == 2:
            extended = with_halo(edges, (("fx", 4),), 1)
        else:
            extended = with_halo(edges, (("fy", 5),), 1)
        below = lax.slice_in_dim(extended, 0, 1, axis=elem_axis)
        above = lax.slice_in_dim(extended, 3, 4, axis=elem_axis)
        received.append((below, above))
    return received


def flow_jumps(values, received):
    cube = as_cube(values)
    result = jnp.zeros(cube.shape, jnp.float32)
    for node_axis in (2, 3, 4):
        elem_axis = node_axis + 2
        lower_face = jnp.take(cube, 0, axis=node_axis).astype(jnp.float32)
        upper_face = jnp.take(cube, 3, axis=node_axis).astype(jnp.float32)
        if received is None or node_axis == 4:
            below = jnp.zeros_like(lax.slice_in_dim(lower_face, 0, 1, axis=elem_axis))
            above = below
        else:
            below = received[node_axis - 2][0].astype(jnp.float32)
            above = received[node_axis - 2][1].astype(jnp.float32)
        jump_low, jump_high = face_pair(lower_face, upper_face, below, above, elem_axis)
        result = result + place_faces(jump_low, jump_high, node_axis)
    return result.reshape(values.shape)


def volume(values, deriv_mats, jac_mats):
    grads = jnp.einsum("kpq,vqxyz->kvpxyz", deriv_mats, values, preferred_element_type=jnp.float32)
    result = jnp.sum(jac_mats[0][:, :, None] * grads[0][None], axis=1)
    for axis_index in (1, 2):
        result = result + jnp.sum(
            jac_mats[axis_index][:, :, None] * grads[axis_index][None], axis=1
        )
    return result


def operator(states, operator_kinds, penalty):
    values = lax.optimization_barrier(states.astype(jnp.bfloat16))
    received = face_edges(values)
    jumps = flow_jumps(values, received)
    volumes = jnp.stack(
        [
            volume(values[member], operator_kinds[member][0], operator_kinds[member][1])
            for member in range(len(operator_kinds))
        ]
    )
    return states + volumes + penalty[None, :, None, None, None, None] * jumps


def halo_body(
    tangent_rhs,
    adjoint_rhs,
    jacobians,
    deriv,
    penalty,
    second_order,
    coupling,
    shell_inverse,
    shell_load,
    shell_adjoint_rhs,
    iface_elem,
    iface_node,
    iface_weight,
    iface_count,
):
    state_shape = tangent_rhs.shape
    variables = state_shape[1]
    points = state_shape[2]
    elements = state_shape[3] * state_shape[4] * state_shape[5]
    slots = iface_elem.shape[1]
    live = (jnp.arange(slots, dtype=jnp.int32) < iface_count[0]).astype(jnp.float32)
    weights = iface_weight[0] * live
    elem_index = iface_elem[0]
    node_index = iface_node[0]
    dof_rows = jnp.arange(SDOF, dtype=jnp.int32)[:, None]
    columns = (node_index // PN)[None, :] * (SDOF * PN) + dof_rows * PN + (node_index % PN)[None, :]
    forward_jac = jacobians.astype(jnp.float32)
    forward_kind = (deriv, forward_jac)
    backward_kind = (jnp.swapaxes(deriv, 1, 2), jnp.swapaxes(forward_jac, 1, 2))
    coupling_cols = coupling.T

    def shell_solve(rhs):
        return jnp.einsum(
            "pab,dpb->dpa",
            shell_inverse,
            rhs.astype(jnp.bfloat16),
            preferred_element_type=jnp.float32,
        )

    shell_tangent = shell_solve(shell_load)
    shell_adjoint = jnp.zeros(shell_load.shape, jnp.float32)
    tangent = jnp.zeros(state_shape, jnp.float32)
    adjoint = jnp.zeros(state_shape, jnp.float32)
    for round_index in range(ROUNDS):
        received = lax.all_to_all(
            shell_tangent.astype(jnp.bfloat16), "st", split_axis=0, concat_axis=1, tiled=True
        )
        picked = received.reshape(-1)[columns]
        pushed_cols = (
            jnp.dot(coupling_cols, picked, preferred_element_type=jnp.float32) * weights[None, :]
        )
        pushed = (
            jnp.zeros((variables * points, elements), jnp.float32)
            .at[:, elem_index]
            .add(pushed_cols)
        )
        force = tangent_rhs.astype(jnp.float32) - pushed.reshape(state_shape)
        adjoint_source = adjoint_rhs.astype(jnp.float32) + second_order[None, :, None] * tangent
        paired = jnp.concatenate([tangent, adjoint])
        sources = jnp.concatenate([force, adjoint_source])
        for sweep in range(FSWEEP):
            paired = paired + SIGMA * (
                sources - operator(paired, (forward_kind, backward_kind), penalty)
            )
        tangent = paired[:1]
        adjoint = paired[1:]
        adjoint_values = adjoint.astype(jnp.bfloat16).reshape(variables * points, elements)
        gathered = adjoint_values[:, elem_index]
        loads = jnp.dot(coupling, gathered, preferred_element_type=jnp.float32) * weights[None, :]
        panels = received.shape[1]
        partial_loads = jnp.zeros((panels * SDOF * PN,), jnp.float32).at[columns].add(loads)
        partial_loads = partial_loads.reshape(1, panels, SDOF * PN)
        summed = lax.psum(partial_loads, ("fx", "fy"))
        owned = lax.all_to_all(summed, "st", split_axis=1, concat_axis=0, tiled=True)
        shell_adjoint = shell_solve(shell_adjoint_rhs - owned)
        shell_tangent = shell_solve(shell_load + shell_adjoint)
    return (
        tangent.astype(jnp.bfloat16),
        adjoint.astype(jnp.bfloat16),
        shell_tangent,
        shell_adjoint,
    )


def _iota(shape, dim):
    return lax.broadcasted_iota(jnp.int32, shape, dim)


def _flag(cond):
    return jnp.where(cond, 1.0, 0.0)


def _nt(a, b):
    return lax.dot_general(a, b, (((1,), (1,)), ((), ())), preferred_element_type=F32)


def _nn(a, b):
    return lax.dot_general(a, b, (((1,), (0,)), ((), ())), preferred_element_type=F32)


def _tn(a, b):
    return lax.dot_general(a, b, (((0,), (0,)), ((), ())), preferred_element_type=F32)


def _split(x):
    high = x.astype(BF16)
    low = (x - high.astype(F32)).astype(BF16)
    return jnp.concatenate([high, low], axis=0)


def _fold(x):
    half = x.shape[0] // 2
    return x[:half] + x[half:]


def _roll(x, shift):
    shift = shift % LANES
    return x if shift == 0 else pltpu.roll(x, shift, 1)


class Plan:
    def __init__(self, nx, ny, ns, nv, span, panels, width):
        self.nx, self.ny, self.ns, self.nv = nx, ny, ns, nv
        self.span, self.panels, self.width = span, panels, width
        self.groups = nx * ny
        self.own = span // self.groups
        self.window = LANES // ny
        self.halo = (self.window - self.own) // 2
        self.held = panels // ns
        self.nodes = panels * PN
        self.tiles = width // LANES
        self.narrow = LANES // self.groups
        self.deps = 3 * nv * nv
        self.granules = 3 * nv + 1
        self.per = -(-self.granules // 4)
        self.field_rows = nv * 16
        self.rows = 2 * self.field_rows + self.per * 8 + 8
        self.depth = 7 * NP + 32
        self.slots = ny * LANES

    def rank(self):
        return lax.axis_index("fx") * self.ny + lax.axis_index("fy")


def fits(nx, ny, ns, local_shape, slots, panels, width):
    members, nv, points, size_x, size_y, span = local_shape
    groups = nx * ny
    if members != 1 or (size_x, size_y) != (1, 1) or points != NP or nv > 8 or nv % 2:
        return False
    if span != LANES or slots != LANES or span % groups or LANES % ny or LANES % groups:
        return False
    own, window = span // groups, LANES // ny
    if window * 4 != LANES or (window - own) % 2 or (window - own) // 2 < ROUNDS * FSWEEP - 1:
        return False
    if own * 8 != LANES or width != SDOF * PN or width % LANES or SDOF > 8:
        return False
    held = panels // ns
    if panels % ns or panels != 16 or groups % held or ns > 4:
        return False
    return (held + 1) * (width // LANES) <= 16 and 8 % held == 0


def shell_solve_rows(plan, rhs, inverse_ref):
    rows = rhs.shape[0]
    rounded = rhs.astype(BF16)
    member = _iota((rows, plan.width), 0) % plan.held
    result = jnp.zeros((rows, plan.width), F32)
    for panel in range(plan.held):
        result = jnp.where(member == panel, _nt(rounded, inverse_ref[panel]), result)
    return result


def member_rows(plan, ref, panel):
    rows = [ref[d, pl.ds(panel, 1), :] for d in range(plan.ns)]
    rows.append(jnp.zeros((8 - plan.ns, plan.width), F32))
    return jnp.concatenate(rows, axis=0)


def fetch(pairs, sems):
    copies = [
        pltpu.make_async_copy(source, target, sems.at[i])
        for i, (source, target) in enumerate(pairs)
    ]
    for copy in copies:
        copy.start()
    return copies


def stacked(ref, count):
    return jnp.concatenate([ref[d] for d in range(count)], axis=0)


def pack_kernel(
    plan, trhs_hbm, arhs_hbm, jac_hbm, second_hbm, elem_hbm, node_hbm, weight_hbm, count_hbm,
    out, trhs, arhs, jac, second, elem, node, weight, scr, count, sems,
):
    nv, window = plan.nv, plan.window
    copies = fetch(
        (
            (trhs_hbm, trhs), (arhs_hbm, arhs), (jac_hbm, jac), (second_hbm, second),
            (elem_hbm, elem), (node_hbm, node), (weight_hbm, weight),
            (count_hbm, count),
        ),
        sems,
    )
    lane = _iota((1, LANES), 1)
    masks = []
    for dest in range(plan.groups):
        start = plan.own * dest - plan.halo
        row = []
        for k in range(4):
            z = start + lane % window
            row.append(_flag((lane // window == k) & (z >= 0) & (z < plan.span)))
        masks.append(row)

    def window_of(parts, dest, dtype):
        start = plan.own * dest - plan.halo
        total = None
        for k in range(4):
            term = _roll(parts[k], window * k - start) * masks[dest][k].astype(dtype)
            total = term if total is None else total + term
        return total

    for f, ref in enumerate((trhs, arhs)):
        copies[f].wait()
        for a in range(nv):
            parts = [ref[a, pl.ds(16 * k, 16), :] for k in range(4)]
            for dest in range(plan.groups):
                out[dest, pl.ds((f * nv + a) * 16, 16), :] = window_of(parts, dest, BF16)

    for copy in copies[2:]:
        copy.wait()
    scr[...] = jnp.zeros(scr.shape, F32)
    for k in range(3):
        for a in range(nv):
            scr[k * nv + a, 0:nv, :] = jac[k, a].astype(F32)
    for a in range(nv):
        scr[3 * nv, a : a + 1, :] = second[a]
    quarter = [
        scr[pl.ds(plan.per * k, plan.per)].reshape(plan.per * 8, LANES) for k in range(4)
    ]
    live = _flag(lane < count[0])
    scaled = weight[...] * live
    coarse = scaled.astype(BF16).astype(F32)
    panel = node[...] // PN
    upper = jnp.where(panel >= 8, 1, 0)
    table = [
        elem[...].astype(F32),
        (panel - 8 * upper).astype(F32),
        (node[...] - panel * PN + PN * upper).astype(F32),
        coarse,
        scaled - coarse,
        jnp.zeros((3, LANES), F32),
    ]
    table = jnp.concatenate(table, axis=0)
    for dest in range(plan.groups):
        block = jnp.concatenate([window_of(quarter, dest, F32), table], axis=0)
        first = 2 * plan.field_rows
        out[dest, pl.ds(first, plan.rows - first), :] = block.astype(BF16)


def coefficients(plan, penalty, coef, rank):
    point = _iota((NP, LANES), 0)
    ends = [point // 16, (point // 4) % 4, point % 4]
    faces = sum(_flag((e == 0) | (e == 3)) for e in ends)
    lane = _iota((16, LANES), 1)
    z = plan.own * rank - plan.halo + lane % plan.window
    inside = _flag((z >= 0) & (z < plan.span))
    rows = []
    for a in range(plan.nv):
        coef[a] = 0.5 - (0.5 * penalty[a]) * faces
        rows.append((penalty[a] * inside).astype(BF16))
    return rows


def sweeps(plan, count, state, source, table, matrix, transposed, coef, rows):
    nv, nx, window = plan.nv, plan.nx, plan.window
    lane = _iota((16, LANES), 1)
    not_last = _flag(lane < LANES - window).astype(BF16)
    not_first = _flag(lane >= window).astype(BF16)
    none = jnp.zeros((16, LANES), BF16)

    def plane(now, h, a, i):
        return state[now, h, a, pl.ds(16 * i, 16), :].astype(BF16)

    def flux(h, k, a, b):
        index, row = (k * nv + b, a) if transposed else (k * nv + a, b)
        line = table[h, index, pl.ds(row, 1), :]
        return jnp.broadcast_to(line, (16, LANES)).astype(BF16)

    for s in range(count):
        now, later = s % 2, (s + 1) % 2
        for h in range(nx):
            own = [[plane(now, h, b, i) for i in range(4)] for b in range(nv)]
            for a0 in range(0, nv, 2):
                stacks = []
                for a in (a0, a0 + 1):
                    parts = []
                    for k in range(3):
                        total = [None] * 4
                        for b in range(nv):
                            factor = flux(h, k, a, b)
                            for i in range(4):
                                term = own[b][i] * factor
                                total[i] = term if b == 0 else total[i] + term
                        parts += total
                    scaled = [own[a][i] * rows[a] for i in range(4)]
                    parts += [_roll(x, -window) * not_last for x in scaled]
                    parts += [_roll(x, window) * not_first for x in scaled]
                    parts += [_roll(x, -1) for x in scaled]
                    parts += [_roll(x, 1) for x in scaled]
                    parts.append(plane(now, h + 1, a, 0) * rows[a] if h + 1 < nx else none)
                    parts.append(plane(now, h - 1, a, 3) * rows[a] if h > 0 else none)
                    stacks.append(jnp.concatenate(parts, axis=0))
                product = _nn(matrix, jnp.concatenate(stacks, axis=1))
                for i, a in enumerate((a0, a0 + 1)):
                    value = coef[a] * state[now, h, a] + source[h, a]
                    state[later, h, a] = value + product[:, LANES * i : LANES * (i + 1)]
    return count % 2


def couple_rows(coupling):
    wide = coupling[...].astype(F32)
    pad = jnp.zeros((8 - SDOF, wide.shape[1]), F32)
    return jnp.concatenate([wide, pad], axis=0).astype(BF16)


def node_loads(plan, couple, values, incidence, places, weights, scr):
    lane = _iota((1, LANES), 1)
    place = lane % plan.window
    owned = _flag((place >= plan.halo) & (place < plan.halo + plan.own))
    picked = []
    for h in range(plan.nx):
        flow = _nn(couple, values[h]) * owned
        picked.append(_fold(_nn(_split(flow), places[h])) * weights[h])
    nodal = _fold(_nt(_split(jnp.concatenate(picked, axis=1)), incidence[...]))
    for j in range(8):
        scr[:, j, :] = nodal[:, LANES * j : LANES * (j + 1)]
    left = _iota((8, LANES), 1) < PN
    low, high = [], []
    for t in range(plan.tiles):
        even, odd = scr[2 * t], scr[2 * t + 1]
        low.append(jnp.where(left, even, _roll(odd, PN)))
        high.append(jnp.where(left, _roll(even, PN), odd))
    return low, high


def first_exchange(plan, low, high, solved, out):
    share = plan.groups // plan.held
    for dest in range(plan.ns):
        for panel in range(plan.held):
            q = dest * plan.held + panel
            rows = [(low[t] if q < 8 else high[t])[q % 8 : q % 8 + 1] for t in range(plan.tiles)]
            line = solved[dest : dest + 1]
            rows += [line[:, LANES * t : LANES * (t + 1)] for t in range(plan.tiles)]
            rows.append(jnp.zeros((8 - 2 * plan.tiles, LANES), F32))
            block = jnp.concatenate(rows, axis=0).astype(BF16)
            for g in range(panel * share, (panel + 1) * share):
                out[g * plan.ns + dest] = block


def second_exchange(plan, low, high, solved, out):
    for dest in range(plan.ns):
        rows = []
        first = dest * plan.held
        for t in range(plan.tiles):
            part = low[t] if first < 8 else high[t]
            rows.append(part[first % 8 : first % 8 + plan.held])
        line = solved[dest : dest + 1]
        rows += [line[:, LANES * t : LANES * (t + 1)] for t in range(plan.tiles)]
        used = (plan.held + 1) * plan.tiles
        if used < 16:
            rows.append(jnp.zeros((16 - used, LANES), F32))
        block = jnp.concatenate(rows, axis=0).astype(BF16)
        for g in range(plan.groups):
            out[g * plan.ns + dest] = block


def summed(plan, received):
    totals = []
    for d in range(plan.ns):
        total = received[d].astype(F32)
        for g in range(1, plan.groups):
            total = total + received[g * plan.ns + d].astype(F32)
        totals.append(total)
    return totals


def read_own_loads(plan, received):
    totals = summed(plan, received)
    tiles = []
    for t in range(plan.tiles):
        rows = [x[t : t + 1] for x in totals] + [jnp.zeros((8 - plan.ns, LANES), F32)]
        tiles.append(jnp.concatenate(rows, axis=0))
    return jnp.concatenate(tiles, axis=1)


def read_loads(plan, received):
    totals = summed(plan, received)
    tiles = []
    for t in range(plan.tiles):
        rows = [x[plan.held * t : plan.held * (t + 1)] for x in totals]
        tiles.append(jnp.concatenate(rows, axis=0))
    return jnp.concatenate(tiles, axis=1)


def push_force(
    plan, received, first, incidence, places, weights, couple, rhs, shell_scr, scr, source
):
    span = plan.groups // plan.held
    for s in range(plan.ns):
        for panel in range(plan.held):
            block = received[panel * span * plan.ns + s].astype(F32)
            q = s * plan.held + panel
            for t in range(plan.tiles):
                line = block[first + t : first + t + 1]
                shell_scr[q : q + 1, LANES * t : LANES * (t + 1)] = line
    left = _iota((8, LANES), 1) < PN
    for t in range(plan.tiles):
        upper = shell_scr[0:8, LANES * t : LANES * (t + 1)]
        lower = shell_scr[8:16, LANES * t : LANES * (t + 1)]
        scr[2 * t] = jnp.where(left, upper, _roll(lower, PN))
        scr[2 * t + 1] = jnp.where(left, _roll(upper, PN), lower)
    for c in range(2 * plan.tiles, 8):
        scr[c] = jnp.zeros((8, LANES), F32)
    nodal = jnp.concatenate([scr[:, j, :] for j in range(8)], axis=1).astype(BF16)
    picked = _nn(nodal, incidence[...])
    twice = jnp.concatenate([couple, couple], axis=0)
    for h in range(plan.nx):
        part = picked[:, plan.slots * h : plan.slots * (h + 1)] * weights[h]
        dofs = _fold(_nt(_split(part), places[h]))
        push = _tn(twice, _split(dofs))
        for a in range(plan.nv):
            value = rhs[0, h, a].astype(F32) - push[NP * a : NP * (a + 1)]
            source[h, a] = 0.5 * value


def prepare_kernel(
    plan, deriv_hbm, load_hbm, inverse_hbm, forward, backward, solved, deriv, load, inverse, sems
):
    mine = plan.rank() // (plan.groups // plan.held)
    copies = fetch(
        ((deriv_hbm, deriv), (load_hbm, load), (inverse_hbm.at[mine], inverse)), sems
    )
    p, c = _iota((NP, plan.depth), 0), _iota((NP, plan.depth), 1)
    j, l = (p // 4) % 4, p % 4

    def block(n, ok, shift):
        return ok & (c - (3 + n) * NP == p + shift)

    links = block(0, j == 3, -12) | block(1, j == 0, 12)
    links = links | block(2, l == 3, -3) | block(3, l == 0, 3)
    links = links | ((p >= 48) & (c - 7 * NP == p - 48))
    links = links | ((p < 16) & (c - 7 * NP - 16 == p))
    base = (0.5 * _flag(links)).astype(BF16)
    forward[...] = base
    backward[...] = base
    for copy in copies:
        copy.wait()
    for k in range(3):
        part = -0.5 * deriv[k].astype(F32)
        forward[:, NP * k : NP * (k + 1)] = part.astype(BF16)
        backward[:, NP * k : NP * (k + 1)] = part.T.astype(BF16)
    solved[...] = _nt(member_rows(plan, load, mine).astype(BF16), inverse[...])


def first_kernel(
    plan, received, backward, solved, coupling_hbm, penalty,
    adjoint, rhs, table, incidence, places, weights, out,
    state, source, coef, scr, coupling, sems,
):
    nv, window, nx, ny = plan.nv, plan.window, plan.nx, plan.ny
    copies = fetch(((coupling_hbm, coupling),), sems)
    rank = plan.rank()
    lane = _iota((1, LANES), 1)
    group = [_flag(lane // window == y) for y in range(ny)]

    def regroup(parts, k, dtype):
        total = None
        for y in range(ny):
            term = _roll(parts[y], window * (y - k)) * group[y].astype(dtype)
            total = term if total is None else total + term
        return total

    for h in range(nx):
        for f in range(2):
            for a in range(nv):
                first = (f * nv + a) * 16
                parts = [received[h * ny + y, pl.ds(first, 16), :] for y in range(ny)]
                for k in range(4):
                    rhs[f, h, a, pl.ds(16 * k, 16), :] = regroup(parts, k, BF16)
        first = 2 * plan.field_rows
        tails = [
            received[h * ny + y, pl.ds(first, plan.rows - first), :].astype(F32)
            for y in range(ny)
        ]
        for k in range(4):
            block = regroup([x[: plan.per * 8] for x in tails], k, F32)
            for i in range(plan.per):
                table[h, k * plan.per + i] = block[8 * i : 8 * (i + 1)]
        info = [x[plan.per * 8 :] for x in tails]
        place = _iota((LANES, LANES), 0)
        spot = _iota((plan.nodes, LANES), 0)
        for y in range(ny):
            at = info[y]
            where = (at[0:1] - (plan.own * rank - plan.halo).astype(F32)).astype(jnp.int32)
            within = (where >= 0) & (where < window)
            target = jnp.where(within, where + y * window, -1)
            columns = pl.ds(LANES * y, LANES)
            places[h, :, columns] = _flag(place == target).astype(BF16)
            weights[h, :, columns] = at[3:4] + at[4:5]
            position = (at[1:2] * LANES + at[2:3]).astype(jnp.int32)
            columns = pl.ds(plan.slots * h + LANES * y, LANES)
            incidence[:, columns] = _flag(spot == position).astype(BF16)

    rows = coefficients(plan, penalty, coef, rank)
    for h in range(nx):
        for a in range(nv):
            value = 0.5 * rhs[1, h, a].astype(F32)
            source[h, a] = value
            state[0, h, a] = value
    last = sweeps(plan, FSWEEP - 1, state, source, table, backward[...], True, coef, rows)
    values = [state[last, h].reshape(nv * NP, LANES).astype(BF16) for h in range(nx)]
    copies[0].wait()
    low, high = node_loads(plan, couple_rows(coupling), values, incidence, places, weights, scr)
    first_exchange(plan, low, high, solved[...], out)
    adjoint[...] = state[last]


def second_kernel(
    plan, received, adjoint_in, rhs, table, incidence, places, weights, forward, backward,
    coupling_hbm, load_hbm, shell_rhs_hbm, inverse_hbm, penalty,
    tangent, adjoint_rounded, out,
    state, source, coef, scr, shell_scr, coupling, load, shell_rhs, inverse, sems,
):
    nv, nx = plan.nv, plan.nx
    rank = plan.rank()
    mine = rank // (plan.groups // plan.held)
    copies = fetch(
        (
            (coupling_hbm, coupling), (load_hbm, load), (shell_rhs_hbm, shell_rhs),
            (inverse_hbm.at[mine], inverse),
        ),
        sems,
    )
    rows = coefficients(plan, penalty, coef, rank)
    for copy in copies:
        copy.wait()
    shell = member_rows(plan, shell_rhs, mine) - read_own_loads(plan, received)
    shell = _nt(shell.astype(BF16), inverse[...])
    shell = member_rows(plan, load, mine) + shell
    solved = _nt(shell.astype(BF16), inverse[...])
    couple = couple_rows(coupling)
    push_force(
        plan, received, plan.tiles, incidence, places, weights, couple, rhs, shell_scr, scr, source
    )
    for h in range(nx):
        for a in range(nv):
            state[0, h, a] = source[h, a]
    last = sweeps(plan, FSWEEP - 1, state, source, table, forward[...], False, coef, rows)
    tangent[...] = state[last]
    for h in range(nx):
        for a in range(nv):
            extra = table[h, 3 * nv, a : a + 1, :] * state[last, h, a]
            source[h, a] = 0.5 * (rhs[1, h, a].astype(F32) + extra)
    for h in range(nx):
        for a in range(nv):
            state[0, h, a] = adjoint_in[h, a]
    last = sweeps(plan, FSWEEP, state, source, table, backward[...], True, coef, rows)
    values = []
    for h in range(nx):
        value = state[last, h].reshape(nv * NP, LANES).astype(BF16)
        adjoint_rounded[h] = value
        values.append(value)
    low, high = node_loads(plan, couple, values, incidence, places, weights, scr)
    second_exchange(plan, low, high, solved, out)


def third_kernel(
    plan, received, tangent_in, adjoint_rounded, rhs, table, incidence, places, weights, forward,
    coupling_hbm, penalty,
    out,
    state, source, coef, scr, shell_scr, coupling, sems,
):
    nv, nx, ny = plan.nv, plan.nx, plan.ny
    rank = plan.rank()
    copies = fetch(((coupling_hbm, coupling),), sems)
    rows = coefficients(plan, penalty, coef, rank)
    copies[0].wait()
    push_force(
        plan, received, plan.held * plan.tiles, incidence, places, weights, couple_rows(coupling),
        rhs, shell_scr, scr, source,
    )
    for h in range(nx):
        for a in range(nv):
            state[0, h, a] = tangent_in[h, a]
    last = sweeps(plan, FSWEEP, state, source, table, forward[...], False, coef, rows)
    lane = _iota((16, LANES), 1)
    narrow = plan.narrow
    group = [_flag(lane // narrow == n).astype(BF16) for n in range(8)]
    for h in range(nx):
        for a in range(nv):
            parts = [state[last, h, a, pl.ds(16 * i, 16), :].astype(BF16) for i in range(4)]
            parts += [adjoint_rounded[h, pl.ds(a * NP + 16 * i, 16), :] for i in range(4)]
            for y in range(ny):
                total = None
                for n in range(8):
                    shift = narrow * n - plan.window * y - plan.halo
                    term = _roll(parts[n], shift) * group[n]
                    total = term if total is None else total + term
                out[h * ny + y, pl.ds(16 * a, 16), :] = total


def shell_kernel(
    plan, received, load_hbm, shell_rhs_hbm, inverse_hbm, shell_tangent, shell_adjoint,
    load, shell_rhs, inverse, sems,
):
    copies = fetch(
        ((load_hbm, load), (shell_rhs_hbm, shell_rhs), (inverse_hbm, inverse)), sems
    )
    for copy in copies:
        copy.wait()
    shell = stacked(shell_rhs, plan.ns) - read_loads(plan, received)
    shell = shell_solve_rows(plan, shell, inverse)
    solved = shell_solve_rows(plan, stacked(load, plan.ns) + shell, inverse)
    for d in range(plan.ns):
        shell_adjoint[d] = shell[plan.held * d : plan.held * (d + 1)]
        shell_tangent[d] = solved[plan.held * d : plan.held * (d + 1)]


def last_kernel(plan, received, tangent, adjoint):
    lane = _iota((16, LANES), 1)
    narrow = plan.narrow
    group = [_flag(lane // narrow == g).astype(BF16) for g in range(plan.groups)]
    for a in range(plan.nv):
        parts = [received[g, pl.ds(16 * a, 16), :] for g in range(plan.groups)]
        for f, ref in enumerate((tangent, adjoint)):
            for i in range(4):
                total = None
                for g in range(plan.groups):
                    term = _roll(parts[g], narrow * (g - 4 * f - i)) * group[g]
                    total = term if total is None else total + term
                ref[a, pl.ds(16 * i, 16), :] = total


def call(kernel, plan, out_shape, scratch, copies, on_chip, in_hbm, scalars, limit=KERNEL_VMEM):
    vmem = pl.BlockSpec(memory_space=pltpu.VMEM)
    hbm = pl.BlockSpec(memory_space=pltpu.HBM)
    smem = pl.BlockSpec(memory_space=pltpu.SMEM)
    specs = [vmem] * len(on_chip) + [hbm] * len(in_hbm) + [smem] * len(scalars)
    scratch_shapes = [x if isinstance(x, pl.MemoryRef) else pltpu.VMEM(*x) for x in scratch]
    if copies:
        scratch_shapes.append(pltpu.SemaphoreType.DMA((copies,)))
    return pl.pallas_call(
        functools.partial(kernel, plan),
        out_shape=[jax.ShapeDtypeStruct(s, d) for s, d in out_shape],
        in_specs=specs,
        out_specs=[vmem] * len(out_shape),
        scratch_shapes=scratch_shapes,
        compiler_params=pltpu.CompilerParams(vmem_limit_bytes=limit),
    )(*on_chip, *in_hbm, *scalars)


def slab_body(
    plan, tangent_rhs, adjoint_rhs, jacobians, deriv, penalty, second_order, coupling,
    shell_inverse, shell_load, shell_adjoint_rhs, iface_elem, iface_node, iface_weight,
    iface_count,
):
    nv, nx, ns, groups = plan.nv, plan.nx, plan.ns, plan.groups
    flow, everyone = ("fx", "fy"), ("fx", "fy", "st")
    state = ((nx, nv, NP, LANES), F32)
    both = ((2, nx, nv, NP, LANES), F32)
    coef = ((nv, NP, LANES), F32)
    scr = ((8, 8, LANES), F32)
    shell_rows = ((plan.panels, plan.width), F32)
    matrix = ((NP, plan.depth), BF16)

    def like(*arrays):
        return [(x.shape, x.dtype) for x in arrays]

    one_panel = (shell_inverse.shape[1:], BF16)
    inputs = (
        tangent_rhs.reshape(nv, NP, LANES), adjoint_rhs.reshape(nv, NP, LANES),
        jacobians.reshape(3, nv, nv, LANES), second_order.reshape(nv, 1, LANES),
        iface_elem, iface_node, iface_weight,
    )
    (packed,) = call(
        pack_kernel, plan, [((groups, plan.rows, LANES), BF16)],
        like(*inputs)
        + [((4 * plan.per, 8, LANES), F32), pltpu.SMEM(iface_count.shape, iface_count.dtype)],
        len(inputs) + 1, (), inputs + (iface_count,), (), None,
    )
    slab = lax.all_to_all(packed, flow, split_axis=0, concat_axis=0, tiled=True)
    forward, backward, solved = call(
        prepare_kernel, plan, [matrix, matrix, ((8, plan.width), F32)],
        like(deriv, shell_load) + [one_panel], 3, (), (deriv, shell_load, shell_inverse), (),
    )
    adjoint, rhs, table, incidence, places, weights, sent = call(
        first_kernel, plan,
        [
            state, ((2,) + state[0], BF16), ((nx, 4 * plan.per, 8, LANES), F32),
            ((plan.nodes, nx * plan.slots), BF16), ((nx, LANES, plan.slots), BF16),
            ((nx, 1, plan.slots), F32), ((groups * ns, 8, LANES), BF16),
        ],
        [both, state, coef, scr] + like(coupling), 1,
        (slab, backward, solved), (coupling,), (penalty,),
    )
    received = lax.all_to_all(sent, everyone, split_axis=0, concat_axis=0, tiled=True)
    tangent, adjoint_rounded, sent = call(
        second_kernel, plan,
        [state, ((nx, nv * NP, LANES), BF16), ((groups * ns, 16, LANES), BF16)],
        [both, state, coef, scr, shell_rows]
        + like(coupling, shell_load, shell_adjoint_rhs) + [one_panel], 4,
        (received, adjoint, rhs, table, incidence, places, weights, forward, backward),
        (coupling, shell_load, shell_adjoint_rhs, shell_inverse), (penalty,),
    )
    received = lax.all_to_all(sent, everyone, split_axis=0, concat_axis=0, tiled=True)
    (sent,) = call(
        third_kernel, plan, [((groups, plan.field_rows, LANES), BF16)],
        [both, state, coef, scr, shell_rows] + like(coupling), 1,
        (received, tangent, adjoint_rounded, rhs, table, incidence, places, weights, forward),
        (coupling,), (penalty,),
    )
    shell_shape = (shell_load.shape, F32)
    shell_tangent, shell_adjoint = call(
        shell_kernel, plan, [shell_shape, shell_shape],
        like(shell_load, shell_adjoint_rhs, shell_inverse), 3,
        (received,), (shell_load, shell_adjoint_rhs, shell_inverse), (),
    )
    received = lax.all_to_all(sent, flow, split_axis=0, concat_axis=0, tiled=True)
    tangent, adjoint = call(
        last_kernel, plan, [((nv, NP, LANES), BF16)] * 2, [], 0, (received,), (), ()
    )
    return (
        tangent.reshape(tangent_rhs.shape), adjoint.reshape(adjoint_rhs.shape),
        shell_tangent, shell_adjoint,
    )


def body(*args):
    tangent_rhs, shell_inverse, shell_load, iface_elem = args[0], args[7], args[8], args[10]
    nx, ny, ns = (lax.axis_size(name) for name in ("fx", "fy", "st"))
    panels, width = shell_inverse.shape[0] * ns, shell_load.shape[2]
    if fits(nx, ny, ns, tangent_rhs.shape, iface_elem.shape[1], panels, width):
        plan = Plan(nx, ny, ns, tangent_rhs.shape[1], tangent_rhs.shape[5], panels, width)
        return slab_body(plan, *args)
    return halo_body(*args)


def solution(mesh):
    in_specs = (
        P("st", None, None, "fx", "fy", None),
        P("st", None, None, "fx", "fy", None),
        P(None, None, None, "fx", "fy", None),
        P(),
        P(),
        P(None, "fx", "fy", None),
        P(),
        P("st", None, None),
        P(None, "st", None),
        P(None, "st", None),
        P(("fx", "fy"), None),
        P(("fx", "fy"), None),
        P(("fx", "fy"), None),
        P(("fx", "fy")),
    )
    out_specs = (
        P("st", None, None, "fx", "fy", None),
        P("st", None, None, "fx", "fy", None),
        P(None, "st", None),
        P(None, "st", None),
    )
    return jax.shard_map(body, mesh=mesh, in_specs=in_specs, out_specs=out_specs, check_vma=False)
```

```python
import functools

import jax
import jax.numpy as jnp
from jax import lax
from jax.experimental import pallas as pl
from jax.experimental.pallas import tpu as pltpu
from jax.sharding import PartitionSpec as P

SDOF = 6
PN = 64
NP = 64
FSWEEP = 3
ROUNDS = 2
LANES = 128
KERNEL_VMEM = 32 * 1024 * 1024
F32 = jnp.float32
BF16 = jnp.bfloat16


SIGMA = 0.5


def with_halo(value, sides, width):
    for axis, dim in sides:
        peers, length = (lax.axis_size(axis), value.shape[dim])
        up = [(i, (i + 1) % peers) for i in range(peers - 1)]
        down = [(j, i) for i, j in up]
        last = lax.slice_in_dim(value, length - width, length, axis=dim)
        initial = lax.slice_in_dim(value, 0, width, axis=dim)
        before = lax.ppermute(last, axis, up)
        after = lax.ppermute(initial, axis, down)
        value = jnp.concatenate([before, value, after], axis=dim)
    return value


def face_pair(lower_face, upper_face, below, above, axis):
    length = lower_face.shape[axis]
    beyond_upper = jnp.concatenate(
        [lax.slice_in_dim(lower_face, 1, length, axis=axis), above], axis=axis
    )
    beyond_lower = jnp.concatenate(
        [below, lax.slice_in_dim(upper_face, 0, length - 1, axis=axis)], axis=axis
    )
    return (lower_face - beyond_lower, upper_face - beyond_upper)


def place_faces(jump_low, jump_high, axis):
    middle_shape = list(jump_low.shape)
    middle_shape.insert(axis, 2)
    middle = jnp.zeros(middle_shape, jump_low.dtype)
    return jnp.concatenate(
        [jnp.expand_dims(jump_low, axis), middle, jnp.expand_dims(jump_high, axis)], axis=axis
    )


def as_cube(values):
    members, variables, points, size_x, size_y, size_z = values.shape
    return values.reshape(members, variables, 4, 4, 4, size_x, size_y, size_z)


def face_edges(values):
    cube = as_cube(values)
    received = []
    for node_axis in (2, 3):
        elem_axis = node_axis + 2
        lower_face = jnp.take(cube, 0, axis=node_axis)
        upper_face = jnp.take(cube, 3, axis=node_axis)
        edges = jnp.concatenate([lower_face, upper_face], axis=elem_axis)
        if node_axis == 2:
            extended = with_halo(edges, (("fx", 4),), 1)
        else:
            extended = with_halo(edges, (("fy", 5),), 1)
        below = lax.slice_in_dim(extended, 0, 1, axis=elem_axis)
        above = lax.slice_in_dim(extended, 3, 4, axis=elem_axis)
        received.append((below, above))
    return received


def flow_jumps(values, received):
    cube = as_cube(values)
    result = jnp.zeros(cube.shape, jnp.float32)
    for node_axis in (2, 3, 4):
        elem_axis = node_axis + 2
        lower_face = jnp.take(cube, 0, axis=node_axis).astype(jnp.float32)
        upper_face = jnp.take(cube, 3, axis=node_axis).astype(jnp.float32)
        if received is None or node_axis == 4:
            below = jnp.zeros_like(lax.slice_in_dim(lower_face, 0, 1, axis=elem_axis))
            above = below
        else:
            below = received[node_axis - 2][0].astype(jnp.float32)
            above = received[node_axis - 2][1].astype(jnp.float32)
        jump_low, jump_high = face_pair(lower_face, upper_face, below, above, elem_axis)
        result = result + place_faces(jump_low, jump_high, node_axis)
    return result.reshape(values.shape)


def volume(values, deriv_mats, jac_mats):
    grads = jnp.einsum("kpq,vqxyz->kvpxyz", deriv_mats, values, preferred_element_type=jnp.float32)
    result = jnp.sum(jac_mats[0][:, :, None] * grads[0][None], axis=1)
    for axis_index in (1, 2):
        result = result + jnp.sum(
            jac_mats[axis_index][:, :, None] * grads[axis_index][None], axis=1
        )
    return result


def operator(states, operator_kinds, penalty):
    values = lax.optimization_barrier(states.astype(jnp.bfloat16))
    received = face_edges(values)
    jumps = flow_jumps(values, received)
    volumes = jnp.stack(
        [
            volume(values[member], operator_kinds[member][0], operator_kinds[member][1])
            for member in range(len(operator_kinds))
        ]
    )
    return states + volumes + penalty[None, :, None, None, None, None] * jumps


def halo_body(
    tangent_rhs,
    adjoint_rhs,
    jacobians,
    deriv,
    penalty,
    second_order,
    coupling,
    shell_inverse,
    shell_load,
    shell_adjoint_rhs,
    iface_elem,
    iface_node,
    iface_weight,
    iface_count,
):
    state_shape = tangent_rhs.shape
    variables = state_shape[1]
    points = state_shape[2]
    elements = state_shape[3] * state_shape[4] * state_shape[5]
    slots = iface_elem.shape[1]
    live = (jnp.arange(slots, dtype=jnp.int32) < iface_count[0]).astype(jnp.float32)
    weights = iface_weight[0] * live
    elem_index = iface_elem[0]
    node_index = iface_node[0]
    dof_rows = jnp.arange(SDOF, dtype=jnp.int32)[:, None]
    columns = (node_index // PN)[None, :] * (SDOF * PN) + dof_rows * PN + (node_index % PN)[None, :]
    forward_jac = jacobians.astype(jnp.float32)
    forward_kind = (deriv, forward_jac)
    backward_kind = (jnp.swapaxes(deriv, 1, 2), jnp.swapaxes(forward_jac, 1, 2))
    coupling_cols = coupling.T

    def shell_solve(rhs):
        return jnp.einsum(
            "pab,dpb->dpa",
            shell_inverse,
            rhs.astype(jnp.bfloat16),
            preferred_element_type=jnp.float32,
        )

    shell_tangent = shell_solve(shell_load)
    shell_adjoint = jnp.zeros(shell_load.shape, jnp.float32)
    tangent = jnp.zeros(state_shape, jnp.float32)
    adjoint = jnp.zeros(state_shape, jnp.float32)
    for round_index in range(ROUNDS):
        received = lax.all_to_all(
            shell_tangent.astype(jnp.bfloat16), "st", split_axis=0, concat_axis=1, tiled=True
        )
        picked = received.reshape(-1)[columns]
        pushed_cols = (
            jnp.dot(coupling_cols, picked, preferred_element_type=jnp.float32) * weights[None, :]
        )
        pushed = (
            jnp.zeros((variables * points, elements), jnp.float32)
            .at[:, elem_index]
            .add(pushed_cols)
        )
        force = tangent_rhs.astype(jnp.float32) - pushed.reshape(state_shape)
        adjoint_source = adjoint_rhs.astype(jnp.float32) + second_order[None, :, None] * tangent
        paired = jnp.concatenate([tangent, adjoint])
        sources = jnp.concatenate([force, adjoint_source])
        for sweep in range(FSWEEP):
            paired = paired + SIGMA * (
                sources - operator(paired, (forward_kind, backward_kind), penalty)
            )
        tangent = paired[:1]
        adjoint = paired[1:]
        adjoint_values = adjoint.astype(jnp.bfloat16).reshape(variables * points, elements)
        gathered = adjoint_values[:, elem_index]
        loads = jnp.dot(coupling, gathered, preferred_element_type=jnp.float32) * weights[None, :]
        panels = received.shape[1]
        partial_loads = jnp.zeros((panels * SDOF * PN,), jnp.float32).at[columns].add(loads)
        partial_loads = partial_loads.reshape(1, panels, SDOF * PN)
        summed = lax.psum(partial_loads, ("fx", "fy"))
        owned = lax.all_to_all(summed, "st", split_axis=1, concat_axis=0, tiled=True)
        shell_adjoint = shell_solve(shell_adjoint_rhs - owned)
        shell_tangent = shell_solve(shell_load + shell_adjoint)
    return (
        tangent.astype(jnp.bfloat16),
        adjoint.astype(jnp.bfloat16),
        shell_tangent,
        shell_adjoint,
    )


def _iota(shape, dim):
    return lax.broadcasted_iota(jnp.int32, shape, dim)


def _flag(cond):
    return jnp.where(cond, 1.0, 0.0)


def _nt(a, b):
    return lax.dot_general(a, b, (((1,), (1,)), ((), ())), preferred_element_type=F32)


def _nn(a, b):
    return lax.dot_general(a, b, (((1,), (0,)), ((), ())), preferred_element_type=F32)


def _tn(a, b):
    return lax.dot_general(a, b, (((0,), (0,)), ((), ())), preferred_element_type=F32)


def _split(x):
    high = x.astype(BF16)
    low = (x - high.astype(F32)).astype(BF16)
    return jnp.concatenate([high, low], axis=0)


def _fold(x):
    half = x.shape[0] // 2
    return x[:half] + x[half:]


def _roll(x, shift):
    shift = shift % LANES
    return x if shift == 0 else pltpu.roll(x, shift, 1)


class Plan:
    def __init__(self, nx, ny, ns, nv, span, panels, width):
        self.nx, self.ny, self.ns, self.nv = nx, ny, ns, nv
        self.span, self.panels, self.width = span, panels, width
        self.groups = nx * ny
        self.own = span // self.groups
        self.window = LANES // ny
        self.halo = (self.window - self.own) // 2
        self.held = panels // ns
        self.nodes = panels * PN
        self.tiles = width // LANES
        self.narrow = LANES // self.groups
        self.deps = 3 * nv * nv
        self.granules = 3 * nv + 1
        self.per = -(-self.granules // 4)
        self.field_rows = nv * 16
        self.rows = 2 * self.field_rows + self.per * 8 + 8
        self.depth = 7 * NP + 32
        self.slots = ny * LANES

    def rank(self):
        return lax.axis_index("fx") * self.ny + lax.axis_index("fy")


def fits(nx, ny, ns, local_shape, slots, panels, width):
    members, nv, points, size_x, size_y, span = local_shape
    groups = nx * ny
    if members != 1 or (size_x, size_y) != (1, 1) or points != NP or nv > 8 or nv % 2:
        return False
    if span != LANES or slots != LANES or span % groups or LANES % ny or LANES % groups:
        return False
    own, window = span // groups, LANES // ny
    if window * 4 != LANES or (window - own) % 2 or (window - own) // 2 < ROUNDS * FSWEEP - 1:
        return False
    if own * 8 != LANES or width != SDOF * PN or width % LANES or SDOF > 8:
        return False
    held = panels // ns
    if panels % ns or panels != 16 or groups % held or ns > 4:
        return False
    return (held + 1) * (width // LANES) <= 16 and 8 % held == 0


def shell_solve_rows(plan, rhs, inverse_ref):
    rows = rhs.shape[0]
    rounded = rhs.astype(BF16)
    member = _iota((rows, plan.width), 0) % plan.held
    result = jnp.zeros((rows, plan.width), F32)
    for panel in range(plan.held):
        result = jnp.where(member == panel, _nt(rounded, inverse_ref[panel]), result)
    return result


def member_rows(plan, ref, panel):
    rows = [ref[d, pl.ds(panel, 1), :] for d in range(plan.ns)]
    rows.append(jnp.zeros((8 - plan.ns, plan.width), F32))
    return jnp.concatenate(rows, axis=0)


def fetch(pairs, sems):
    copies = [
        pltpu.make_async_copy(source, target, sems.at[i])
        for i, (source, target) in enumerate(pairs)
    ]
    for copy in copies:
        copy.start()
    return copies


def stacked(ref, count):
    return jnp.concatenate([ref[d] for d in range(count)], axis=0)


def pack_kernel(
    plan, trhs_hbm, arhs_hbm, jac_hbm, second_hbm, elem_hbm, node_hbm, weight_hbm, count_hbm,
    out_hbm, trhs, arhs, jac, second, elem, node, weight, count, scr, out, sems,
):
    nv, window = plan.nv, plan.window
    copies = fetch(
        (
            (trhs_hbm, trhs), (arhs_hbm, arhs), (jac_hbm, jac), (second_hbm, second),
            (elem_hbm, elem), (node_hbm, node), (weight_hbm, weight),
            (count_hbm, count),
        ),
        sems,
    )
    lane = _iota((1, LANES), 1)
    masks = []
    for dest in range(plan.groups):
        start = plan.own * dest - plan.halo
        row = []
        for k in range(4):
            z = start + lane % window
            row.append(_flag((lane // window == k) & (z >= 0) & (z < plan.span)))
        masks.append(row)

    def window_of(parts, dest, dtype):
        start = plan.own * dest - plan.halo
        total = None
        for k in range(4):
            term = _roll(parts[k], window * k - start) * masks[dest][k].astype(dtype)
            total = term if total is None else total + term
        return total

    sent = []

    def send(first, count):
        part = pl.ds(first, count)
        sem = sems.at[len(copies) + len(sent)]
        sent.append(pltpu.make_async_copy(out.at[:, part], out_hbm.at[:, part], sem))
        sent[-1].start()

    for f, ref in enumerate((trhs, arhs)):
        copies[f].wait()
        for a in range(nv):
            parts = [ref[a, pl.ds(16 * k, 16), :] for k in range(4)]
            for dest in range(plan.groups):
                out[dest, pl.ds((f * nv + a) * 16, 16), :] = window_of(parts, dest, BF16)
        send(f * plan.field_rows, plan.field_rows)

    for copy in copies[2:]:
        copy.wait()
    scr[...] = jnp.zeros(scr.shape, F32)
    for k in range(3):
        for a in range(nv):
            scr[k * nv + a, 0:nv, :] = jac[k, a].astype(F32)
    for a in range(nv):
        scr[3 * nv, a : a + 1, :] = second[a]
    quarter = [
        scr[pl.ds(plan.per * k, plan.per)].reshape(plan.per * 8, LANES) for k in range(4)
    ]
    live = _flag(lane < jnp.broadcast_to(count[...], (1, LANES)))
    scaled = weight[...] * live
    coarse = scaled.astype(BF16).astype(F32)
    panel = node[...] // PN
    upper = jnp.where(panel >= 8, 1, 0)
    table = [
        elem[...].astype(F32),
        (panel - 8 * upper).astype(F32),
        (node[...] - panel * PN + PN * upper).astype(F32),
        coarse,
        scaled - coarse,
        jnp.zeros((3, LANES), F32),
    ]
    table = jnp.concatenate(table, axis=0)
    for dest in range(plan.groups):
        block = jnp.concatenate([window_of(quarter, dest, F32), table], axis=0)
        first = 2 * plan.field_rows
        out[dest, pl.ds(first, plan.rows - first), :] = block.astype(BF16)
    send(2 * plan.field_rows, plan.rows - 2 * plan.field_rows)
    for copy in sent:
        copy.wait()


def coefficients(plan, penalty, coef, rank):
    point = _iota((NP, LANES), 0)
    ends = [point // 16, (point // 4) % 4, point % 4]
    faces = sum(_flag((e == 0) | (e == 3)) for e in ends)
    lane = _iota((16, LANES), 1)
    z = plan.own * rank - plan.halo + lane % plan.window
    inside = _flag((z >= 0) & (z < plan.span))
    rows = []
    for a in range(plan.nv):
        coef[a] = 0.5 - (0.5 * penalty[a]) * faces
        rows.append((penalty[a] * inside).astype(BF16))
    return rows


def sweeps(plan, count, state, source, table, matrix, transposed, coef, rows):
    nv, nx, window = plan.nv, plan.nx, plan.window
    lane = _iota((16, LANES), 1)
    not_last = _flag(lane < LANES - window).astype(BF16)
    not_first = _flag(lane >= window).astype(BF16)
    none = jnp.zeros((16, LANES), BF16)

    def plane(now, h, a, i):
        return state[now, h, a, pl.ds(16 * i, 16), :].astype(BF16)

    def flux(h, k, a, b):
        index, row = (k * nv + b, a) if transposed else (k * nv + a, b)
        line = table[h, index, pl.ds(row, 1), :]
        return jnp.broadcast_to(line, (16, LANES)).astype(BF16)

    for s in range(count):
        now, later = s % 2, (s + 1) % 2
        for h in range(nx):
            own = [[plane(now, h, b, i) for i in range(4)] for b in range(nv)]
            for a0 in range(0, nv, 2):
                stacks = []
                for a in (a0, a0 + 1):
                    parts = []
                    for k in range(3):
                        total = [None] * 4
                        for b in range(nv):
                            factor = flux(h, k, a, b)
                            for i in range(4):
                                term = own[b][i] * factor
                                total[i] = term if b == 0 else total[i] + term
                        parts += total
                    scaled = [own[a][i] * rows[a] for i in range(4)]
                    parts += [_roll(x, -window) * not_last for x in scaled]
                    parts += [_roll(x, window) * not_first for x in scaled]
                    parts += [_roll(x, -1) for x in scaled]
                    parts += [_roll(x, 1) for x in scaled]
                    parts.append(plane(now, h + 1, a, 0) * rows[a] if h + 1 < nx else none)
                    parts.append(plane(now, h - 1, a, 3) * rows[a] if h > 0 else none)
                    stacks.append(jnp.concatenate(parts, axis=0))
                product = _nn(matrix, jnp.concatenate(stacks, axis=1))
                for i, a in enumerate((a0, a0 + 1)):
                    value = coef[a] * state[now, h, a] + source[h, a]
                    state[later, h, a] = value + product[:, LANES * i : LANES * (i + 1)]
    return count % 2


def couple_rows(coupling):
    wide = coupling[...].astype(F32)
    pad = jnp.zeros((8 - SDOF, wide.shape[1]), F32)
    return jnp.concatenate([wide, pad], axis=0).astype(BF16)


def node_loads(plan, couple, values, hot, tile_hot, places, weights):
    lane = _iota((1, LANES), 1)
    place = lane % plan.window
    owned = _flag((place >= plan.halo) & (place < plan.halo + plan.own))
    picked = []
    for h in range(plan.nx):
        flow = _nn(couple, values[h]) * owned
        picked.append(_fold(_nn(_split(flow), places[h])))
    picked = jnp.concatenate(picked, axis=1) * weights[...]
    spread = [picked[c : c + 1] * tile_hot[...] for c in range(SDOF)]
    nodal = _fold(_nt(_split(jnp.concatenate(spread, axis=0)), hot[...]))
    left = _iota((8, LANES), 1) < PN
    low, high = [], []
    for t in range(plan.tiles):
        even, odd = nodal[16 * t : 16 * t + 8], nodal[16 * t + 8 : 16 * t + 16]
        low.append(jnp.where(left, even, _roll(odd, PN)))
        high.append(jnp.where(left, _roll(even, PN), odd))
    return low, high


def first_exchange(plan, low, high, solved, out):
    share = plan.groups // plan.held
    for dest in range(plan.ns):
        for panel in range(plan.held):
            q = dest * plan.held + panel
            rows = [(low[t] if q < 8 else high[t])[q % 8 : q % 8 + 1] for t in range(plan.tiles)]
            line = solved[dest : dest + 1]
            rows += [line[:, LANES * t : LANES * (t + 1)] for t in range(plan.tiles)]
            rows.append(jnp.zeros((8 - 2 * plan.tiles, LANES), F32))
            block = jnp.concatenate(rows, axis=0).astype(BF16)
            for g in range(panel * share, (panel + 1) * share):
                out[g * plan.ns + dest] = block


def second_exchange(plan, low, high, solved, out):
    for dest in range(plan.ns):
        rows = []
        first = dest * plan.held
        for t in range(plan.tiles):
            part = low[t] if first < 8 else high[t]
            rows.append(part[first % 8 : first % 8 + plan.held])
        line = solved[dest : dest + 1]
        rows += [line[:, LANES * t : LANES * (t + 1)] for t in range(plan.tiles)]
        used = (plan.held + 1) * plan.tiles
        if used < 16:
            rows.append(jnp.zeros((16 - used, LANES), F32))
        block = jnp.concatenate(rows, axis=0).astype(BF16)
        for g in range(plan.groups):
            out[g * plan.ns + dest] = block


def summed(plan, received):
    totals = []
    for d in range(plan.ns):
        total = received[d].astype(F32)
        for g in range(1, plan.groups):
            total = total + received[g * plan.ns + d].astype(F32)
        totals.append(total)
    return totals


def read_own_loads(plan, received):
    totals = summed(plan, received)
    tiles = []
    for t in range(plan.tiles):
        rows = [x[t : t + 1] for x in totals] + [jnp.zeros((8 - plan.ns, LANES), F32)]
        tiles.append(jnp.concatenate(rows, axis=0))
    return jnp.concatenate(tiles, axis=1)


def read_loads(plan, received):
    totals = summed(plan, received)
    tiles = []
    for t in range(plan.tiles):
        rows = [x[plan.held * t : plan.held * (t + 1)] for x in totals]
        tiles.append(jnp.concatenate(rows, axis=0))
    return jnp.concatenate(tiles, axis=1)


def push_force(
    plan, received, first, hot, tile_hot, places, weights, couple, rhs, shell_scr, scr, source
):
    span = plan.groups // plan.held
    for s in range(plan.ns):
        for panel in range(plan.held):
            block = received[panel * span * plan.ns + s].astype(F32)
            q = s * plan.held + panel
            for t in range(plan.tiles):
                line = block[first + t : first + t + 1]
                shell_scr[q : q + 1, LANES * t : LANES * (t + 1)] = line
    left = _iota((8, LANES), 1) < PN
    for t in range(plan.tiles):
        upper = shell_scr[0:8, LANES * t : LANES * (t + 1)]
        lower = shell_scr[8:16, LANES * t : LANES * (t + 1)]
        scr[2 * t] = jnp.where(left, upper, _roll(lower, PN))
        scr[2 * t + 1] = jnp.where(left, _roll(upper, PN), lower)
    for c in range(2 * plan.tiles, 8):
        scr[c] = jnp.zeros((8, LANES), F32)
    nodal = jnp.concatenate([scr[:, j, :] for j in range(8)], axis=0).astype(BF16)
    spread = _nn(nodal, hot[...])
    picked = sum(spread[8 * j : 8 * (j + 1)] * tile_hot[j : j + 1, :] for j in range(8))
    picked = picked * weights[...]
    twice = jnp.concatenate([couple, couple], axis=0)
    for h in range(plan.nx):
        part = picked[:, plan.slots * h : plan.slots * (h + 1)]
        dofs = _fold(_nt(_split(part), places[h]))
        push = _tn(twice, _split(dofs))
        for a in range(plan.nv):
            value = rhs[0, h, a].astype(F32) - push[NP * a : NP * (a + 1)]
            source[h, a] = 0.5 * value


def prepare_kernel(plan, deriv, load, inverse, forward, backward, solved):
    mine = plan.rank() // (plan.groups // plan.held)
    p, c = _iota((NP, plan.depth), 0), _iota((NP, plan.depth), 1)
    j, l = (p // 4) % 4, p % 4

    def block(n, ok, shift):
        return ok & (c - (3 + n) * NP == p + shift)

    links = block(0, j == 3, -12) | block(1, j == 0, 12)
    links = links | block(2, l == 3, -3) | block(3, l == 0, 3)
    links = links | ((p >= 48) & (c - 7 * NP == p - 48))
    links = links | ((p < 16) & (c - 7 * NP - 16 == p))
    base = (0.5 * _flag(links)).astype(BF16)
    forward[...] = base
    backward[...] = base
    for k in range(3):
        part = -0.5 * deriv[k].astype(F32)
        forward[:, NP * k : NP * (k + 1)] = part.astype(BF16)
        backward[:, NP * k : NP * (k + 1)] = part.T.astype(BF16)
    solved[...] = _nt(member_rows(plan, load, mine).astype(BF16), inverse[mine])


def first_kernel(
    plan, received, backward, solved, coupling, penalty,
    adjoint, rhs, table, hot, tile_hot, places, weights, out,
    state, source, coef,
):
    nv, window, nx, ny = plan.nv, plan.window, plan.nx, plan.ny
    rank = plan.rank()
    lane = _iota((1, LANES), 1)
    group = [_flag(lane // window == y) for y in range(ny)]

    def regroup(parts, k, dtype):
        total = None
        for y in range(ny):
            term = _roll(parts[y], window * (y - k)) * group[y].astype(dtype)
            total = term if total is None else total + term
        return total

    for h in range(nx):
        for f in range(2):
            for a in range(nv):
                first = (f * nv + a) * 16
                parts = [received[h * ny + y, pl.ds(first, 16), :] for y in range(ny)]
                for k in range(4):
                    rhs[f, h, a, pl.ds(16 * k, 16), :] = regroup(parts, k, BF16)
        first = 2 * plan.field_rows
        tails = [
            received[h * ny + y, pl.ds(first, plan.rows - first), :] for y in range(ny)
        ]
        for k in range(4):
            block = regroup(tails, k, BF16).astype(F32)
            for i in range(plan.per):
                table[h, k * plan.per + i] = block[8 * i : 8 * (i + 1)]
        info = [x.astype(F32)[plan.per * 8 :] for x in tails]
        place = _iota((LANES, LANES), 0)
        spot = _iota((8, LANES), 0)
        for y in range(ny):
            at = info[y]
            where = (at[0:1] - (plan.own * rank - plan.halo).astype(F32)).astype(jnp.int32)
            within = (where >= 0) & (where < window)
            target = jnp.where(within, where + y * window, -1)
            columns = pl.ds(LANES * y, LANES)
            places[h, :, columns] = _flag(place == target).astype(BF16)
            columns = pl.ds(plan.slots * h + LANES * y, LANES)
            weights[:, columns] = at[3:4] + at[4:5]
            tile_hot[:, columns] = _flag(spot == at[1:2].astype(jnp.int32))
            hot[:, columns] = _flag(place == at[2:3].astype(jnp.int32)).astype(BF16)

    rows = coefficients(plan, penalty, coef, rank)
    for h in range(nx):
        for a in range(nv):
            value = 0.5 * rhs[1, h, a].astype(F32)
            source[h, a] = value
            state[0, h, a] = value
    last = sweeps(plan, FSWEEP - 1, state, source, table, backward[...], True, coef, rows)
    values = [state[last, h].reshape(nv * NP, LANES).astype(BF16) for h in range(nx)]
    low, high = node_loads(plan, couple_rows(coupling), values, hot, tile_hot, places, weights)
    first_exchange(plan, low, high, solved[...], out)
    adjoint[...] = state[last]


def second_kernel(
    plan, received, adjoint_in, rhs, table, hot, tile_hot, places, weights, forward, backward,
    coupling, load, shell_rhs, inverse, penalty,
    tangent, adjoint_rounded, out,
    state, source, coef, scr, shell_scr,
):
    nv, nx = plan.nv, plan.nx
    rank = plan.rank()
    mine = rank // (plan.groups // plan.held)
    rows = coefficients(plan, penalty, coef, rank)
    shell = member_rows(plan, shell_rhs, mine) - read_own_loads(plan, received)
    shell = _nt(shell.astype(BF16), inverse[mine])
    shell = member_rows(plan, load, mine) + shell
    solved = _nt(shell.astype(BF16), inverse[mine])
    couple = couple_rows(coupling)
    push_force(
        plan, received, plan.tiles, hot, tile_hot, places, weights, couple, rhs, shell_scr, scr,
        source,
    )
    for h in range(nx):
        for a in range(nv):
            state[0, h, a] = source[h, a]
    last = sweeps(plan, FSWEEP - 1, state, source, table, forward[...], False, coef, rows)
    tangent[...] = state[last]
    for h in range(nx):
        for a in range(nv):
            extra = table[h, 3 * nv, a : a + 1, :] * state[last, h, a]
            source[h, a] = 0.5 * (rhs[1, h, a].astype(F32) + extra)
    for h in range(nx):
        for a in range(nv):
            state[0, h, a] = adjoint_in[h, a]
    last = sweeps(plan, FSWEEP, state, source, table, backward[...], True, coef, rows)
    values = []
    for h in range(nx):
        value = state[last, h].reshape(nv * NP, LANES).astype(BF16)
        adjoint_rounded[h] = value
        values.append(value)
    low, high = node_loads(plan, couple, values, hot, tile_hot, places, weights)
    second_exchange(plan, low, high, solved, out)


def third_kernel(
    plan, received, tangent_in, adjoint_rounded, rhs, table, hot, tile_hot, places, weights, forward,
    coupling, load, shell_rhs, inverse, penalty,
    out, shell_tangent, shell_adjoint,
    state, source, coef, scr, shell_scr,
):
    nv, nx, ny = plan.nv, plan.nx, plan.ny
    rank = plan.rank()
    rows = coefficients(plan, penalty, coef, rank)
    shell = stacked(shell_rhs, plan.ns) - read_loads(plan, received)
    shell = shell_solve_rows(plan, shell, inverse)
    solved = shell_solve_rows(plan, stacked(load, plan.ns) + shell, inverse)
    for d in range(plan.ns):
        shell_adjoint[d] = shell[plan.held * d : plan.held * (d + 1)]
        shell_tangent[d] = solved[plan.held * d : plan.held * (d + 1)]
    push_force(
        plan, received, plan.held * plan.tiles, hot, tile_hot, places, weights,
        couple_rows(coupling), rhs, shell_scr, scr, source,
    )
    for h in range(nx):
        for a in range(nv):
            state[0, h, a] = tangent_in[h, a]
    last = sweeps(plan, FSWEEP, state, source, table, forward[...], False, coef, rows)
    lane = _iota((16, LANES), 1)
    narrow = plan.narrow
    group = [_flag(lane // narrow == n).astype(BF16) for n in range(8)]
    for h in range(nx):
        for a in range(nv):
            parts = [state[last, h, a, pl.ds(16 * i, 16), :].astype(BF16) for i in range(4)]
            parts += [adjoint_rounded[h, pl.ds(a * NP + 16 * i, 16), :] for i in range(4)]
            for y in range(ny):
                total = None
                for n in range(8):
                    shift = narrow * n - plan.window * y - plan.halo
                    term = _roll(parts[n], shift) * group[n]
                    total = term if total is None else total + term
                out[h * ny + y, pl.ds(16 * a, 16), :] = total


def last_kernel(plan, received, tangent, adjoint):
    lane = _iota((16, LANES), 1)
    narrow = plan.narrow
    group = [_flag(lane // narrow == g).astype(BF16) for g in range(plan.groups)]
    for a in range(plan.nv):
        parts = [received[g, pl.ds(16 * a, 16), :] for g in range(plan.groups)]
        for f, ref in enumerate((tangent, adjoint)):
            for i in range(4):
                total = None
                for g in range(plan.groups):
                    term = _roll(parts[g], narrow * (g - 4 * f - i)) * group[g]
                    total = term if total is None else total + term
                ref[a, pl.ds(16 * i, 16), :] = total


def call(kernel, plan, out_shape, scratch, copies, on_chip, in_hbm, scalars, limit=KERNEL_VMEM,
         out_space=pltpu.VMEM):
    vmem = pl.BlockSpec(memory_space=pltpu.VMEM)
    hbm = pl.BlockSpec(memory_space=pltpu.HBM)
    smem = pl.BlockSpec(memory_space=pltpu.SMEM)
    specs = [vmem] * len(on_chip) + [hbm] * len(in_hbm) + [smem] * len(scalars)
    scratch_shapes = [pltpu.VMEM(s, d) for s, d in scratch]
    if copies:
        scratch_shapes.append(pltpu.SemaphoreType.DMA((copies,)))
    return pl.pallas_call(
        functools.partial(kernel, plan),
        out_shape=[jax.ShapeDtypeStruct(s, d) for s, d in out_shape],
        in_specs=specs,
        out_specs=[pl.BlockSpec(memory_space=out_space)] * len(out_shape),
        scratch_shapes=scratch_shapes,
        compiler_params=pltpu.CompilerParams(vmem_limit_bytes=limit),
    )(*on_chip, *in_hbm, *scalars)


def slab_body(
    plan, tangent_rhs, adjoint_rhs, jacobians, deriv, penalty, second_order, coupling,
    shell_inverse, shell_load, shell_adjoint_rhs, iface_elem, iface_node, iface_weight,
    iface_count,
):
    nv, nx, ns, groups = plan.nv, plan.nx, plan.ns, plan.groups
    flow, everyone = ("fx", "fy"), ("fx", "fy", "st")
    state = ((nx, nv, NP, LANES), F32)
    both = ((2, nx, nv, NP, LANES), F32)
    coef = ((nv, NP, LANES), F32)
    scr = ((8, 8, LANES), F32)
    shell_rows = ((plan.panels, plan.width), F32)
    matrix = ((NP, plan.depth), BF16)

    def like(*arrays):
        return [(x.shape, x.dtype) for x in arrays]

    inputs = (
        tangent_rhs.reshape(nv, NP, LANES), adjoint_rhs.reshape(nv, NP, LANES),
        jacobians.reshape(3, nv, nv, LANES), second_order.reshape(nv, 1, LANES),
        iface_elem, iface_node, iface_weight, iface_count.reshape(1, 1),
    )
    (packed,) = call(
        pack_kernel, plan, [((groups, plan.rows, LANES), BF16)],
        like(*inputs)
        + [((4 * plan.per, 8, LANES), F32), ((groups, plan.rows, LANES), BF16)],
        len(inputs) + 3, (), inputs, (), None, pltpu.HBM,
    )
    slab = lax.all_to_all(packed, flow, split_axis=0, concat_axis=0, tiled=True)
    forward, backward, solved = call(
        prepare_kernel, plan, [matrix, matrix, ((8, plan.width), F32)],
        [], 0, (deriv, shell_load, shell_inverse), (), (),
    )
    adjoint, rhs, table, hot, tile_hot, places, weights, sent = call(
        first_kernel, plan,
        [
            state, ((2,) + state[0], BF16), ((nx, 4 * plan.per, 8, LANES), F32),
            ((LANES, nx * plan.slots), BF16), ((8, nx * plan.slots), F32),
            ((nx, LANES, plan.slots), BF16), ((1, nx * plan.slots), F32),
            ((groups * ns, 8, LANES), BF16),
        ],
        [both, state, coef], 0, (slab, backward, solved, coupling), (), (penalty,),
    )
    received = lax.all_to_all(sent, everyone, split_axis=0, concat_axis=0, tiled=True)
    tangent, adjoint_rounded, sent = call(
        second_kernel, plan,
        [state, ((nx, nv * NP, LANES), BF16), ((groups * ns, 16, LANES), BF16)],
        [both, state, coef, scr, shell_rows], 0,
        (
            received, adjoint, rhs, table, hot, tile_hot, places, weights, forward, backward,
            coupling, shell_load, shell_adjoint_rhs, shell_inverse,
        ),
        (), (penalty,),
    )
    received = lax.all_to_all(sent, everyone, split_axis=0, concat_axis=0, tiled=True)
    shell_shape = (shell_load.shape, F32)
    sent, shell_tangent, shell_adjoint = call(
        third_kernel, plan,
        [((groups, plan.field_rows, LANES), BF16), shell_shape, shell_shape],
        [both, state, coef, scr, shell_rows], 0,
        (
            received, tangent, adjoint_rounded, rhs, table, hot, tile_hot, places, weights,
            forward, coupling, shell_load, shell_adjoint_rhs, shell_inverse,
        ),
        (), (penalty,),
    )
    received = lax.all_to_all(sent, flow, split_axis=0, concat_axis=0, tiled=True)
    tangent, adjoint = call(
        last_kernel, plan, [((nv, NP, LANES), BF16)] * 2, [], 0, (received,), (), ()
    )
    return (
        tangent.reshape(tangent_rhs.shape), adjoint.reshape(adjoint_rhs.shape),
        shell_tangent, shell_adjoint,
    )


def body(*args):
    tangent_rhs, shell_inverse, shell_load, iface_elem = args[0], args[7], args[8], args[10]
    nx, ny, ns = (lax.axis_size(name) for name in ("fx", "fy", "st"))
    panels, width = shell_inverse.shape[0] * ns, shell_load.shape[2]
    if fits(nx, ny, ns, tangent_rhs.shape, iface_elem.shape[1], panels, width):
        plan = Plan(nx, ny, ns, tangent_rhs.shape[1], tangent_rhs.shape[5], panels, width)
        return slab_body(plan, *args)
    return halo_body(*args)


def solution(mesh):
    in_specs = (
        P("st", None, None, "fx", "fy", None),
        P("st", None, None, "fx", "fy", None),
        P(None, None, None, "fx", "fy", None),
        P(),
        P(),
        P(None, "fx", "fy", None),
        P(),
        P("st", None, None),
        P(None, "st", None),
        P(None, "st", None),
        P(("fx", "fy"), None),
        P(("fx", "fy"), None),
        P(("fx", "fy"), None),
        P(("fx", "fy")),
    )
    out_specs = (
        P("st", None, None, "fx", "fy", None),
        P("st", None, None, "fx", "fy", None),
        P(None, "st", None),
        P(None, "st", None),
    )
    return jax.shard_map(body, mesh=mesh, in_specs=in_specs, out_specs=out_specs, check_vma=False)
```

```python
import functools

import jax
import jax.numpy as jnp
from jax import lax
from jax.experimental import pallas as pl
from jax.experimental.pallas import tpu as pltpu
from jax.sharding import PartitionSpec as P

SDOF = 6
PN = 64
NP = 64
FSWEEP = 3
ROUNDS = 2
LANES = 128
KERNEL_VMEM = 32 * 1024 * 1024
F32 = jnp.float32
BF16 = jnp.bfloat16


SIGMA = 0.5


def with_halo(value, sides, width):
    for axis, dim in sides:
        peers, length = (lax.axis_size(axis), value.shape[dim])
        up = [(i, (i + 1) % peers) for i in range(peers - 1)]
        down = [(j, i) for i, j in up]
        last = lax.slice_in_dim(value, length - width, length, axis=dim)
        initial = lax.slice_in_dim(value, 0, width, axis=dim)
        before = lax.ppermute(last, axis, up)
        after = lax.ppermute(initial, axis, down)
        value = jnp.concatenate([before, value, after], axis=dim)
    return value


def face_pair(lower_face, upper_face, below, above, axis):
    length = lower_face.shape[axis]
    beyond_upper = jnp.concatenate(
        [lax.slice_in_dim(lower_face, 1, length, axis=axis), above], axis=axis
    )
    beyond_lower = jnp.concatenate(
        [below, lax.slice_in_dim(upper_face, 0, length - 1, axis=axis)], axis=axis
    )
    return (lower_face - beyond_lower, upper_face - beyond_upper)


def place_faces(jump_low, jump_high, axis):
    middle_shape = list(jump_low.shape)
    middle_shape.insert(axis, 2)
    middle = jnp.zeros(middle_shape, jump_low.dtype)
    return jnp.concatenate(
        [jnp.expand_dims(jump_low, axis), middle, jnp.expand_dims(jump_high, axis)], axis=axis
    )


def as_cube(values):
    members, variables, points, size_x, size_y, size_z = values.shape
    return values.reshape(members, variables, 4, 4, 4, size_x, size_y, size_z)


def face_edges(values):
    cube = as_cube(values)
    received = []
    for node_axis in (2, 3):
        elem_axis = node_axis + 2
        lower_face = jnp.take(cube, 0, axis=node_axis)
        upper_face = jnp.take(cube, 3, axis=node_axis)
        edges = jnp.concatenate([lower_face, upper_face], axis=elem_axis)
        if node_axis == 2:
            extended = with_halo(edges, (("fx", 4),), 1)
        else:
            extended = with_halo(edges, (("fy", 5),), 1)
        below = lax.slice_in_dim(extended, 0, 1, axis=elem_axis)
        above = lax.slice_in_dim(extended, 3, 4, axis=elem_axis)
        received.append((below, above))
    return received


def flow_jumps(values, received):
    cube = as_cube(values)
    result = jnp.zeros(cube.shape, jnp.float32)
    for node_axis in (2, 3, 4):
        elem_axis = node_axis + 2
        lower_face = jnp.take(cube, 0, axis=node_axis).astype(jnp.float32)
        upper_face = jnp.take(cube, 3, axis=node_axis).astype(jnp.float32)
        if received is None or node_axis == 4:
            below = jnp.zeros_like(lax.slice_in_dim(lower_face, 0, 1, axis=elem_axis))
            above = below
        else:
            below = received[node_axis - 2][0].astype(jnp.float32)
            above = received[node_axis - 2][1].astype(jnp.float32)
        jump_low, jump_high = face_pair(lower_face, upper_face, below, above, elem_axis)
        result = result + place_faces(jump_low, jump_high, node_axis)
    return result.reshape(values.shape)


def volume(values, deriv_mats, jac_mats):
    grads = jnp.einsum("kpq,vqxyz->kvpxyz", deriv_mats, values, preferred_element_type=jnp.float32)
    result = jnp.sum(jac_mats[0][:, :, None] * grads[0][None], axis=1)
    for axis_index in (1, 2):
        result = result + jnp.sum(
            jac_mats[axis_index][:, :, None] * grads[axis_index][None], axis=1
        )
    return result


def operator(states, operator_kinds, penalty):
    values = lax.optimization_barrier(states.astype(jnp.bfloat16))
    received = face_edges(values)
    jumps = flow_jumps(values, received)
    volumes = jnp.stack(
        [
            volume(values[member], operator_kinds[member][0], operator_kinds[member][1])
            for member in range(len(operator_kinds))
        ]
    )
    return states + volumes + penalty[None, :, None, None, None, None] * jumps


def halo_body(
    tangent_rhs,
    adjoint_rhs,
    jacobians,
    deriv,
    penalty,
    second_order,
    coupling,
    shell_inverse,
    shell_load,
    shell_adjoint_rhs,
    iface_elem,
    iface_node,
    iface_weight,
    iface_count,
):
    state_shape = tangent_rhs.shape
    variables = state_shape[1]
    points = state_shape[2]
    elements = state_shape[3] * state_shape[4] * state_shape[5]
    slots = iface_elem.shape[1]
    live = (jnp.arange(slots, dtype=jnp.int32) < iface_count[0]).astype(jnp.float32)
    weights = iface_weight[0] * live
    elem_index = iface_elem[0]
    node_index = iface_node[0]
    dof_rows = jnp.arange(SDOF, dtype=jnp.int32)[:, None]
    columns = (node_index // PN)[None, :] * (SDOF * PN) + dof_rows * PN + (node_index % PN)[None, :]
    forward_jac = jacobians.astype(jnp.float32)
    forward_kind = (deriv, forward_jac)
    backward_kind = (jnp.swapaxes(deriv, 1, 2), jnp.swapaxes(forward_jac, 1, 2))
    coupling_cols = coupling.T

    def shell_solve(rhs):
        return jnp.einsum(
            "pab,dpb->dpa",
            shell_inverse,
            rhs.astype(jnp.bfloat16),
            preferred_element_type=jnp.float32,
        )

    shell_tangent = shell_solve(shell_load)
    shell_adjoint = jnp.zeros(shell_load.shape, jnp.float32)
    tangent = jnp.zeros(state_shape, jnp.float32)
    adjoint = jnp.zeros(state_shape, jnp.float32)
    for round_index in range(ROUNDS):
        received = lax.all_to_all(
            shell_tangent.astype(jnp.bfloat16), "st", split_axis=0, concat_axis=1, tiled=True
        )
        picked = received.reshape(-1)[columns]
        pushed_cols = (
            jnp.dot(coupling_cols, picked, preferred_element_type=jnp.float32) * weights[None, :]
        )
        pushed = (
            jnp.zeros((variables * points, elements), jnp.float32)
            .at[:, elem_index]
            .add(pushed_cols)
        )
        force = tangent_rhs.astype(jnp.float32) - pushed.reshape(state_shape)
        adjoint_source = adjoint_rhs.astype(jnp.float32) + second_order[None, :, None] * tangent
        paired = jnp.concatenate([tangent, adjoint])
        sources = jnp.concatenate([force, adjoint_source])
        for sweep in range(FSWEEP):
            paired = paired + SIGMA * (
                sources - operator(paired, (forward_kind, backward_kind), penalty)
            )
        tangent = paired[:1]
        adjoint = paired[1:]
        adjoint_values = adjoint.astype(jnp.bfloat16).reshape(variables * points, elements)
        gathered = adjoint_values[:, elem_index]
        loads = jnp.dot(coupling, gathered, preferred_element_type=jnp.float32) * weights[None, :]
        panels = received.shape[1]
        partial_loads = jnp.zeros((panels * SDOF * PN,), jnp.float32).at[columns].add(loads)
        partial_loads = partial_loads.reshape(1, panels, SDOF * PN)
        summed = lax.psum(partial_loads, ("fx", "fy"))
        owned = lax.all_to_all(summed, "st", split_axis=1, concat_axis=0, tiled=True)
        shell_adjoint = shell_solve(shell_adjoint_rhs - owned)
        shell_tangent = shell_solve(shell_load + shell_adjoint)
    return (
        tangent.astype(jnp.bfloat16),
        adjoint.astype(jnp.bfloat16),
        shell_tangent,
        shell_adjoint,
    )


def _iota(shape, dim):
    return lax.broadcasted_iota(jnp.int32, shape, dim)


def _flag(cond):
    return jnp.where(cond, 1.0, 0.0)


def _nt(a, b):
    return lax.dot_general(a, b, (((1,), (1,)), ((), ())), preferred_element_type=F32)


def _nn(a, b):
    return lax.dot_general(a, b, (((1,), (0,)), ((), ())), preferred_element_type=F32)


def _tn(a, b):
    return lax.dot_general(a, b, (((0,), (0,)), ((), ())), preferred_element_type=F32)


def _split(x):
    high = x.astype(BF16)
    low = (x - high.astype(F32)).astype(BF16)
    return jnp.concatenate([high, low], axis=0)


def _fold(x):
    half = x.shape[0] // 2
    return x[:half] + x[half:]


def _roll(x, shift):
    shift = shift % LANES
    return x if shift == 0 else pltpu.roll(x, shift, 1)


def swap_masks(count):
    group = _iota((16, LANES), 1) // (LANES // count)
    masks, step = [], 1
    while step < count:
        has = (group // step) % 2
        masks.append((_flag(has == 0).astype(BF16), _flag(has == 1).astype(BF16)))
        step *= 2
    return masks


def swap_groups(parts, masks):
    width = LANES // len(parts)
    for bit, (without, having) in enumerate(masks):
        step = 1 << bit
        swapped = list(parts)
        for a in range(len(parts)):
            if not a & step:
                x, y = parts[a], parts[a | step]
                swapped[a] = x * without + _roll(y, width * step) * having
                swapped[a | step] = y * having + _roll(x, -width * step) * without
        parts = swapped
    return parts


class Plan:
    def __init__(self, nx, ny, ns, nv, span, panels, width):
        self.nx, self.ny, self.ns, self.nv = nx, ny, ns, nv
        self.span, self.panels, self.width = span, panels, width
        self.groups = nx * ny
        self.own = span // self.groups
        self.window = LANES // ny
        self.halo = (self.window - self.own) // 2
        self.held = panels // ns
        self.nodes = panels * PN
        self.tiles = width // LANES
        self.deps = 3 * nv * nv
        self.granules = 3 * nv + 1
        self.per = -(-self.granules // 4)
        self.field_rows = nv * 16
        self.rows = 2 * self.field_rows + self.per * 8
        self.depth = 7 * NP + 32
        self.slots = ny * LANES
        self.shell_rows = 2 * ns * self.tiles

    def rank(self):
        return lax.axis_index("fx") * self.ny + lax.axis_index("fy")


def fits(nx, ny, ns, local_shape, slots, panels, width):
    members, nv, points, size_x, size_y, span = local_shape
    groups = nx * ny
    if members != 1 or (size_x, size_y) != (1, 1) or points != NP or nv > 6 or nv % 2:
        return False
    if span != LANES or slots != LANES or span % groups or LANES % ny or LANES % groups:
        return False
    own, window = span // groups, LANES // ny
    if window * 4 != LANES or (window - own) % 2 or (window - own) // 2 < ROUNDS * FSWEEP - 1:
        return False
    if own * 8 != LANES or width != SDOF * PN or width % LANES or SDOF > 8:
        return False
    held = panels // ns
    if panels % ns or panels != 16 or 8 % held or groups % held or groups < 2 * held:
        return False
    return ns <= 4 and 2 * (width // LANES) <= 8


def solve_steps(plan, received, load, shell_rhs, inverse, mine, result):
    def first():
        rows = member_rows(plan, shell_rhs, mine) - read_own_loads(plan, received)
        result.append(_nt(rows.astype(BF16), inverse[mine]))

    def second():
        rows = member_rows(plan, load, mine) + result[0]
        result.append(_nt(rows.astype(BF16), inverse[mine]))

    return [first, second]


def member_rows(plan, ref, panel):
    rows = [ref[d, pl.ds(panel, 1), :] for d in range(plan.ns)]
    rows.append(jnp.zeros((8 - plan.ns, plan.width), F32))
    return jnp.concatenate(rows, axis=0)


def fetch(pairs, sems):
    copies = [
        pltpu.make_async_copy(source, target, sems.at[i])
        for i, (source, target) in enumerate(pairs)
    ]
    for copy in copies:
        copy.start()
    return copies


def pack_kernel(
    plan, trhs_hbm, arhs_hbm, jac_hbm, second_hbm, elem_hbm, node_hbm, weight_hbm, count_hbm,
    out_hbm, trhs, arhs, jac, second, elem, node, weight, count, scr, out, sems,
):
    nv, window = plan.nv, plan.window
    copies = fetch(
        (
            (trhs_hbm, trhs), (arhs_hbm, arhs), (jac_hbm, jac), (second_hbm, second),
            (elem_hbm, elem), (node_hbm, node), (weight_hbm, weight),
            (count_hbm, count),
        ),
        sems,
    )
    lane = _iota((1, LANES), 1)
    masks = []
    for dest in range(plan.groups):
        start = plan.own * dest - plan.halo
        row = []
        for k in range(4):
            z = start + lane % window
            row.append(_flag((lane // window == k) & (z >= 0) & (z < plan.span)))
        masks.append(row)

    def window_of(parts, dest, dtype):
        start = plan.own * dest - plan.halo
        total = None
        for k in range(4):
            term = _roll(parts[k], window * k - start) * masks[dest][k].astype(dtype)
            total = term if total is None else total + term
        return total

    sent = []

    def send(first, count):
        part = pl.ds(first, count)
        sem = sems.at[len(copies) + len(sent)]
        sent.append(pltpu.make_async_copy(out.at[:, part], out_hbm.at[:, part], sem))
        sent[-1].start()

    for f, ref in enumerate((trhs, arhs)):
        copies[f].wait()
        for a in range(nv):
            parts = [ref[a, pl.ds(16 * k, 16), :] for k in range(4)]
            for dest in range(plan.groups):
                out[dest, pl.ds((f * nv + a) * 16, 16), :] = window_of(parts, dest, BF16)
        send(f * plan.field_rows, plan.field_rows)

    for copy in copies[2:]:
        copy.wait()
    scr[...] = jnp.zeros(scr.shape, F32)
    for k in range(3):
        for a in range(nv):
            scr[k * nv + a, 0:nv, :] = jac[k, a].astype(F32)
    for a in range(nv):
        scr[3 * nv, a : a + 1, :] = second[a]
    quarter = [
        scr[pl.ds(plan.per * k, plan.per)].reshape(plan.per * 8, LANES) for k in range(4)
    ]
    live = _flag(lane < jnp.broadcast_to(count[...], (1, LANES)))
    scaled = weight[...] * live
    coarse = scaled.astype(BF16).astype(F32)
    panel = node[...] // PN
    upper = jnp.where(panel >= 8, 1, 0)
    table = [
        elem[...].astype(F32),
        (panel - 8 * upper).astype(F32),
        (node[...] - panel * PN + PN * upper).astype(F32),
        coarse,
        scaled - coarse,
    ]
    row = _iota((8, LANES), 0)
    zero = jnp.zeros((8, LANES), F32)
    table = [jnp.where(row == 6, line, 0.0) for line in table] + [zero] * (plan.per - len(table))
    table = jnp.concatenate(table, axis=0)
    for dest in range(plan.groups):
        block = window_of(quarter, dest, F32) + table
        first = 2 * plan.field_rows
        out[dest, pl.ds(first, plan.rows - first), :] = block.astype(BF16)
    send(2 * plan.field_rows, plan.rows - 2 * plan.field_rows)
    for copy in sent:
        copy.wait()


def coefficients(plan, penalty, coef, rank):
    point = _iota((NP, LANES), 0)
    ends = [point // 16, (point // 4) % 4, point % 4]
    faces = sum(_flag((e == 0) | (e == 3)) for e in ends)
    lane = _iota((16, LANES), 1)
    z = plan.own * rank - plan.halo + lane % plan.window
    inside = _flag((z >= 0) & (z < plan.span))
    rows = []
    for a in range(plan.nv):
        coef[a] = 0.5 - (0.5 * penalty[a]) * faces
        rows.append((penalty[a] * inside).astype(BF16))
    return rows


def sweeps(plan, count, state, source, table, matrix, transposed, coef, rows, steps=()):
    nv, nx, window = plan.nv, plan.nx, plan.window
    lane = _iota((16, LANES), 1)
    not_last = _flag(lane < LANES - window).astype(BF16)
    not_first = _flag(lane >= window).astype(BF16)
    none = jnp.zeros((16, LANES), BF16)

    def plane(now, h, a, i):
        return state[now, h, a, pl.ds(16 * i, 16), :].astype(BF16)

    def flux(h, k, a, b):
        index, row = (k * nv + b, a) if transposed else (k * nv + a, b)
        line = table[h, index, pl.ds(row, 1), :]
        return jnp.broadcast_to(line, (16, LANES)).astype(BF16)

    for s in range(count):
        now, later = s % 2, (s + 1) % 2
        for h in range(nx):
            if steps:
                steps.pop(0)()
            own = [[plane(now, h, b, i) for i in range(4)] for b in range(nv)]
            for a0 in range(0, nv, 2):
                stacks = []
                for a in (a0, a0 + 1):
                    parts = []
                    for k in range(3):
                        total = [None] * 4
                        for b in range(nv):
                            factor = flux(h, k, a, b)
                            for i in range(4):
                                term = own[b][i] * factor
                                total[i] = term if b == 0 else total[i] + term
                        parts += total
                    scaled = [own[a][i] * rows[a] for i in range(4)]
                    parts += [_roll(x, -window) * not_last for x in scaled]
                    parts += [_roll(x, window) * not_first for x in scaled]
                    parts += [_roll(x, -1) for x in scaled]
                    parts += [_roll(x, 1) for x in scaled]
                    parts.append(plane(now, h + 1, a, 0) * rows[a] if h + 1 < nx else none)
                    parts.append(plane(now, h - 1, a, 3) * rows[a] if h > 0 else none)
                    stacks.append(jnp.concatenate(parts, axis=0))
                product = _nn(matrix, jnp.concatenate(stacks, axis=1))
                for i, a in enumerate((a0, a0 + 1)):
                    value = coef[a] * state[now, h, a] + source[h, a]
                    state[later, h, a] = value + product[:, LANES * i : LANES * (i + 1)]
    return count % 2


def couple_rows(coupling):
    wide = coupling[...].astype(F32)
    pad = jnp.zeros((8 - SDOF, wide.shape[1]), F32)
    return jnp.concatenate([wide, pad], axis=0).astype(BF16)


def node_loads(plan, couple, values, hot, tile_hot, places, weights):
    lane = _iota((1, LANES), 1)
    place = lane % plan.window
    owned = _flag((place >= plan.halo) & (place < plan.halo + plan.own))
    picked = []
    for h in range(plan.nx):
        flow = _nn(couple, values[h]) * owned
        picked.append(_fold(_nn(_split(flow), places[h])))
    picked = jnp.concatenate(picked, axis=1) * weights[...]
    spread = [picked[c : c + 1] * tile_hot[...] for c in range(SDOF)]
    nodal = _fold(_nt(_split(jnp.concatenate(spread, axis=0)), hot[...]))
    left = _iota((8, LANES), 1) < PN
    low, high = [], []
    for t in range(plan.tiles):
        even, odd = nodal[16 * t : 16 * t + 8], nodal[16 * t + 8 : 16 * t + 16]
        low.append(jnp.where(left, even, _roll(odd, PN)))
        high.append(jnp.where(left, _roll(even, PN), odd))
    return low, high


def write_exchange(plan, low, high, solved, out):
    share, tiles = plan.groups // plan.held, plan.tiles
    row = _iota((8, LANES), 0)
    for dest in range(plan.ns):
        tail = jnp.zeros((8, LANES), F32)
        for t in range(tiles):
            part = pltpu.roll(solved[:, LANES * t : LANES * (t + 1)], (tiles + t - dest) % 8, 0)
            tail = jnp.where(row == tiles + t, part, tail)
        for panel in range(plan.held):
            q = dest * plan.held + panel
            block = tail
            for t in range(tiles):
                part = pltpu.roll(low[t] if q < 8 else high[t], (t - q) % 8, 0)
                block = jnp.where(row == t, part, block)
            block = block.astype(BF16)
            for g in range(panel * share, (panel + 1) * share):
                out[g * plan.ns + dest] = block


def summed(plan, received):
    totals = []
    for d in range(plan.ns):
        total = received[d].astype(F32)
        for g in range(1, plan.groups):
            total = total + received[g * plan.ns + d].astype(F32)
        totals.append(total)
    return totals


def read_own_loads(plan, received):
    totals = summed(plan, received)
    tiles = []
    for t in range(plan.tiles):
        rows = [x[t : t + 1] for x in totals] + [jnp.zeros((8 - plan.ns, LANES), F32)]
        tiles.append(jnp.concatenate(rows, axis=0))
    return jnp.concatenate(tiles, axis=1)


def push_force(
    plan, received, first, hot, tile_hot, places, weights, couple, rhs, shell_scr, scr, source
):
    span = plan.groups // plan.held
    for s in range(plan.ns):
        for panel in range(plan.held):
            block = received[panel * span * plan.ns + s].astype(F32)
            q = s * plan.held + panel
            for t in range(plan.tiles):
                line = block[first + t : first + t + 1]
                shell_scr[q : q + 1, LANES * t : LANES * (t + 1)] = line
    left = _iota((8, LANES), 1) < PN
    for t in range(plan.tiles):
        upper = shell_scr[0:8, LANES * t : LANES * (t + 1)]
        lower = shell_scr[8:16, LANES * t : LANES * (t + 1)]
        scr[2 * t] = jnp.where(left, upper, _roll(lower, PN))
        scr[2 * t + 1] = jnp.where(left, _roll(upper, PN), lower)
    for c in range(2 * plan.tiles, 8):
        scr[c] = jnp.zeros((8, LANES), F32)
    nodal = jnp.concatenate([scr[:, j, :] for j in range(8)], axis=0).astype(BF16)
    spread = _nn(nodal, hot[...])
    picked = sum(spread[8 * j : 8 * (j + 1)] * tile_hot[j : j + 1, :] for j in range(8))
    picked = picked * weights[...]
    twice = jnp.concatenate([couple, couple], axis=0)
    for h in range(plan.nx):
        part = picked[:, plan.slots * h : plan.slots * (h + 1)]
        dofs = _fold(_nt(_split(part), places[h]))
        push = _tn(twice, _split(dofs))
        for a in range(plan.nv):
            value = rhs[0, h, a].astype(F32) - push[NP * a : NP * (a + 1)]
            source[h, a] = 0.5 * value


def prepare_kernel(plan, deriv, load, inverse, forward, backward, solved):
    mine = plan.rank() // (plan.groups // plan.held)
    p, c = _iota((NP, plan.depth), 0), _iota((NP, plan.depth), 1)
    j, l = (p // 4) % 4, p % 4

    def block(n, ok, shift):
        return ok & (c - (3 + n) * NP == p + shift)

    links = block(0, j == 3, -12) | block(1, j == 0, 12)
    links = links | block(2, l == 3, -3) | block(3, l == 0, 3)
    links = links | ((p >= 48) & (c - 7 * NP == p - 48))
    links = links | ((p < 16) & (c - 7 * NP - 16 == p))
    base = (0.5 * _flag(links)).astype(BF16)
    forward[...] = base
    backward[...] = base
    for k in range(3):
        part = -0.5 * deriv[k].astype(F32)
        forward[:, NP * k : NP * (k + 1)] = part.astype(BF16)
        backward[:, NP * k : NP * (k + 1)] = part.T.astype(BF16)
    solved[...] = _nt(member_rows(plan, load, mine).astype(BF16), inverse[mine])


def first_kernel(
    plan, received, backward, solved, coupling, penalty,
    adjoint, rhs, table, hot, tile_hot, places, weights, out,
    state, source, coef,
):
    nv, window, nx, ny = plan.nv, plan.window, plan.nx, plan.ny
    rank = plan.rank()
    masks = swap_masks(ny)
    for h in range(nx):
        for f in range(2):
            for a in range(nv):
                first = (f * nv + a) * 16
                parts = [received[h * ny + y, pl.ds(first, 16), :] for y in range(ny)]
                for k, part in enumerate(swap_groups(parts, masks)):
                    rhs[f, h, a, pl.ds(16 * k, 16), :] = part
        first = 2 * plan.field_rows
        count = plan.rows - first
        tails = [received[h * ny + y, pl.ds(first, count), :] for y in range(ny)]
        info = [x.astype(F32).reshape(plan.per, 8, LANES) for x in tails]
        pieces = [[] for _ in range(ny)]
        for r in range(0, count, 16):
            size = min(16, count - r)
            parts = [received[h * ny + y, pl.ds(first + r, size), :] for y in range(ny)]
            short = [(a[:size], b[:size]) for a, b in masks]
            for k, part in enumerate(swap_groups(parts, short)):
                pieces[k] += [part.astype(F32)[i : i + 8] for i in range(0, size, 8)]
        for k in range(ny):
            for i in range(plan.per):
                table[h, k * plan.per + i] = pieces[k][i]
        place = _iota((LANES, LANES), 0)
        row = _iota((8, LANES), 0)
        for y in range(ny):
            elem, tile, spot, coarse, fine = [info[y][i, 6:7, :] for i in range(5)]
            where = (elem - (plan.own * rank - plan.halo).astype(F32)).astype(jnp.int32)
            within = (where >= 0) & (where < window)
            target = jnp.where(within, where + y * window, -1)
            columns = pl.ds(LANES * y, LANES)
            places[h, :, columns] = _flag(place == target).astype(BF16)
            columns = pl.ds(plan.slots * h + LANES * y, LANES)
            weights[:, columns] = coarse + fine
            tile_hot[:, columns] = _flag(row == tile.astype(jnp.int32))
            hot[:, columns] = _flag(place == spot.astype(jnp.int32)).astype(BF16)

    rows = coefficients(plan, penalty, coef, rank)
    for h in range(nx):
        for a in range(nv):
            value = 0.5 * rhs[1, h, a].astype(F32)
            source[h, a] = value
            state[0, h, a] = value
    last = sweeps(plan, FSWEEP - 1, state, source, table, backward[...], True, coef, rows)
    values = [state[last, h].reshape(nv * NP, LANES).astype(BF16) for h in range(nx)]
    low, high = node_loads(plan, couple_rows(coupling), values, hot, tile_hot, places, weights)
    write_exchange(plan, low, high, solved[...], out)
    adjoint[...] = state[last]


def second_kernel(
    plan, received, adjoint_in, rhs, table, hot, tile_hot, places, weights, forward, backward,
    coupling, load, shell_rhs, inverse, penalty,
    tangent, adjoint_last, out,
    state, source, coef, scr, shell_scr,
):
    nv, nx = plan.nv, plan.nx
    rank = plan.rank()
    mine = rank // (plan.groups // plan.held)
    rows = coefficients(plan, penalty, coef, rank)
    result = []
    steps = solve_steps(plan, received, load, shell_rhs, inverse, mine, result)
    couple = couple_rows(coupling)
    push_force(
        plan, received, plan.tiles, hot, tile_hot, places, weights, couple, rhs, shell_scr, scr,
        source,
    )
    for h in range(nx):
        for a in range(nv):
            state[0, h, a] = source[h, a]
    last = sweeps(plan, FSWEEP - 1, state, source, table, forward[...], False, coef, rows, steps)
    tangent[...] = state[last]
    for h in range(nx):
        for a in range(nv):
            extra = table[h, 3 * nv, a : a + 1, :] * state[last, h, a]
            source[h, a] = 0.5 * (rhs[1, h, a].astype(F32) + extra)
    for h in range(nx):
        for a in range(nv):
            state[0, h, a] = adjoint_in[h, a]
    last = sweeps(plan, FSWEEP, state, source, table, backward[...], True, coef, rows)
    values = []
    for h in range(nx):
        value = state[last, h].reshape(nv * NP, LANES).astype(BF16)
        adjoint_last[h] = value
        values.append(value)
    low, high = node_loads(plan, couple, values, hot, tile_hot, places, weights)
    write_exchange(plan, low, high, result[1], out)


def third_kernel(
    plan, received, tangent_in, adjoint_last, rhs, table, hot, tile_hot, places, weights, forward,
    coupling, load, shell_rhs, inverse, penalty,
    out,
    state, source, coef, scr, shell_scr,
):
    nv, nx, ny, ns = plan.nv, plan.nx, plan.ny, plan.ns
    rank, share = plan.rank(), plan.groups // plan.held
    rows = coefficients(plan, penalty, coef, rank)
    result = []
    steps = solve_steps(plan, received, load, shell_rhs, inverse, rank // share, result)
    push_force(
        plan, received, plan.tiles, hot, tile_hot, places, weights,
        couple_rows(coupling), rhs, shell_scr, scr, source,
    )
    for h in range(nx):
        for a in range(nv):
            state[0, h, a] = tangent_in[h, a]
    last = sweeps(plan, FSWEEP, state, source, table, forward[...], False, coef, rows, steps)
    shell = jnp.where(lax.rem(rank, share) == 0, result[0], result[1])
    tiles = [shell[:ns, LANES * t : LANES * (t + 1)] for t in range(plan.tiles)]
    shell = _split(jnp.concatenate(tiles, axis=0))
    for dest in range(plan.groups):
        out[dest, pl.ds(plan.field_rows, shell.shape[0]), :] = shell
    lane = _iota((16, LANES), 1)
    group = [_flag(lane // plan.own == n).astype(BF16) for n in range(plan.groups)]
    for h in range(nx):
        for a in range(nv):
            parts = [state[last, h, a, pl.ds(16 * i, 16), :].astype(BF16) for i in range(4)]
            parts += [adjoint_last[h, pl.ds(a * NP + 16 * i, 16), :] for i in range(4)]
            for y in range(ny):
                total = None
                for n in range(plan.groups):
                    shift = plan.own * n - plan.window * y - plan.halo
                    term = _roll(parts[n], shift) * group[n]
                    total = term if total is None else total + term
                out[h * ny + y, pl.ds(16 * a, 16), :] = total


def last_kernel(plan, received, tangent, adjoint, shell_tangent, shell_adjoint):
    share, ns = plan.groups // plan.held, plan.ns
    for panel in range(plan.held):
        for i, ref in enumerate((shell_adjoint, shell_tangent)):
            block = received[panel * share + i, pl.ds(plan.field_rows, plan.shell_rows), :]
            block = _fold(block.astype(F32))
            for t in range(plan.tiles):
                columns = pl.ds(LANES * t, LANES)
                ref[:, panel, columns] = block[ns * t : ns * (t + 1)]
    masks = swap_masks(plan.groups)
    for a in range(plan.nv):
        parts = [received[g, pl.ds(16 * a, 16), :] for g in range(plan.groups)]
        for n, part in enumerate(swap_groups(parts, masks)):
            (tangent, adjoint)[n // 4][a, pl.ds(16 * (n % 4), 16), :] = part


def call(kernel, plan, out_shape, scratch, copies, on_chip, in_hbm, scalars, limit=KERNEL_VMEM,
         out_space=pltpu.VMEM):
    vmem = pl.BlockSpec(memory_space=pltpu.VMEM)
    hbm = pl.BlockSpec(memory_space=pltpu.HBM)
    smem = pl.BlockSpec(memory_space=pltpu.SMEM)
    specs = [vmem] * len(on_chip) + [hbm] * len(in_hbm) + [smem] * len(scalars)
    scratch_shapes = [pltpu.VMEM(s, d) for s, d in scratch]
    if copies:
        scratch_shapes.append(pltpu.SemaphoreType.DMA((copies,)))
    return pl.pallas_call(
        functools.partial(kernel, plan),
        out_shape=[jax.ShapeDtypeStruct(s, d) for s, d in out_shape],
        in_specs=specs,
        out_specs=[pl.BlockSpec(memory_space=out_space)] * len(out_shape),
        scratch_shapes=scratch_shapes,
        compiler_params=pltpu.CompilerParams(vmem_limit_bytes=limit),
    )(*on_chip, *in_hbm, *scalars)


def slab_body(
    plan, tangent_rhs, adjoint_rhs, jacobians, deriv, penalty, second_order, coupling,
    shell_inverse, shell_load, shell_adjoint_rhs, iface_elem, iface_node, iface_weight,
    iface_count,
):
    nv, nx, ns, groups = plan.nv, plan.nx, plan.ns, plan.groups
    flow, everyone = ("fx", "fy"), ("fx", "fy", "st")
    state = ((nx, nv, NP, LANES), F32)
    both = ((2, nx, nv, NP, LANES), F32)
    coef = ((nv, NP, LANES), F32)
    scr = ((8, 8, LANES), F32)
    shell_rows = ((plan.panels, plan.width), F32)
    matrix = ((NP, plan.depth), BF16)

    def like(*arrays):
        return [(x.shape, x.dtype) for x in arrays]

    inputs = (
        tangent_rhs.reshape(nv, NP, LANES), adjoint_rhs.reshape(nv, NP, LANES),
        jacobians.reshape(3, nv, nv, LANES), second_order.reshape(nv, 1, LANES),
        iface_elem, iface_node, iface_weight, iface_count.reshape(1, 1),
    )
    (packed,) = call(
        pack_kernel, plan, [((groups, plan.rows, LANES), BF16)],
        like(*inputs)
        + [((4 * plan.per, 8, LANES), F32), ((groups, plan.rows, LANES), BF16)],
        len(inputs) + 3, (), inputs, (), None, pltpu.HBM,
    )
    slab = lax.all_to_all(packed, flow, split_axis=0, concat_axis=0, tiled=True)
    forward, backward, solved = call(
        prepare_kernel, plan, [matrix, matrix, ((8, plan.width), F32)],
        [], 0, (deriv, shell_load, shell_inverse), (), (),
    )
    adjoint, rhs, table, hot, tile_hot, places, weights, sent = call(
        first_kernel, plan,
        [
            state, ((2,) + state[0], BF16), ((nx, 4 * plan.per, 8, LANES), F32),
            ((LANES, nx * plan.slots), BF16), ((8, nx * plan.slots), F32),
            ((nx, LANES, plan.slots), BF16), ((1, nx * plan.slots), F32),
            ((groups * ns, 8, LANES), BF16),
        ],
        [both, state, coef], 0, (slab, backward, solved, coupling), (), (penalty,),
    )
    received = lax.all_to_all(sent, everyone, split_axis=0, concat_axis=0, tiled=True)
    tangent, adjoint_last, sent = call(
        second_kernel, plan,
        [state, ((nx, nv * NP, LANES), BF16), ((groups * ns, 8, LANES), BF16)],
        [both, state, coef, scr, shell_rows], 0,
        (
            received, adjoint, rhs, table, hot, tile_hot, places, weights, forward, backward,
            coupling, shell_load, shell_adjoint_rhs, shell_inverse,
        ),
        (), (penalty,),
    )
    received = lax.all_to_all(sent, everyone, split_axis=0, concat_axis=0, tiled=True)
    (sent,) = call(
        third_kernel, plan,
        [((groups, plan.field_rows + plan.shell_rows, LANES), BF16)],
        [both, state, coef, scr, shell_rows], 0,
        (
            received, tangent, adjoint_last, rhs, table, hot, tile_hot, places, weights,
            forward, coupling, shell_load, shell_adjoint_rhs, shell_inverse,
        ),
        (), (penalty,),
    )
    received = lax.all_to_all(sent, flow, split_axis=0, concat_axis=0, tiled=True)
    shell_shape = (shell_load.shape, F32)
    tangent, adjoint, shell_tangent, shell_adjoint = call(
        last_kernel, plan, [((nv, NP, LANES), BF16)] * 2 + [shell_shape] * 2, [], 0,
        (received,), (), (),
    )
    return (
        tangent.reshape(tangent_rhs.shape), adjoint.reshape(adjoint_rhs.shape),
        shell_tangent, shell_adjoint,
    )


def body(*args):
    tangent_rhs, shell_inverse, shell_load, iface_elem = args[0], args[7], args[8], args[10]
    nx, ny, ns = (lax.axis_size(name) for name in ("fx", "fy", "st"))
    panels, width = shell_inverse.shape[0] * ns, shell_load.shape[2]
    if fits(nx, ny, ns, tangent_rhs.shape, iface_elem.shape[1], panels, width):
        plan = Plan(nx, ny, ns, tangent_rhs.shape[1], tangent_rhs.shape[5], panels, width)
        return slab_body(plan, *args)
    return halo_body(*args)


def solution(mesh):
    in_specs = (
        P("st", None, None, "fx", "fy", None),
        P("st", None, None, "fx", "fy", None),
        P(None, None, None, "fx", "fy", None),
        P(),
        P(),
        P(None, "fx", "fy", None),
        P(),
        P("st", None, None),
        P(None, "st", None),
        P(None, "st", None),
        P(("fx", "fy"), None),
        P(("fx", "fy"), None),
        P(("fx", "fy"), None),
        P(("fx", "fy")),
    )
    out_specs = (
        P("st", None, None, "fx", "fy", None),
        P("st", None, None, "fx", "fy", None),
        P(None, "st", None),
        P(None, "st", None),
    )
    return jax.shard_map(body, mesh=mesh, in_specs=in_specs, out_specs=out_specs, check_vma=False)
```

```python
import functools

import jax
import jax.numpy as jnp
from jax import lax
from jax.experimental import pallas as pl
from jax.experimental.pallas import tpu as pltpu
from jax.sharding import PartitionSpec as P

SDOF = 6
PN = 64
NP = 64
FSWEEP = 3
ROUNDS = 2
LANES = 128
KERNEL_VMEM = 32 * 1024 * 1024
F32 = jnp.float32
BF16 = jnp.bfloat16


SIGMA = 0.5


def with_halo(value, sides, width):
    for axis, dim in sides:
        peers, length = (lax.axis_size(axis), value.shape[dim])
        up = [(i, (i + 1) % peers) for i in range(peers - 1)]
        down = [(j, i) for i, j in up]
        last = lax.slice_in_dim(value, length - width, length, axis=dim)
        initial = lax.slice_in_dim(value, 0, width, axis=dim)
        before = lax.ppermute(last, axis, up)
        after = lax.ppermute(initial, axis, down)
        value = jnp.concatenate([before, value, after], axis=dim)
    return value


def face_pair(lower_face, upper_face, below, above, axis):
    length = lower_face.shape[axis]
    beyond_upper = jnp.concatenate(
        [lax.slice_in_dim(lower_face, 1, length, axis=axis), above], axis=axis
    )
    beyond_lower = jnp.concatenate(
        [below, lax.slice_in_dim(upper_face, 0, length - 1, axis=axis)], axis=axis
    )
    return (lower_face - beyond_lower, upper_face - beyond_upper)


def place_faces(jump_low, jump_high, axis):
    middle_shape = list(jump_low.shape)
    middle_shape.insert(axis, 2)
    middle = jnp.zeros(middle_shape, jump_low.dtype)
    return jnp.concatenate(
        [jnp.expand_dims(jump_low, axis), middle, jnp.expand_dims(jump_high, axis)], axis=axis
    )


def as_cube(values):
    members, variables, points, size_x, size_y, size_z = values.shape
    return values.reshape(members, variables, 4, 4, 4, size_x, size_y, size_z)


def face_edges(values):
    cube = as_cube(values)
    received = []
    for node_axis in (2, 3):
        elem_axis = node_axis + 2
        lower_face = jnp.take(cube, 0, axis=node_axis)
        upper_face = jnp.take(cube, 3, axis=node_axis)
        edges = jnp.concatenate([lower_face, upper_face], axis=elem_axis)
        if node_axis == 2:
            extended = with_halo(edges, (("fx", 4),), 1)
        else:
            extended = with_halo(edges, (("fy", 5),), 1)
        below = lax.slice_in_dim(extended, 0, 1, axis=elem_axis)
        above = lax.slice_in_dim(extended, 3, 4, axis=elem_axis)
        received.append((below, above))
    return received


def flow_jumps(values, received):
    cube = as_cube(values)
    result = jnp.zeros(cube.shape, jnp.float32)
    for node_axis in (2, 3, 4):
        elem_axis = node_axis + 2
        lower_face = jnp.take(cube, 0, axis=node_axis).astype(jnp.float32)
        upper_face = jnp.take(cube, 3, axis=node_axis).astype(jnp.float32)
        if received is None or node_axis == 4:
            below = jnp.zeros_like(lax.slice_in_dim(lower_face, 0, 1, axis=elem_axis))
            above = below
        else:
            below = received[node_axis - 2][0].astype(jnp.float32)
            above = received[node_axis - 2][1].astype(jnp.float32)
        jump_low, jump_high = face_pair(lower_face, upper_face, below, above, elem_axis)
        result = result + place_faces(jump_low, jump_high, node_axis)
    return result.reshape(values.shape)


def volume(values, deriv_mats, jac_mats):
    grads = jnp.einsum("kpq,vqxyz->kvpxyz", deriv_mats, values, preferred_element_type=jnp.float32)
    result = jnp.sum(jac_mats[0][:, :, None] * grads[0][None], axis=1)
    for axis_index in (1, 2):
        result = result + jnp.sum(
            jac_mats[axis_index][:, :, None] * grads[axis_index][None], axis=1
        )
    return result


def operator(states, operator_kinds, penalty):
    values = lax.optimization_barrier(states.astype(jnp.bfloat16))
    received = face_edges(values)
    jumps = flow_jumps(values, received)
    volumes = jnp.stack(
        [
            volume(values[member], operator_kinds[member][0], operator_kinds[member][1])
            for member in range(len(operator_kinds))
        ]
    )
    return states + volumes + penalty[None, :, None, None, None, None] * jumps


def halo_body(
    tangent_rhs,
    adjoint_rhs,
    jacobians,
    deriv,
    penalty,
    second_order,
    coupling,
    shell_inverse,
    shell_load,
    shell_adjoint_rhs,
    iface_elem,
    iface_node,
    iface_weight,
    iface_count,
):
    state_shape = tangent_rhs.shape
    variables = state_shape[1]
    points = state_shape[2]
    elements = state_shape[3] * state_shape[4] * state_shape[5]
    slots = iface_elem.shape[1]
    live = (jnp.arange(slots, dtype=jnp.int32) < iface_count[0]).astype(jnp.float32)
    weights = iface_weight[0] * live
    elem_index = iface_elem[0]
    node_index = iface_node[0]
    dof_rows = jnp.arange(SDOF, dtype=jnp.int32)[:, None]
    columns = (node_index // PN)[None, :] * (SDOF * PN) + dof_rows * PN + (node_index % PN)[None, :]
    forward_jac = jacobians.astype(jnp.float32)
    forward_kind = (deriv, forward_jac)
    backward_kind = (jnp.swapaxes(deriv, 1, 2), jnp.swapaxes(forward_jac, 1, 2))
    coupling_cols = coupling.T

    def shell_solve(rhs):
        return jnp.einsum(
            "pab,dpb->dpa",
            shell_inverse,
            rhs.astype(jnp.bfloat16),
            preferred_element_type=jnp.float32,
        )

    shell_tangent = shell_solve(shell_load)
    shell_adjoint = jnp.zeros(shell_load.shape, jnp.float32)
    tangent = jnp.zeros(state_shape, jnp.float32)
    adjoint = jnp.zeros(state_shape, jnp.float32)
    for round_index in range(ROUNDS):
        received = lax.all_to_all(
            shell_tangent.astype(jnp.bfloat16), "st", split_axis=0, concat_axis=1, tiled=True
        )
        picked = received.reshape(-1)[columns]
        pushed_cols = (
            jnp.dot(coupling_cols, picked, preferred_element_type=jnp.float32) * weights[None, :]
        )
        pushed = (
            jnp.zeros((variables * points, elements), jnp.float32)
            .at[:, elem_index]
            .add(pushed_cols)
        )
        force = tangent_rhs.astype(jnp.float32) - pushed.reshape(state_shape)
        adjoint_source = adjoint_rhs.astype(jnp.float32) + second_order[None, :, None] * tangent
        paired = jnp.concatenate([tangent, adjoint])
        sources = jnp.concatenate([force, adjoint_source])
        for sweep in range(FSWEEP):
            paired = paired + SIGMA * (
                sources - operator(paired, (forward_kind, backward_kind), penalty)
            )
        tangent = paired[:1]
        adjoint = paired[1:]
        adjoint_values = adjoint.astype(jnp.bfloat16).reshape(variables * points, elements)
        gathered = adjoint_values[:, elem_index]
        loads = jnp.dot(coupling, gathered, preferred_element_type=jnp.float32) * weights[None, :]
        panels = received.shape[1]
        partial_loads = jnp.zeros((panels * SDOF * PN,), jnp.float32).at[columns].add(loads)
        partial_loads = partial_loads.reshape(1, panels, SDOF * PN)
        summed = lax.psum(partial_loads, ("fx", "fy"))
        owned = lax.all_to_all(summed, "st", split_axis=1, concat_axis=0, tiled=True)
        shell_adjoint = shell_solve(shell_adjoint_rhs - owned)
        shell_tangent = shell_solve(shell_load + shell_adjoint)
    return (
        tangent.astype(jnp.bfloat16),
        adjoint.astype(jnp.bfloat16),
        shell_tangent,
        shell_adjoint,
    )


def _iota(shape, dim):
    return lax.broadcasted_iota(jnp.int32, shape, dim)


def _flag(cond):
    return jnp.where(cond, 1.0, 0.0)


def _nt(a, b):
    return lax.dot_general(a, b, (((1,), (1,)), ((), ())), preferred_element_type=F32)


def _nn(a, b):
    return lax.dot_general(a, b, (((1,), (0,)), ((), ())), preferred_element_type=F32)


def _tn(a, b):
    return lax.dot_general(a, b, (((0,), (0,)), ((), ())), preferred_element_type=F32)


def _split(x):
    high = x.astype(BF16)
    low = (x - high.astype(F32)).astype(BF16)
    return jnp.concatenate([high, low], axis=0)


def _fold(x):
    half = x.shape[0] // 2
    return x[:half] + x[half:]


def _roll(x, shift):
    shift = shift % LANES
    return x if shift == 0 else pltpu.roll(x, shift, 1)


def swap_masks(count):
    group = _iota((16, LANES), 1) // (LANES // count)
    masks, step = [], 1
    while step < count:
        has = (group // step) % 2
        masks.append((_flag(has == 0).astype(BF16), _flag(has == 1).astype(BF16)))
        step *= 2
    return masks


def swap_groups(parts, masks):
    width = LANES // len(parts)
    for bit, (without, having) in enumerate(masks):
        step = 1 << bit
        swapped = list(parts)
        for a in range(len(parts)):
            if not a & step:
                x, y = parts[a], parts[a | step]
                swapped[a] = x * without + _roll(y, width * step) * having
                swapped[a | step] = y * having + _roll(x, -width * step) * without
        parts = swapped
    return parts


class Plan:
    def __init__(self, nx, ny, ns, nv, span, panels, width):
        self.nx, self.ny, self.ns, self.nv = nx, ny, ns, nv
        self.span, self.panels, self.width = span, panels, width
        self.groups = nx * ny
        self.own = span // self.groups
        self.window = LANES // ny
        self.halo = (self.window - self.own) // 2
        self.held = panels // ns
        self.nodes = panels * PN
        self.tiles = width // LANES
        self.deps = 3 * nv * nv
        self.granules = 3 * nv + 1
        self.per = -(-self.granules // 4)
        self.field_rows = nv * 16
        self.rows = 2 * self.field_rows + self.per * 8
        self.depth = 7 * NP + 32
        self.slots = ny * LANES
        self.shell_rows = 2 * ns * self.tiles

    def rank(self):
        return lax.axis_index("fx") * self.ny + lax.axis_index("fy")


def fits(nx, ny, ns, local_shape, slots, panels, width):
    members, nv, points, size_x, size_y, span = local_shape
    groups = nx * ny
    if members != 1 or (size_x, size_y) != (1, 1) or points != NP or nv > 6 or nv % 2:
        return False
    if span != LANES or slots != LANES or span % groups or LANES % ny or LANES % groups:
        return False
    own, window = span // groups, LANES // ny
    if window * 4 != LANES or (window - own) % 2 or (window - own) // 2 < ROUNDS * FSWEEP - 1:
        return False
    if own * 8 != LANES or width != SDOF * PN or width % LANES or SDOF > 8:
        return False
    held = panels // ns
    if panels % ns or panels != 16 or 8 % held or groups % held or groups < 2 * held:
        return False
    return ns <= 4 and 2 * (width // LANES) <= 8


def solve_steps(plan, received, load, shell_rhs, inverse, mine, result):
    def first():
        rows = member_rows(plan, shell_rhs, mine) - read_own_loads(plan, received)
        result.append(_nt(rows.astype(BF16), inverse[mine]))

    def second():
        rows = member_rows(plan, load, mine) + result[0]
        result.append(_nt(rows.astype(BF16), inverse[mine]))

    return [first, second]


def member_rows(plan, ref, panel):
    rows = [ref[d, pl.ds(panel, 1), :] for d in range(plan.ns)]
    rows.append(jnp.zeros((8 - plan.ns, plan.width), F32))
    return jnp.concatenate(rows, axis=0)


def fetch(pairs, sems):
    copies = [
        pltpu.make_async_copy(source, target, sems.at[i])
        for i, (source, target) in enumerate(pairs)
    ]
    for copy in copies:
        copy.start()
    return copies


def pack_kernel(
    plan, trhs_hbm, arhs_hbm, jac_hbm, second_hbm, elem_hbm, node_hbm, weight_hbm, count_hbm,
    out_hbm, trhs, arhs, jac, second, elem, node, weight, count, scr, out, sems,
):
    nv, window = plan.nv, plan.window
    copies = fetch(
        (
            (trhs_hbm, trhs), (arhs_hbm, arhs), (jac_hbm, jac), (second_hbm, second),
            (elem_hbm, elem), (node_hbm, node), (weight_hbm, weight),
            (count_hbm, count),
        ),
        sems,
    )
    lane = _iota((1, LANES), 1)
    masks = []
    for dest in range(plan.groups):
        start = plan.own * dest - plan.halo
        row = []
        for k in range(4):
            z = start + lane % window
            row.append(_flag((lane // window == k) & (z >= 0) & (z < plan.span)))
        masks.append(row)

    def window_of(parts, dest, dtype):
        start = plan.own * dest - plan.halo
        total = None
        for k in range(4):
            term = _roll(parts[k], window * k - start) * masks[dest][k].astype(dtype)
            total = term if total is None else total + term
        return total

    sent = []

    def send(first, count):
        part = pl.ds(first, count)
        sem = sems.at[len(copies) + len(sent)]
        sent.append(pltpu.make_async_copy(out.at[:, part], out_hbm.at[:, part], sem))
        sent[-1].start()

    for f, ref in enumerate((trhs, arhs)):
        copies[f].wait()
        for a in range(nv):
            parts = [ref[a, pl.ds(16 * k, 16), :] for k in range(4)]
            for dest in range(plan.groups):
                out[dest, pl.ds((f * nv + a) * 16, 16), :] = window_of(parts, dest, BF16)
        send(f * plan.field_rows, plan.field_rows)

    for copy in copies[2:]:
        copy.wait()
    scr[...] = jnp.zeros(scr.shape, F32)
    for k in range(3):
        for a in range(nv):
            scr[k * nv + a, 0:nv, :] = jac[k, a].astype(F32)
    for a in range(nv):
        scr[3 * nv, a : a + 1, :] = second[a]
    quarter = [
        scr[pl.ds(plan.per * k, plan.per)].reshape(plan.per * 8, LANES) for k in range(4)
    ]
    live = _flag(lane < jnp.broadcast_to(count[...], (1, LANES)))
    scaled = weight[...] * live
    coarse = scaled.astype(BF16).astype(F32)
    panel = node[...] // PN
    upper = jnp.where(panel >= 8, 1, 0)
    table = [
        elem[...].astype(F32),
        (panel - 8 * upper).astype(F32),
        (node[...] - panel * PN + PN * upper).astype(F32),
        coarse,
        scaled - coarse,
    ]
    row = _iota((8, LANES), 0)
    zero = jnp.zeros((8, LANES), F32)
    table = [jnp.where(row == 6, line, 0.0) for line in table] + [zero] * (plan.per - len(table))
    table = jnp.concatenate(table, axis=0)
    for dest in range(plan.groups):
        block = window_of(quarter, dest, F32) + table
        first = 2 * plan.field_rows
        out[dest, pl.ds(first, plan.rows - first), :] = block.astype(BF16)
    send(2 * plan.field_rows, plan.rows - 2 * plan.field_rows)
    for copy in sent:
        copy.wait()


def coefficients(plan, penalty, coef, strength):
    point = _iota((NP, LANES), 0)
    ends = [point // 16, (point // 4) % 4, point % 4]
    faces = sum(_flag((e == 0) | (e == 3)) for e in ends)
    lane = _iota((16, LANES), 1)
    z = plan.own * plan.rank() - plan.halo + lane % plan.window
    inside = _flag((z >= 0) & (z < plan.span))
    for a in range(plan.nv):
        coef[a] = 0.5 - (0.5 * penalty[a]) * faces
        strength[a] = penalty[a] * inside


def sweeps(plan, states, source, table, matrix, transposed, coef, strength, steps=()):
    nv, nx, window = plan.nv, plan.nx, plan.window
    lane = _iota((16, LANES), 1)
    not_last = _flag(lane < LANES - window).astype(BF16)
    not_first = _flag(lane >= window).astype(BF16)
    none = jnp.zeros((16, LANES), BF16)
    rows = [strength[a].astype(BF16) for a in range(nv)]

    def plane(state, h, a, i):
        return state[h, a, pl.ds(16 * i, 16), :].astype(BF16)

    def flux(h, k, a, b):
        index, row = (k * nv + b, a) if transposed else (k * nv + a, b)
        line = table[h, index, pl.ds(row, 1), :]
        return jnp.broadcast_to(line, (16, LANES)).astype(BF16)

    for now, later in zip(states[:-1], states[1:]):
        for h in range(nx):
            if steps:
                steps.pop(0)()
            own = [[plane(now, h, b, i) for i in range(4)] for b in range(nv)]
            for a0 in range(0, nv, 2):
                stacks = []
                for a in (a0, a0 + 1):
                    parts = []
                    for k in range(3):
                        total = [None] * 4
                        for b in range(nv):
                            factor = flux(h, k, a, b)
                            for i in range(4):
                                term = own[b][i] * factor
                                total[i] = term if b == 0 else total[i] + term
                        parts += total
                    scaled = [own[a][i] * rows[a] for i in range(4)]
                    parts += [_roll(x, -window) * not_last for x in scaled]
                    parts += [_roll(x, window) * not_first for x in scaled]
                    parts += [_roll(x, -1) for x in scaled]
                    parts += [_roll(x, 1) for x in scaled]
                    parts.append(plane(now, h + 1, a, 0) * rows[a] if h + 1 < nx else none)
                    parts.append(plane(now, h - 1, a, 3) * rows[a] if h > 0 else none)
                    stacks.append(jnp.concatenate(parts, axis=0))
                product = _nn(matrix, jnp.concatenate(stacks, axis=1))
                for i, a in enumerate((a0, a0 + 1)):
                    value = coef[a] * now[h, a] + source[h, a]
                    later[h, a] = value + product[:, LANES * i : LANES * (i + 1)]


def chain(start, refs, count):
    return [start] + [refs[(i - count) % len(refs)] for i in range(count)]


def couple_rows(coupling):
    wide = coupling[...].astype(F32)
    pad = jnp.zeros((8 - SDOF, wide.shape[1]), F32)
    return jnp.concatenate([wide, pad], axis=0).astype(BF16)


def node_loads(plan, couple, values, hot, tile_hot, places, weights):
    lane = _iota((1, LANES), 1)
    place = lane % plan.window
    owned = _flag((place >= plan.halo) & (place < plan.halo + plan.own))
    picked = []
    for h in range(plan.nx):
        flow = _nn(couple, values[h]) * owned
        picked.append(_fold(_nn(_split(flow), places[h])))
    picked = jnp.concatenate(picked, axis=1) * weights[...]
    spread = [picked[c : c + 1] * tile_hot[...] for c in range(SDOF)]
    nodal = _fold(_nt(_split(jnp.concatenate(spread, axis=0)), hot[...]))
    left = _iota((8, LANES), 1) < PN
    low, high = [], []
    for t in range(plan.tiles):
        even, odd = nodal[16 * t : 16 * t + 8], nodal[16 * t + 8 : 16 * t + 16]
        low.append(jnp.where(left, even, _roll(odd, PN)))
        high.append(jnp.where(left, _roll(even, PN), odd))
    return low, high


def write_exchange(plan, low, high, solved, out):
    share, tiles = plan.groups // plan.held, plan.tiles
    row = _iota((8, LANES), 0)
    for dest in range(plan.ns):
        tail = jnp.zeros((8, LANES), F32)
        for t in range(tiles):
            part = pltpu.roll(solved[:, LANES * t : LANES * (t + 1)], (tiles + t - dest) % 8, 0)
            tail = jnp.where(row == tiles + t, part, tail)
        for panel in range(plan.held):
            q = dest * plan.held + panel
            block = tail
            for t in range(tiles):
                part = pltpu.roll(low[t] if q < 8 else high[t], (t - q) % 8, 0)
                block = jnp.where(row == t, part, block)
            block = block.astype(BF16)
            for g in range(panel * share, (panel + 1) * share):
                out[g * plan.ns + dest] = block


def summed(plan, received):
    totals = []
    for d in range(plan.ns):
        total = received[d].astype(F32)
        for g in range(1, plan.groups):
            total = total + received[g * plan.ns + d].astype(F32)
        totals.append(total)
    return totals


def read_own_loads(plan, received):
    totals = summed(plan, received)
    tiles = []
    for t in range(plan.tiles):
        rows = [x[t : t + 1] for x in totals] + [jnp.zeros((8 - plan.ns, LANES), F32)]
        tiles.append(jnp.concatenate(rows, axis=0))
    return jnp.concatenate(tiles, axis=1)


def push_force(
    plan, received, first, hot, tile_hot, places, weights, couple, rhs, shell_scr, scr, source
):
    span = plan.groups // plan.held
    for s in range(plan.ns):
        for panel in range(plan.held):
            block = received[panel * span * plan.ns + s].astype(F32)
            q = s * plan.held + panel
            for t in range(plan.tiles):
                line = block[first + t : first + t + 1]
                shell_scr[q : q + 1, LANES * t : LANES * (t + 1)] = line
    left = _iota((8, LANES), 1) < PN
    for t in range(plan.tiles):
        upper = shell_scr[0:8, LANES * t : LANES * (t + 1)]
        lower = shell_scr[8:16, LANES * t : LANES * (t + 1)]
        scr[2 * t] = jnp.where(left, upper, _roll(lower, PN))
        scr[2 * t + 1] = jnp.where(left, _roll(upper, PN), lower)
    for c in range(2 * plan.tiles, 8):
        scr[c] = jnp.zeros((8, LANES), F32)
    nodal = jnp.concatenate([scr[:, j, :] for j in range(8)], axis=0).astype(BF16)
    spread = _nn(nodal, hot[...])
    picked = sum(spread[8 * j : 8 * (j + 1)] * tile_hot[j : j + 1, :] for j in range(8))
    picked = picked * weights[...]
    twice = jnp.concatenate([couple, couple], axis=0)
    for h in range(plan.nx):
        part = picked[:, plan.slots * h : plan.slots * (h + 1)]
        dofs = _fold(_nt(_split(part), places[h]))
        push = _tn(twice, _split(dofs))
        for a in range(plan.nv):
            value = rhs[0, h, a].astype(F32) - push[NP * a : NP * (a + 1)]
            source[h, a] = 0.5 * value


def prepare_kernel(
    plan, deriv, load, inverse, penalty, forward, backward, solved, coef, strength
):
    coefficients(plan, penalty, coef, strength)
    mine = plan.rank() // (plan.groups // plan.held)
    p, c = _iota((NP, plan.depth), 0), _iota((NP, plan.depth), 1)
    j, l = (p // 4) % 4, p % 4

    def block(n, ok, shift):
        return ok & (c - (3 + n) * NP == p + shift)

    links = block(0, j == 3, -12) | block(1, j == 0, 12)
    links = links | block(2, l == 3, -3) | block(3, l == 0, 3)
    links = links | ((p >= 48) & (c - 7 * NP == p - 48))
    links = links | ((p < 16) & (c - 7 * NP - 16 == p))
    base = (0.5 * _flag(links)).astype(BF16)
    forward[...] = base
    backward[...] = base
    for k in range(3):
        part = -0.5 * deriv[k].astype(F32)
        forward[:, NP * k : NP * (k + 1)] = part.astype(BF16)
        backward[:, NP * k : NP * (k + 1)] = part.T.astype(BF16)
    solved[...] = _nt(member_rows(plan, load, mine).astype(BF16), inverse[mine])


def first_kernel(
    plan, received, backward, solved, coupling, coef, strength,
    adjoint, rhs, table, hot, tile_hot, places, weights, out,
    middle, source,
):
    nv, window, nx, ny = plan.nv, plan.window, plan.nx, plan.ny
    rank = plan.rank()
    masks = swap_masks(ny)
    for h in range(nx):
        for f in range(2):
            for a in range(nv):
                first = (f * nv + a) * 16
                parts = [received[h * ny + y, pl.ds(first, 16), :] for y in range(ny)]
                for k, part in enumerate(swap_groups(parts, masks)):
                    rhs[f, h, a, pl.ds(16 * k, 16), :] = part
        first = 2 * plan.field_rows
        count = plan.rows - first
        tails = [received[h * ny + y, pl.ds(first, count), :] for y in range(ny)]
        info = [x.astype(F32).reshape(plan.per, 8, LANES) for x in tails]
        pieces = [[] for _ in range(ny)]
        for r in range(0, count, 16):
            size = min(16, count - r)
            parts = [received[h * ny + y, pl.ds(first + r, size), :] for y in range(ny)]
            short = [(a[:size], b[:size]) for a, b in masks]
            for k, part in enumerate(swap_groups(parts, short)):
                pieces[k] += [part.astype(F32)[i : i + 8] for i in range(0, size, 8)]
        for k in range(ny):
            for i in range(plan.per):
                table[h, k * plan.per + i] = pieces[k][i]
        place = _iota((LANES, LANES), 0)
        row = _iota((8, LANES), 0)
        for y in range(ny):
            elem, tile, spot, coarse, fine = [info[y][i, 6:7, :] for i in range(5)]
            where = (elem - (plan.own * rank - plan.halo).astype(F32)).astype(jnp.int32)
            within = (where >= 0) & (where < window)
            target = jnp.where(within, where + y * window, -1)
            columns = pl.ds(LANES * y, LANES)
            places[h, :, columns] = _flag(place == target).astype(BF16)
            columns = pl.ds(plan.slots * h + LANES * y, LANES)
            weights[:, columns] = coarse + fine
            tile_hot[:, columns] = _flag(row == tile.astype(jnp.int32))
            hot[:, columns] = _flag(place == spot.astype(jnp.int32)).astype(BF16)

    for h in range(nx):
        for a in range(nv):
            source[h, a] = 0.5 * rhs[1, h, a].astype(F32)
    states = chain(source, [middle, adjoint], FSWEEP - 1)
    sweeps(plan, states, source, table, backward[...], True, coef, strength)
    values = [adjoint[h].reshape(nv * NP, LANES).astype(BF16) for h in range(nx)]
    low, high = node_loads(plan, couple_rows(coupling), values, hot, tile_hot, places, weights)
    write_exchange(plan, low, high, solved[...], out)


def second_kernel(
    plan, received, adjoint_in, rhs, table, hot, tile_hot, places, weights, forward, backward,
    coef, strength, coupling, load, shell_rhs, inverse,
    tangent, adjoint_last, out,
    first, second, source, scr, shell_scr,
):
    nv, nx = plan.nv, plan.nx
    rank = plan.rank()
    mine = rank // (plan.groups // plan.held)
    result = []
    steps = solve_steps(plan, received, load, shell_rhs, inverse, mine, result)
    couple = couple_rows(coupling)
    push_force(
        plan, received, plan.tiles, hot, tile_hot, places, weights, couple, rhs, shell_scr, scr,
        source,
    )
    states = chain(source, [first, tangent], FSWEEP - 1)
    sweeps(plan, states, source, table, forward[...], False, coef, strength, steps)
    for h in range(nx):
        for a in range(nv):
            extra = table[h, 3 * nv, a : a + 1, :] * tangent[h, a]
            source[h, a] = 0.5 * (rhs[1, h, a].astype(F32) + extra)
    states = chain(adjoint_in, [second, first], FSWEEP)
    sweeps(plan, states, source, table, backward[...], True, coef, strength)
    adjoint = states[-1]
    values = []
    for h in range(nx):
        value = adjoint[h].reshape(nv * NP, LANES).astype(BF16)
        adjoint_last[h] = value
        values.append(value)
    low, high = node_loads(plan, couple, values, hot, tile_hot, places, weights)
    write_exchange(plan, low, high, result[1], out)


def third_kernel(
    plan, received, tangent_in, adjoint_last, rhs, table, hot, tile_hot, places, weights, forward,
    coef, strength, coupling, load, shell_rhs, inverse,
    out,
    first, second, source, scr, shell_scr,
):
    nv, nx, ny, ns = plan.nv, plan.nx, plan.ny, plan.ns
    rank, share = plan.rank(), plan.groups // plan.held
    result = []
    steps = solve_steps(plan, received, load, shell_rhs, inverse, rank // share, result)
    push_force(
        plan, received, plan.tiles, hot, tile_hot, places, weights,
        couple_rows(coupling), rhs, shell_scr, scr, source,
    )
    states = chain(tangent_in, [first, second], FSWEEP)
    sweeps(plan, states, source, table, forward[...], False, coef, strength, steps)
    tangent = states[-1]
    shell = jnp.where(lax.rem(rank, share) == 0, result[0], result[1])
    tiles = [shell[:ns, LANES * t : LANES * (t + 1)] for t in range(plan.tiles)]
    shell = _split(jnp.concatenate(tiles, axis=0))
    for dest in range(plan.groups):
        out[dest, pl.ds(plan.field_rows, shell.shape[0]), :] = shell
    lane = _iota((16, LANES), 1)
    group = [_flag(lane // plan.own == n).astype(BF16) for n in range(plan.groups)]
    for h in range(nx):
        for a in range(nv):
            parts = [tangent[h, a, pl.ds(16 * i, 16), :].astype(BF16) for i in range(4)]
            parts += [adjoint_last[h, pl.ds(a * NP + 16 * i, 16), :] for i in range(4)]
            for y in range(ny):
                total = None
                for n in range(plan.groups):
                    shift = plan.own * n - plan.window * y - plan.halo
                    term = _roll(parts[n], shift) * group[n]
                    total = term if total is None else total + term
                out[h * ny + y, pl.ds(16 * a, 16), :] = total


def last_kernel(plan, received, tangent, adjoint, shell_tangent, shell_adjoint):
    share, ns = plan.groups // plan.held, plan.ns
    for panel in range(plan.held):
        for i, ref in enumerate((shell_adjoint, shell_tangent)):
            block = received[panel * share + i, pl.ds(plan.field_rows, plan.shell_rows), :]
            block = _fold(block.astype(F32))
            for t in range(plan.tiles):
                columns = pl.ds(LANES * t, LANES)
                ref[:, panel, columns] = block[ns * t : ns * (t + 1)]
    masks = swap_masks(plan.groups)
    for a in range(plan.nv):
        parts = [received[g, pl.ds(16 * a, 16), :] for g in range(plan.groups)]
        for n, part in enumerate(swap_groups(parts, masks)):
            (tangent, adjoint)[n // 4][a, pl.ds(16 * (n % 4), 16), :] = part


def call(kernel, plan, out_shape, scratch, copies, on_chip, in_hbm, scalars, limit=KERNEL_VMEM,
         out_space=pltpu.VMEM):
    vmem = pl.BlockSpec(memory_space=pltpu.VMEM)
    hbm = pl.BlockSpec(memory_space=pltpu.HBM)
    smem = pl.BlockSpec(memory_space=pltpu.SMEM)
    specs = [vmem] * len(on_chip) + [hbm] * len(in_hbm) + [smem] * len(scalars)
    scratch_shapes = [pltpu.VMEM(s, d) for s, d in scratch]
    if copies:
        scratch_shapes.append(pltpu.SemaphoreType.DMA((copies,)))
    return pl.pallas_call(
        functools.partial(kernel, plan),
        out_shape=[jax.ShapeDtypeStruct(s, d) for s, d in out_shape],
        in_specs=specs,
        out_specs=[pl.BlockSpec(memory_space=out_space)] * len(out_shape),
        scratch_shapes=scratch_shapes,
        compiler_params=pltpu.CompilerParams(vmem_limit_bytes=limit),
    )(*on_chip, *in_hbm, *scalars)


def slab_body(
    plan, tangent_rhs, adjoint_rhs, jacobians, deriv, penalty, second_order, coupling,
    shell_inverse, shell_load, shell_adjoint_rhs, iface_elem, iface_node, iface_weight,
    iface_count,
):
    nv, nx, ns, groups = plan.nv, plan.nx, plan.ns, plan.groups
    flow, everyone = ("fx", "fy"), ("fx", "fy", "st")
    state = ((nx, nv, NP, LANES), F32)
    coef = ((nv, NP, LANES), F32)
    scr = ((8, 8, LANES), F32)
    shell_rows = ((plan.panels, plan.width), F32)
    matrix = ((NP, plan.depth), BF16)

    def like(*arrays):
        return [(x.shape, x.dtype) for x in arrays]

    inputs = (
        tangent_rhs.reshape(nv, NP, LANES), adjoint_rhs.reshape(nv, NP, LANES),
        jacobians.reshape(3, nv, nv, LANES), second_order.reshape(nv, 1, LANES),
        iface_elem, iface_node, iface_weight, iface_count.reshape(1, 1),
    )
    (packed,) = call(
        pack_kernel, plan, [((groups, plan.rows, LANES), BF16)],
        like(*inputs)
        + [((4 * plan.per, 8, LANES), F32), ((groups, plan.rows, LANES), BF16)],
        len(inputs) + 3, (), inputs, (), None, pltpu.HBM,
    )
    slab = lax.all_to_all(packed, flow, split_axis=0, concat_axis=0, tiled=True)
    forward, backward, solved, coef, strength = call(
        prepare_kernel, plan,
        [matrix, matrix, ((8, plan.width), F32), coef, ((nv, 16, LANES), F32)],
        [], 0, (deriv, shell_load, shell_inverse), (), (penalty,),
    )
    adjoint, rhs, table, hot, tile_hot, places, weights, sent = call(
        first_kernel, plan,
        [
            state, ((2,) + state[0], BF16), ((nx, 4 * plan.per, 8, LANES), F32),
            ((LANES, nx * plan.slots), BF16), ((8, nx * plan.slots), F32),
            ((nx, LANES, plan.slots), BF16), ((1, nx * plan.slots), F32),
            ((groups * ns, 8, LANES), BF16),
        ],
        [state, state], 0, (slab, backward, solved, coupling, coef, strength), (), (),
    )
    received = lax.all_to_all(sent, everyone, split_axis=0, concat_axis=0, tiled=True)
    tangent, adjoint_last, sent = call(
        second_kernel, plan,
        [state, ((nx, nv * NP, LANES), BF16), ((groups * ns, 8, LANES), BF16)],
        [state, state, state, scr, shell_rows], 0,
        (
            received, adjoint, rhs, table, hot, tile_hot, places, weights, forward, backward,
            coef, strength, coupling, shell_load, shell_adjoint_rhs, shell_inverse,
        ),
        (), (),
    )
    received = lax.all_to_all(sent, everyone, split_axis=0, concat_axis=0, tiled=True)
    (sent,) = call(
        third_kernel, plan,
        [((groups, plan.field_rows + plan.shell_rows, LANES), BF16)],
        [state, state, state, scr, shell_rows], 0,
        (
            received, tangent, adjoint_last, rhs, table, hot, tile_hot, places, weights,
            forward, coef, strength, coupling, shell_load, shell_adjoint_rhs, shell_inverse,
        ),
        (), (),
    )
    received = lax.all_to_all(sent, flow, split_axis=0, concat_axis=0, tiled=True)
    shell_shape = (shell_load.shape, F32)
    tangent, adjoint, shell_tangent, shell_adjoint = call(
        last_kernel, plan, [((nv, NP, LANES), BF16)] * 2 + [shell_shape] * 2, [], 0,
        (received,), (), (),
    )
    return (
        tangent.reshape(tangent_rhs.shape), adjoint.reshape(adjoint_rhs.shape),
        shell_tangent, shell_adjoint,
    )


def body(*args):
    tangent_rhs, shell_inverse, shell_load, iface_elem = args[0], args[7], args[8], args[10]
    nx, ny, ns = (lax.axis_size(name) for name in ("fx", "fy", "st"))
    panels, width = shell_inverse.shape[0] * ns, shell_load.shape[2]
    if fits(nx, ny, ns, tangent_rhs.shape, iface_elem.shape[1], panels, width):
        plan = Plan(nx, ny, ns, tangent_rhs.shape[1], tangent_rhs.shape[5], panels, width)
        return slab_body(plan, *args)
    return halo_body(*args)


def solution(mesh):
    in_specs = (
        P("st", None, None, "fx", "fy", None),
        P("st", None, None, "fx", "fy", None),
        P(None, None, None, "fx", "fy", None),
        P(),
        P(),
        P(None, "fx", "fy", None),
        P(),
        P("st", None, None),
        P(None, "st", None),
        P(None, "st", None),
        P(("fx", "fy"), None),
        P(("fx", "fy"), None),
        P(("fx", "fy"), None),
        P(("fx", "fy")),
    )
    out_specs = (
        P("st", None, None, "fx", "fy", None),
        P("st", None, None, "fx", "fy", None),
        P(None, "st", None),
        P(None, "st", None),
    )
    return jax.shard_map(body, mesh=mesh, in_specs=in_specs, out_specs=out_specs, check_vma=False)
```

```python
import functools

import jax
import jax.numpy as jnp
from jax import lax
from jax.experimental import pallas as pl
from jax.experimental.pallas import tpu as pltpu
from jax.sharding import PartitionSpec as P

SDOF = 6
PN = 64
NP = 64
FSWEEP = 3
ROUNDS = 2
LANES = 128
KERNEL_VMEM = 32 * 1024 * 1024
F32 = jnp.float32
BF16 = jnp.bfloat16


SIGMA = 0.5


def with_halo(value, sides, width):
    for axis, dim in sides:
        peers, length = (lax.axis_size(axis), value.shape[dim])
        up = [(i, (i + 1) % peers) for i in range(peers - 1)]
        down = [(j, i) for i, j in up]
        last = lax.slice_in_dim(value, length - width, length, axis=dim)
        initial = lax.slice_in_dim(value, 0, width, axis=dim)
        before = lax.ppermute(last, axis, up)
        after = lax.ppermute(initial, axis, down)
        value = jnp.concatenate([before, value, after], axis=dim)
    return value


def face_pair(lower_face, upper_face, below, above, axis):
    length = lower_face.shape[axis]
    beyond_upper = jnp.concatenate(
        [lax.slice_in_dim(lower_face, 1, length, axis=axis), above], axis=axis
    )
    beyond_lower = jnp.concatenate(
        [below, lax.slice_in_dim(upper_face, 0, length - 1, axis=axis)], axis=axis
    )
    return (lower_face - beyond_lower, upper_face - beyond_upper)


def place_faces(jump_low, jump_high, axis):
    middle_shape = list(jump_low.shape)
    middle_shape.insert(axis, 2)
    middle = jnp.zeros(middle_shape, jump_low.dtype)
    return jnp.concatenate(
        [jnp.expand_dims(jump_low, axis), middle, jnp.expand_dims(jump_high, axis)], axis=axis
    )


def as_cube(values):
    members, variables, points, size_x, size_y, size_z = values.shape
    return values.reshape(members, variables, 4, 4, 4, size_x, size_y, size_z)


def face_edges(values):
    cube = as_cube(values)
    received = []
    for node_axis in (2, 3):
        elem_axis = node_axis + 2
        lower_face = jnp.take(cube, 0, axis=node_axis)
        upper_face = jnp.take(cube, 3, axis=node_axis)
        edges = jnp.concatenate([lower_face, upper_face], axis=elem_axis)
        if node_axis == 2:
            extended = with_halo(edges, (("fx", 4),), 1)
        else:
            extended = with_halo(edges, (("fy", 5),), 1)
        below = lax.slice_in_dim(extended, 0, 1, axis=elem_axis)
        above = lax.slice_in_dim(extended, 3, 4, axis=elem_axis)
        received.append((below, above))
    return received


def flow_jumps(values, received):
    cube = as_cube(values)
    result = jnp.zeros(cube.shape, jnp.float32)
    for node_axis in (2, 3, 4):
        elem_axis = node_axis + 2
        lower_face = jnp.take(cube, 0, axis=node_axis).astype(jnp.float32)
        upper_face = jnp.take(cube, 3, axis=node_axis).astype(jnp.float32)
        if received is None or node_axis == 4:
            below = jnp.zeros_like(lax.slice_in_dim(lower_face, 0, 1, axis=elem_axis))
            above = below
        else:
            below = received[node_axis - 2][0].astype(jnp.float32)
            above = received[node_axis - 2][1].astype(jnp.float32)
        jump_low, jump_high = face_pair(lower_face, upper_face, below, above, elem_axis)
        result = result + place_faces(jump_low, jump_high, node_axis)
    return result.reshape(values.shape)


def volume(values, deriv_mats, jac_mats):
    grads = jnp.einsum("kpq,vqxyz->kvpxyz", deriv_mats, values, preferred_element_type=jnp.float32)
    result = jnp.sum(jac_mats[0][:, :, None] * grads[0][None], axis=1)
    for axis_index in (1, 2):
        result = result + jnp.sum(
            jac_mats[axis_index][:, :, None] * grads[axis_index][None], axis=1
        )
    return result


def operator(states, operator_kinds, penalty):
    values = lax.optimization_barrier(states.astype(jnp.bfloat16))
    received = face_edges(values)
    jumps = flow_jumps(values, received)
    volumes = jnp.stack(
        [
            volume(values[member], operator_kinds[member][0], operator_kinds[member][1])
            for member in range(len(operator_kinds))
        ]
    )
    return states + volumes + penalty[None, :, None, None, None, None] * jumps


def halo_body(
    tangent_rhs,
    adjoint_rhs,
    jacobians,
    deriv,
    penalty,
    second_order,
    coupling,
    shell_inverse,
    shell_load,
    shell_adjoint_rhs,
    iface_elem,
    iface_node,
    iface_weight,
    iface_count,
):
    state_shape = tangent_rhs.shape
    variables = state_shape[1]
    points = state_shape[2]
    elements = state_shape[3] * state_shape[4] * state_shape[5]
    slots = iface_elem.shape[1]
    live = (jnp.arange(slots, dtype=jnp.int32) < iface_count[0]).astype(jnp.float32)
    weights = iface_weight[0] * live
    elem_index = iface_elem[0]
    node_index = iface_node[0]
    dof_rows = jnp.arange(SDOF, dtype=jnp.int32)[:, None]
    columns = (node_index // PN)[None, :] * (SDOF * PN) + dof_rows * PN + (node_index % PN)[None, :]
    forward_jac = jacobians.astype(jnp.float32)
    forward_kind = (deriv, forward_jac)
    backward_kind = (jnp.swapaxes(deriv, 1, 2), jnp.swapaxes(forward_jac, 1, 2))
    coupling_cols = coupling.T

    def shell_solve(rhs):
        return jnp.einsum(
            "pab,dpb->dpa",
            shell_inverse,
            rhs.astype(jnp.bfloat16),
            preferred_element_type=jnp.float32,
        )

    shell_tangent = shell_solve(shell_load)
    shell_adjoint = jnp.zeros(shell_load.shape, jnp.float32)
    tangent = jnp.zeros(state_shape, jnp.float32)
    adjoint = jnp.zeros(state_shape, jnp.float32)
    for round_index in range(ROUNDS):
        received = lax.all_to_all(
            shell_tangent.astype(jnp.bfloat16), "st", split_axis=0, concat_axis=1, tiled=True
        )
        picked = received.reshape(-1)[columns]
        pushed_cols = (
            jnp.dot(coupling_cols, picked, preferred_element_type=jnp.float32) * weights[None, :]
        )
        pushed = (
            jnp.zeros((variables * points, elements), jnp.float32)
            .at[:, elem_index]
            .add(pushed_cols)
        )
        force = tangent_rhs.astype(jnp.float32) - pushed.reshape(state_shape)
        adjoint_source = adjoint_rhs.astype(jnp.float32) + second_order[None, :, None] * tangent
        paired = jnp.concatenate([tangent, adjoint])
        sources = jnp.concatenate([force, adjoint_source])
        for sweep in range(FSWEEP):
            paired = paired + SIGMA * (
                sources - operator(paired, (forward_kind, backward_kind), penalty)
            )
        tangent = paired[:1]
        adjoint = paired[1:]
        adjoint_values = adjoint.astype(jnp.bfloat16).reshape(variables * points, elements)
        gathered = adjoint_values[:, elem_index]
        loads = jnp.dot(coupling, gathered, preferred_element_type=jnp.float32) * weights[None, :]
        panels = received.shape[1]
        partial_loads = jnp.zeros((panels * SDOF * PN,), jnp.float32).at[columns].add(loads)
        partial_loads = partial_loads.reshape(1, panels, SDOF * PN)
        summed = lax.psum(partial_loads, ("fx", "fy"))
        owned = lax.all_to_all(summed, "st", split_axis=1, concat_axis=0, tiled=True)
        shell_adjoint = shell_solve(shell_adjoint_rhs - owned)
        shell_tangent = shell_solve(shell_load + shell_adjoint)
    return (
        tangent.astype(jnp.bfloat16),
        adjoint.astype(jnp.bfloat16),
        shell_tangent,
        shell_adjoint,
    )


def _iota(shape, dim):
    return lax.broadcasted_iota(jnp.int32, shape, dim)


def _flag(cond):
    return jnp.where(cond, 1.0, 0.0)


def _nt(a, b):
    return lax.dot_general(a, b, (((1,), (1,)), ((), ())), preferred_element_type=F32)


def _nn(a, b):
    return lax.dot_general(a, b, (((1,), (0,)), ((), ())), preferred_element_type=F32)


def _tn(a, b):
    return lax.dot_general(a, b, (((0,), (0,)), ((), ())), preferred_element_type=F32)


def _split(x):
    high = x.astype(BF16)
    low = (x - high.astype(F32)).astype(BF16)
    return jnp.concatenate([high, low], axis=0)


def _fold(x):
    half = x.shape[0] // 2
    return x[:half] + x[half:]


def _roll(x, shift):
    shift = shift % LANES
    return x if shift == 0 else pltpu.roll(x, shift, 1)


def swap_masks(count):
    group = _iota((16, LANES), 1) // (LANES // count)
    masks, step = [], 1
    while step < count:
        has = (group // step) % 2
        masks.append((_flag(has == 0).astype(BF16), _flag(has == 1).astype(BF16)))
        step *= 2
    return masks


def swap_groups(parts, masks):
    width = LANES // len(parts)
    for bit, (without, having) in enumerate(masks):
        step = 1 << bit
        swapped = list(parts)
        for a in range(len(parts)):
            if not a & step:
                x, y = parts[a], parts[a | step]
                swapped[a] = x * without + _roll(y, width * step) * having
                swapped[a | step] = y * having + _roll(x, -width * step) * without
        parts = swapped
    return parts


class Plan:
    def __init__(self, nx, ny, ns, nv, span, panels, width):
        self.nx, self.ny, self.ns, self.nv = nx, ny, ns, nv
        self.span, self.panels, self.width = span, panels, width
        self.groups = nx * ny
        self.own = span // self.groups
        self.window = LANES // ny
        self.halo = (self.window - self.own) // 2
        self.held = panels // ns
        self.nodes = panels * PN
        self.tiles = width // LANES
        self.deps = 3 * nv * nv
        self.granules = 3 * nv + 1
        self.per = -(-self.granules // 4)
        self.field_rows = nv * 16
        self.rows = 2 * self.field_rows + self.per * 8
        self.depth = 7 * NP + 32
        self.slots = ny * LANES
        self.shell_rows = 2 * ns * self.tiles

    def rank(self):
        return lax.axis_index("fy") * self.nx + lax.axis_index("fx")


def fits(nx, ny, ns, local_shape, slots, panels, width):
    members, nv, points, size_x, size_y, span = local_shape
    groups = nx * ny
    if members != 1 or (size_x, size_y) != (1, 1) or points != NP or nv > 6 or nv % 2:
        return False
    if span != LANES or slots != LANES or span % groups or LANES % ny or LANES % groups:
        return False
    own, window = span // groups, LANES // ny
    if window * 4 != LANES or (window - own) % 2 or (window - own) // 2 < ROUNDS * FSWEEP - 1:
        return False
    if own * 8 != LANES or width != SDOF * PN or width % LANES or SDOF > 8:
        return False
    held = panels // ns
    if panels % ns or panels != 16 or 8 % held or groups % held or groups < 2 * held:
        return False
    return ns <= 4 and 2 * (width // LANES) <= 8


def solve_steps(plan, received, load, shell_rhs, inverse, mine, result):
    def first():
        rows = member_rows(plan, shell_rhs, mine) - read_own_loads(plan, received)
        result.append(_nt(rows.astype(BF16), inverse[mine]))

    def second():
        rows = member_rows(plan, load, mine) + result[0]
        result.append(_nt(rows.astype(BF16), inverse[mine]))

    return [first, second]


def member_rows(plan, ref, panel):
    rows = [ref[d, pl.ds(panel, 1), :] for d in range(plan.ns)]
    rows.append(jnp.zeros((8 - plan.ns, plan.width), F32))
    return jnp.concatenate(rows, axis=0)


def fetch(pairs, sems):
    copies = [
        pltpu.make_async_copy(source, target, sems.at[i])
        for i, (source, target) in enumerate(pairs)
    ]
    for copy in copies:
        copy.start()
    return copies


def pack_kernel(
    plan, trhs_hbm, arhs_hbm, jac_hbm, second_hbm, elem_hbm, node_hbm, weight_hbm, count_hbm,
    out_hbm, trhs, arhs, jac, second, elem, node, weight, count, scr, out, sems,
):
    nv, window = plan.nv, plan.window
    copies = fetch(
        (
            (trhs_hbm, trhs), (arhs_hbm, arhs), (jac_hbm, jac), (second_hbm, second),
            (elem_hbm, elem), (node_hbm, node), (weight_hbm, weight),
            (count_hbm, count),
        ),
        sems,
    )
    lane = _iota((1, LANES), 1)
    masks = []
    for dest in range(plan.groups):
        start = plan.own * dest - plan.halo
        row = []
        for k in range(4):
            z = start + lane % window
            row.append(_flag((lane // window == k) & (z >= 0) & (z < plan.span)))
        masks.append(row)

    def window_of(parts, dest, dtype):
        start = plan.own * dest - plan.halo
        total = None
        for k in range(4):
            term = _roll(parts[k], window * k - start) * masks[dest][k].astype(dtype)
            total = term if total is None else total + term
        return total

    sent = []

    def send(first, count):
        part = pl.ds(first, count)
        sem = sems.at[len(copies) + len(sent)]
        sent.append(pltpu.make_async_copy(out.at[:, part], out_hbm.at[:, part], sem))
        sent[-1].start()

    for f, ref in enumerate((trhs, arhs)):
        copies[f].wait()
        for a in range(nv):
            parts = [ref[a, pl.ds(16 * k, 16), :] for k in range(4)]
            for dest in range(plan.groups):
                out[dest, pl.ds((f * nv + a) * 16, 16), :] = window_of(parts, dest, BF16)
        send(f * plan.field_rows, plan.field_rows)

    for copy in copies[2:]:
        copy.wait()
    scr[...] = jnp.zeros(scr.shape, F32)
    for k in range(3):
        for a in range(nv):
            scr[k * nv + a, 0:nv, :] = jac[k, a].astype(F32)
    for a in range(nv):
        scr[3 * nv, a : a + 1, :] = second[a]
    quarter = [
        scr[pl.ds(plan.per * k, plan.per)].reshape(plan.per * 8, LANES) for k in range(4)
    ]
    live = _flag(lane < jnp.broadcast_to(count[...], (1, LANES)))
    scaled = weight[...] * live
    coarse = scaled.astype(BF16).astype(F32)
    panel = node[...] // PN
    upper = jnp.where(panel >= 8, 1, 0)
    table = [
        elem[...].astype(F32),
        (panel - 8 * upper).astype(F32),
        (node[...] - panel * PN + PN * upper).astype(F32),
        coarse,
        scaled - coarse,
    ]
    row = _iota((8, LANES), 0)
    zero = jnp.zeros((8, LANES), F32)
    table = [jnp.where(row == 6, line, 0.0) for line in table] + [zero] * (plan.per - len(table))
    table = jnp.concatenate(table, axis=0)
    for dest in range(plan.groups):
        block = window_of(quarter, dest, F32) + table
        first = 2 * plan.field_rows
        out[dest, pl.ds(first, plan.rows - first), :] = block.astype(BF16)
    send(2 * plan.field_rows, plan.rows - 2 * plan.field_rows)
    for copy in sent:
        copy.wait()


def coefficients(plan, penalty, coef, strength):
    point = _iota((NP, LANES), 0)
    ends = [point // 16, (point // 4) % 4, point % 4]
    faces = sum(_flag((e == 0) | (e == 3)) for e in ends)
    lane = _iota((16, LANES), 1)
    z = plan.own * plan.rank() - plan.halo + lane % plan.window
    inside = _flag((z >= 0) & (z < plan.span))
    for a in range(plan.nv):
        coef[a] = 0.5 - (0.5 * penalty[a]) * faces
        strength[a] = penalty[a] * inside


def sweeps(plan, states, source, table, matrix, transposed, coef, strength, steps=()):
    nv, nx, window = plan.nv, plan.nx, plan.window
    lane = _iota((16, LANES), 1)
    not_last = _flag(lane < LANES - window).astype(BF16)
    not_first = _flag(lane >= window).astype(BF16)
    none = jnp.zeros((16, LANES), BF16)
    rows = [strength[a].astype(BF16) for a in range(nv)]

    def plane(state, h, a, i):
        return state[h, a, pl.ds(16 * i, 16), :].astype(BF16)

    def flux(h, k, a, b):
        index, row = (k * nv + b, a) if transposed else (k * nv + a, b)
        line = table[h, index, pl.ds(row, 1), :]
        return jnp.broadcast_to(line, (16, LANES)).astype(BF16)

    for now, later in zip(states[:-1], states[1:]):
        for h in range(nx):
            if steps:
                steps.pop(0)()
            own = [[plane(now, h, b, i) for i in range(4)] for b in range(nv)]
            for a0 in range(0, nv, 2):
                stacks = []
                for a in (a0, a0 + 1):
                    parts = []
                    for k in range(3):
                        total = [None] * 4
                        for b in range(nv):
                            factor = flux(h, k, a, b)
                            for i in range(4):
                                term = own[b][i] * factor
                                total[i] = term if b == 0 else total[i] + term
                        parts += total
                    scaled = [own[a][i] * rows[a] for i in range(4)]
                    parts += [_roll(x, -window) * not_last for x in scaled]
                    parts += [_roll(x, window) * not_first for x in scaled]
                    parts += [_roll(x, -1) for x in scaled]
                    parts += [_roll(x, 1) for x in scaled]
                    parts.append(plane(now, h + 1, a, 0) * rows[a] if h + 1 < nx else none)
                    parts.append(plane(now, h - 1, a, 3) * rows[a] if h > 0 else none)
                    stacks.append(jnp.concatenate(parts, axis=0))
                product = _nn(matrix, jnp.concatenate(stacks, axis=1))
                for i, a in enumerate((a0, a0 + 1)):
                    value = coef[a] * now[h, a] + source[h, a]
                    later[h, a] = value + product[:, LANES * i : LANES * (i + 1)]


def chain(start, refs, count):
    return [start] + [refs[(i - count) % len(refs)] for i in range(count)]


def couple_rows(coupling):
    wide = coupling[...].astype(F32)
    pad = jnp.zeros((8 - SDOF, wide.shape[1]), F32)
    return jnp.concatenate([wide, pad], axis=0).astype(BF16)


def node_loads(plan, couple, values, hot, tile_hot, places, weights):
    lane = _iota((1, LANES), 1)
    place = lane % plan.window
    owned = _flag((place >= plan.halo) & (place < plan.halo + plan.own))
    picked = []
    for h in range(plan.nx):
        flow = _nn(couple, values[h]) * owned
        picked.append(_fold(_nn(_split(flow), places[h])))
    picked = jnp.concatenate(picked, axis=1) * weights[...]
    spread = [picked[c : c + 1] * tile_hot[...] for c in range(SDOF)]
    nodal = _fold(_nt(_split(jnp.concatenate(spread, axis=0)), hot[...]))
    left = _iota((8, LANES), 1) < PN
    low, high = [], []
    for t in range(plan.tiles):
        even, odd = nodal[16 * t : 16 * t + 8], nodal[16 * t + 8 : 16 * t + 16]
        low.append(jnp.where(left, even, _roll(odd, PN)))
        high.append(jnp.where(left, _roll(even, PN), odd))
    return low, high


def write_exchange(plan, low, high, solved, out):
    share, tiles = plan.groups // plan.held, plan.tiles
    row = _iota((8, LANES), 0)
    for dest in range(plan.ns):
        tail = jnp.zeros((8, LANES), F32)
        for t in range(tiles):
            part = pltpu.roll(solved[:, LANES * t : LANES * (t + 1)], (tiles + t - dest) % 8, 0)
            tail = jnp.where(row == tiles + t, part, tail)
        for panel in range(plan.held):
            q = dest * plan.held + panel
            block = tail
            for t in range(tiles):
                part = pltpu.roll(low[t] if q < 8 else high[t], (t - q) % 8, 0)
                block = jnp.where(row == t, part, block)
            block = block.astype(BF16)
            for g in range(panel * share, (panel + 1) * share):
                out[g * plan.ns + dest] = block


def summed(plan, received):
    totals = []
    for d in range(plan.ns):
        total = received[d].astype(F32)
        for g in range(1, plan.groups):
            total = total + received[g * plan.ns + d].astype(F32)
        totals.append(total)
    return totals


def read_own_loads(plan, received):
    totals = summed(plan, received)
    tiles = []
    for t in range(plan.tiles):
        rows = [x[t : t + 1] for x in totals] + [jnp.zeros((8 - plan.ns, LANES), F32)]
        tiles.append(jnp.concatenate(rows, axis=0))
    return jnp.concatenate(tiles, axis=1)


def push_force(
    plan, received, first, hot, tile_hot, places, weights, couple, rhs, shell_scr, scr, source
):
    span = plan.groups // plan.held
    for s in range(plan.ns):
        for panel in range(plan.held):
            block = received[panel * span * plan.ns + s].astype(F32)
            q = s * plan.held + panel
            for t in range(plan.tiles):
                line = block[first + t : first + t + 1]
                shell_scr[q : q + 1, LANES * t : LANES * (t + 1)] = line
    left = _iota((8, LANES), 1) < PN
    for t in range(plan.tiles):
        upper = shell_scr[0:8, LANES * t : LANES * (t + 1)]
        lower = shell_scr[8:16, LANES * t : LANES * (t + 1)]
        scr[2 * t] = jnp.where(left, upper, _roll(lower, PN))
        scr[2 * t + 1] = jnp.where(left, _roll(upper, PN), lower)
    for c in range(2 * plan.tiles, 8):
        scr[c] = jnp.zeros((8, LANES), F32)
    nodal = jnp.concatenate([scr[:, j, :] for j in range(8)], axis=0).astype(BF16)
    spread = _nn(nodal, hot[...])
    picked = sum(spread[8 * j : 8 * (j + 1)] * tile_hot[j : j + 1, :] for j in range(8))
    picked = picked * weights[...]
    twice = jnp.concatenate([couple, couple], axis=0)
    for h in range(plan.nx):
        part = picked[:, plan.slots * h : plan.slots * (h + 1)]
        dofs = _fold(_nt(_split(part), places[h]))
        push = _tn(twice, _split(dofs))
        for a in range(plan.nv):
            value = rhs[0, h, a].astype(F32) - push[NP * a : NP * (a + 1)]
            source[h, a] = 0.5 * value


def prepare_kernel(
    plan, deriv, load, inverse, penalty, forward, backward, solved, coef, strength
):
    coefficients(plan, penalty, coef, strength)
    mine = plan.rank() // (plan.groups // plan.held)
    p, c = _iota((NP, plan.depth), 0), _iota((NP, plan.depth), 1)
    j, l = (p // 4) % 4, p % 4

    def block(n, ok, shift):
        return ok & (c - (3 + n) * NP == p + shift)

    links = block(0, j == 3, -12) | block(1, j == 0, 12)
    links = links | block(2, l == 3, -3) | block(3, l == 0, 3)
    links = links | ((p >= 48) & (c - 7 * NP == p - 48))
    links = links | ((p < 16) & (c - 7 * NP - 16 == p))
    base = (0.5 * _flag(links)).astype(BF16)
    forward[...] = base
    backward[...] = base
    for k in range(3):
        part = -0.5 * deriv[k].astype(F32)
        forward[:, NP * k : NP * (k + 1)] = part.astype(BF16)
        backward[:, NP * k : NP * (k + 1)] = part.T.astype(BF16)
    solved[...] = _nt(member_rows(plan, load, mine).astype(BF16), inverse[mine])


def first_kernel(
    plan, received, backward, solved, coupling, coef, strength,
    adjoint, rhs, table, hot, tile_hot, places, weights, out,
    middle, source,
):
    nv, window, nx, ny = plan.nv, plan.window, plan.nx, plan.ny
    rank = plan.rank()
    masks = swap_masks(ny)
    for h in range(nx):
        for f in range(2):
            for a in range(nv):
                first = (f * nv + a) * 16
                parts = [received[y * nx + h, pl.ds(first, 16), :] for y in range(ny)]
                for k, part in enumerate(swap_groups(parts, masks)):
                    rhs[f, h, a, pl.ds(16 * k, 16), :] = part
        first = 2 * plan.field_rows
        count = plan.rows - first
        tails = [received[y * nx + h, pl.ds(first, count), :] for y in range(ny)]
        info = [x.astype(F32).reshape(plan.per, 8, LANES) for x in tails]
        pieces = [[] for _ in range(ny)]
        for r in range(0, count, 16):
            size = min(16, count - r)
            parts = [received[y * nx + h, pl.ds(first + r, size), :] for y in range(ny)]
            short = [(a[:size], b[:size]) for a, b in masks]
            for k, part in enumerate(swap_groups(parts, short)):
                pieces[k] += [part.astype(F32)[i : i + 8] for i in range(0, size, 8)]
        for k in range(ny):
            for i in range(plan.per):
                table[h, k * plan.per + i] = pieces[k][i]
        place = _iota((LANES, LANES), 0)
        row = _iota((8, LANES), 0)
        for y in range(ny):
            elem, tile, spot, coarse, fine = [info[y][i, 6:7, :] for i in range(5)]
            where = (elem - (plan.own * rank - plan.halo).astype(F32)).astype(jnp.int32)
            within = (where >= 0) & (where < window)
            target = jnp.where(within, where + y * window, -1)
            columns = pl.ds(LANES * y, LANES)
            places[h, :, columns] = _flag(place == target).astype(BF16)
            columns = pl.ds(plan.slots * h + LANES * y, LANES)
            weights[:, columns] = coarse + fine
            tile_hot[:, columns] = _flag(row == tile.astype(jnp.int32))
            hot[:, columns] = _flag(place == spot.astype(jnp.int32)).astype(BF16)

    for h in range(nx):
        for a in range(nv):
            source[h, a] = 0.5 * rhs[1, h, a].astype(F32)
    states = chain(source, [middle, adjoint], FSWEEP - 1)
    sweeps(plan, states, source, table, backward[...], True, coef, strength)
    values = [adjoint[h].reshape(nv * NP, LANES).astype(BF16) for h in range(nx)]
    low, high = node_loads(plan, couple_rows(coupling), values, hot, tile_hot, places, weights)
    write_exchange(plan, low, high, solved[...], out)


def second_kernel(
    plan, received, adjoint_in, rhs, table, hot, tile_hot, places, weights, forward, backward,
    coef, strength, coupling, load, shell_rhs, inverse,
    tangent, adjoint_last, out,
    first, second, source, scr, shell_scr,
):
    nv, nx = plan.nv, plan.nx
    rank = plan.rank()
    mine = rank // (plan.groups // plan.held)
    result = []
    steps = solve_steps(plan, received, load, shell_rhs, inverse, mine, result)
    couple = couple_rows(coupling)
    push_force(
        plan, received, plan.tiles, hot, tile_hot, places, weights, couple, rhs, shell_scr, scr,
        source,
    )
    states = chain(source, [first, tangent], FSWEEP - 1)
    sweeps(plan, states, source, table, forward[...], False, coef, strength, steps)
    for h in range(nx):
        for a in range(nv):
            extra = table[h, 3 * nv, a : a + 1, :] * tangent[h, a]
            source[h, a] = 0.5 * (rhs[1, h, a].astype(F32) + extra)
    states = chain(adjoint_in, [second, first], FSWEEP)
    sweeps(plan, states, source, table, backward[...], True, coef, strength)
    adjoint = states[-1]
    values = []
    for h in range(nx):
        value = adjoint[h].reshape(nv * NP, LANES).astype(BF16)
        adjoint_last[h] = value
        values.append(value)
    low, high = node_loads(plan, couple, values, hot, tile_hot, places, weights)
    write_exchange(plan, low, high, result[1], out)


def third_kernel(
    plan, received, tangent_in, adjoint_last, rhs, table, hot, tile_hot, places, weights, forward,
    coef, strength, coupling, load, shell_rhs, inverse,
    out,
    first, second, source, scr, shell_scr,
):
    nv, nx, ny, ns = plan.nv, plan.nx, plan.ny, plan.ns
    rank, share = plan.rank(), plan.groups // plan.held
    result = []
    steps = solve_steps(plan, received, load, shell_rhs, inverse, rank // share, result)
    push_force(
        plan, received, plan.tiles, hot, tile_hot, places, weights,
        couple_rows(coupling), rhs, shell_scr, scr, source,
    )
    states = chain(tangent_in, [first, second], FSWEEP)
    sweeps(plan, states, source, table, forward[...], False, coef, strength, steps)
    tangent = states[-1]
    shell = jnp.where(lax.rem(rank, share) == 0, result[0], result[1])
    tiles = [shell[:ns, LANES * t : LANES * (t + 1)] for t in range(plan.tiles)]
    shell = _split(jnp.concatenate(tiles, axis=0))
    for dest in range(plan.groups):
        out[dest, pl.ds(plan.field_rows, shell.shape[0]), :] = shell
    lane = _iota((16, LANES), 1)
    group = [_flag(lane // plan.own == n).astype(BF16) for n in range(plan.groups)]
    for h in range(nx):
        for a in range(nv):
            parts = [tangent[h, a, pl.ds(16 * i, 16), :].astype(BF16) for i in range(4)]
            parts += [adjoint_last[h, pl.ds(a * NP + 16 * i, 16), :] for i in range(4)]
            for y in range(ny):
                total = None
                for n in range(plan.groups):
                    shift = plan.own * n - plan.window * y - plan.halo
                    term = _roll(parts[n], shift) * group[n]
                    total = term if total is None else total + term
                out[y * nx + h, pl.ds(16 * a, 16), :] = total


def last_kernel(plan, received, tangent, adjoint, shell_tangent, shell_adjoint):
    share, ns = plan.groups // plan.held, plan.ns
    for panel in range(plan.held):
        for i, ref in enumerate((shell_adjoint, shell_tangent)):
            block = received[panel * share + i, pl.ds(plan.field_rows, plan.shell_rows), :]
            block = _fold(block.astype(F32))
            for t in range(plan.tiles):
                columns = pl.ds(LANES * t, LANES)
                ref[:, panel, columns] = block[ns * t : ns * (t + 1)]
    masks = swap_masks(plan.groups)
    for a in range(plan.nv):
        parts = [received[g, pl.ds(16 * a, 16), :] for g in range(plan.groups)]
        for n, part in enumerate(swap_groups(parts, masks)):
            (tangent, adjoint)[n // 4][a, pl.ds(16 * (n % 4), 16), :] = part


def call(kernel, plan, out_shape, scratch, copies, on_chip, in_hbm, scalars, limit=KERNEL_VMEM,
         out_space=pltpu.VMEM):
    vmem = pl.BlockSpec(memory_space=pltpu.VMEM)
    hbm = pl.BlockSpec(memory_space=pltpu.HBM)
    smem = pl.BlockSpec(memory_space=pltpu.SMEM)
    specs = [vmem] * len(on_chip) + [hbm] * len(in_hbm) + [smem] * len(scalars)
    scratch_shapes = [pltpu.VMEM(s, d) for s, d in scratch]
    if copies:
        scratch_shapes.append(pltpu.SemaphoreType.DMA((copies,)))
    return pl.pallas_call(
        functools.partial(kernel, plan),
        out_shape=[jax.ShapeDtypeStruct(s, d) for s, d in out_shape],
        in_specs=specs,
        out_specs=[pl.BlockSpec(memory_space=out_space)] * len(out_shape),
        scratch_shapes=scratch_shapes,
        compiler_params=pltpu.CompilerParams(vmem_limit_bytes=limit),
    )(*on_chip, *in_hbm, *scalars)


def slab_body(
    plan, tangent_rhs, adjoint_rhs, jacobians, deriv, penalty, second_order, coupling,
    shell_inverse, shell_load, shell_adjoint_rhs, iface_elem, iface_node, iface_weight,
    iface_count,
):
    nv, nx, ns, groups = plan.nv, plan.nx, plan.ns, plan.groups
    flow, everyone = ("fy", "fx"), ("fy", "fx", "st")
    state = ((nx, nv, NP, LANES), F32)
    coef = ((nv, NP, LANES), F32)
    scr = ((8, 8, LANES), F32)
    shell_rows = ((plan.panels, plan.width), F32)
    matrix = ((NP, plan.depth), BF16)

    def like(*arrays):
        return [(x.shape, x.dtype) for x in arrays]

    inputs = (
        tangent_rhs.reshape(nv, NP, LANES), adjoint_rhs.reshape(nv, NP, LANES),
        jacobians.reshape(3, nv, nv, LANES), second_order.reshape(nv, 1, LANES),
        iface_elem, iface_node, iface_weight, iface_count.reshape(1, 1),
    )
    (packed,) = call(
        pack_kernel, plan, [((groups, plan.rows, LANES), BF16)],
        like(*inputs)
        + [((4 * plan.per, 8, LANES), F32), ((groups, plan.rows, LANES), BF16)],
        len(inputs) + 3, (), inputs, (), None, pltpu.HBM,
    )
    slab = lax.all_to_all(packed, flow, split_axis=0, concat_axis=0, tiled=True)
    forward, backward, solved, coef, strength = call(
        prepare_kernel, plan,
        [matrix, matrix, ((8, plan.width), F32), coef, ((nv, 16, LANES), F32)],
        [], 0, (deriv, shell_load, shell_inverse), (), (penalty,),
    )
    adjoint, rhs, table, hot, tile_hot, places, weights, sent = call(
        first_kernel, plan,
        [
            state, ((2,) + state[0], BF16), ((nx, 4 * plan.per, 8, LANES), F32),
            ((LANES, nx * plan.slots), BF16), ((8, nx * plan.slots), F32),
            ((nx, LANES, plan.slots), BF16), ((1, nx * plan.slots), F32),
            ((groups * ns, 8, LANES), BF16),
        ],
        [state, state], 0, (slab, backward, solved, coupling, coef, strength), (), (),
    )
    received = lax.all_to_all(sent, everyone, split_axis=0, concat_axis=0, tiled=True)
    tangent, adjoint_last, sent = call(
        second_kernel, plan,
        [state, ((nx, nv * NP, LANES), BF16), ((groups * ns, 8, LANES), BF16)],
        [state, state, state, scr, shell_rows], 0,
        (
            received, adjoint, rhs, table, hot, tile_hot, places, weights, forward, backward,
            coef, strength, coupling, shell_load, shell_adjoint_rhs, shell_inverse,
        ),
        (), (),
    )
    received = lax.all_to_all(sent, everyone, split_axis=0, concat_axis=0, tiled=True)
    (sent,) = call(
        third_kernel, plan,
        [((groups, plan.field_rows + plan.shell_rows, LANES), BF16)],
        [state, state, state, scr, shell_rows], 0,
        (
            received, tangent, adjoint_last, rhs, table, hot, tile_hot, places, weights,
            forward, coef, strength, coupling, shell_load, shell_adjoint_rhs, shell_inverse,
        ),
        (), (),
    )
    received = lax.all_to_all(sent, flow, split_axis=0, concat_axis=0, tiled=True)
    shell_shape = (shell_load.shape, F32)
    tangent, adjoint, shell_tangent, shell_adjoint = call(
        last_kernel, plan, [((nv, NP, LANES), BF16)] * 2 + [shell_shape] * 2, [], 0,
        (received,), (), (),
    )
    return (
        tangent.reshape(tangent_rhs.shape), adjoint.reshape(adjoint_rhs.shape),
        shell_tangent, shell_adjoint,
    )


def body(*args):
    tangent_rhs, shell_inverse, shell_load, iface_elem = args[0], args[7], args[8], args[10]
    nx, ny, ns = (lax.axis_size(name) for name in ("fx", "fy", "st"))
    panels, width = shell_inverse.shape[0] * ns, shell_load.shape[2]
    if fits(nx, ny, ns, tangent_rhs.shape, iface_elem.shape[1], panels, width):
        plan = Plan(nx, ny, ns, tangent_rhs.shape[1], tangent_rhs.shape[5], panels, width)
        return slab_body(plan, *args)
    return halo_body(*args)


def solution(mesh):
    in_specs = (
        P("st", None, None, "fx", "fy", None),
        P("st", None, None, "fx", "fy", None),
        P(None, None, None, "fx", "fy", None),
        P(),
        P(),
        P(None, "fx", "fy", None),
        P(),
        P("st", None, None),
        P(None, "st", None),
        P(None, "st", None),
        P(("fx", "fy"), None),
        P(("fx", "fy"), None),
        P(("fx", "fy"), None),
        P(("fx", "fy")),
    )
    out_specs = (
        P("st", None, None, "fx", "fy", None),
        P("st", None, None, "fx", "fy", None),
        P(None, "st", None),
        P(None, "st", None),
    )
    return jax.shard_map(body, mesh=mesh, in_specs=in_specs, out_specs=out_specs, check_vma=False)
```

```python
import functools

import jax
import jax.numpy as jnp
from jax import lax
from jax.experimental import pallas as pl
from jax.experimental.pallas import tpu as pltpu
from jax.sharding import PartitionSpec as P

SDOF = 6
PN = 64
NP = 64
FSWEEP = 3
ROUNDS = 2
LANES = 128
KERNEL_VMEM = 32 * 1024 * 1024
F32 = jnp.float32
BF16 = jnp.bfloat16


SIGMA = 0.5


def with_halo(value, sides, width):
    for axis, dim in sides:
        peers, length = (lax.axis_size(axis), value.shape[dim])
        up = [(i, (i + 1) % peers) for i in range(peers - 1)]
        down = [(j, i) for i, j in up]
        last = lax.slice_in_dim(value, length - width, length, axis=dim)
        initial = lax.slice_in_dim(value, 0, width, axis=dim)
        before = lax.ppermute(last, axis, up)
        after = lax.ppermute(initial, axis, down)
        value = jnp.concatenate([before, value, after], axis=dim)
    return value


def face_pair(lower_face, upper_face, below, above, axis):
    length = lower_face.shape[axis]
    beyond_upper = jnp.concatenate(
        [lax.slice_in_dim(lower_face, 1, length, axis=axis), above], axis=axis
    )
    beyond_lower = jnp.concatenate(
        [below, lax.slice_in_dim(upper_face, 0, length - 1, axis=axis)], axis=axis
    )
    return (lower_face - beyond_lower, upper_face - beyond_upper)


def place_faces(jump_low, jump_high, axis):
    middle_shape = list(jump_low.shape)
    middle_shape.insert(axis, 2)
    middle = jnp.zeros(middle_shape, jump_low.dtype)
    return jnp.concatenate(
        [jnp.expand_dims(jump_low, axis), middle, jnp.expand_dims(jump_high, axis)], axis=axis
    )


def as_cube(values):
    members, variables, points, size_x, size_y, size_z = values.shape
    return values.reshape(members, variables, 4, 4, 4, size_x, size_y, size_z)


def face_edges(values):
    cube = as_cube(values)
    received = []
    for node_axis in (2, 3):
        elem_axis = node_axis + 2
        lower_face = jnp.take(cube, 0, axis=node_axis)
        upper_face = jnp.take(cube, 3, axis=node_axis)
        edges = jnp.concatenate([lower_face, upper_face], axis=elem_axis)
        if node_axis == 2:
            extended = with_halo(edges, (("fx", 4),), 1)
        else:
            extended = with_halo(edges, (("fy", 5),), 1)
        below = lax.slice_in_dim(extended, 0, 1, axis=elem_axis)
        above = lax.slice_in_dim(extended, 3, 4, axis=elem_axis)
        received.append((below, above))
    return received


def flow_jumps(values, received):
    cube = as_cube(values)
    result = jnp.zeros(cube.shape, jnp.float32)
    for node_axis in (2, 3, 4):
        elem_axis = node_axis + 2
        lower_face = jnp.take(cube, 0, axis=node_axis).astype(jnp.float32)
        upper_face = jnp.take(cube, 3, axis=node_axis).astype(jnp.float32)
        if received is None or node_axis == 4:
            below = jnp.zeros_like(lax.slice_in_dim(lower_face, 0, 1, axis=elem_axis))
            above = below
        else:
            below = received[node_axis - 2][0].astype(jnp.float32)
            above = received[node_axis - 2][1].astype(jnp.float32)
        jump_low, jump_high = face_pair(lower_face, upper_face, below, above, elem_axis)
        result = result + place_faces(jump_low, jump_high, node_axis)
    return result.reshape(values.shape)


def volume(values, deriv_mats, jac_mats):
    grads = jnp.einsum("kpq,vqxyz->kvpxyz", deriv_mats, values, preferred_element_type=jnp.float32)
    result = jnp.sum(jac_mats[0][:, :, None] * grads[0][None], axis=1)
    for axis_index in (1, 2):
        result = result + jnp.sum(
            jac_mats[axis_index][:, :, None] * grads[axis_index][None], axis=1
        )
    return result


def operator(states, operator_kinds, penalty):
    values = lax.optimization_barrier(states.astype(jnp.bfloat16))
    received = face_edges(values)
    jumps = flow_jumps(values, received)
    volumes = jnp.stack(
        [
            volume(values[member], operator_kinds[member][0], operator_kinds[member][1])
            for member in range(len(operator_kinds))
        ]
    )
    return states + volumes + penalty[None, :, None, None, None, None] * jumps


def halo_body(
    tangent_rhs,
    adjoint_rhs,
    jacobians,
    deriv,
    penalty,
    second_order,
    coupling,
    shell_inverse,
    shell_load,
    shell_adjoint_rhs,
    iface_elem,
    iface_node,
    iface_weight,
    iface_count,
):
    state_shape = tangent_rhs.shape
    variables = state_shape[1]
    points = state_shape[2]
    elements = state_shape[3] * state_shape[4] * state_shape[5]
    slots = iface_elem.shape[1]
    live = (jnp.arange(slots, dtype=jnp.int32) < iface_count[0]).astype(jnp.float32)
    weights = iface_weight[0] * live
    elem_index = iface_elem[0]
    node_index = iface_node[0]
    dof_rows = jnp.arange(SDOF, dtype=jnp.int32)[:, None]
    columns = (node_index // PN)[None, :] * (SDOF * PN) + dof_rows * PN + (node_index % PN)[None, :]
    forward_jac = jacobians.astype(jnp.float32)
    forward_kind = (deriv, forward_jac)
    backward_kind = (jnp.swapaxes(deriv, 1, 2), jnp.swapaxes(forward_jac, 1, 2))
    coupling_cols = coupling.T

    def shell_solve(rhs):
        return jnp.einsum(
            "pab,dpb->dpa",
            shell_inverse,
            rhs.astype(jnp.bfloat16),
            preferred_element_type=jnp.float32,
        )

    shell_tangent = shell_solve(shell_load)
    shell_adjoint = jnp.zeros(shell_load.shape, jnp.float32)
    tangent = jnp.zeros(state_shape, jnp.float32)
    adjoint = jnp.zeros(state_shape, jnp.float32)
    for round_index in range(ROUNDS):
        received = lax.all_to_all(
            shell_tangent.astype(jnp.bfloat16), "st", split_axis=0, concat_axis=1, tiled=True
        )
        picked = received.reshape(-1)[columns]
        pushed_cols = (
            jnp.dot(coupling_cols, picked, preferred_element_type=jnp.float32) * weights[None, :]
        )
        pushed = (
            jnp.zeros((variables * points, elements), jnp.float32)
            .at[:, elem_index]
            .add(pushed_cols)
        )
        force = tangent_rhs.astype(jnp.float32) - pushed.reshape(state_shape)
        adjoint_source = adjoint_rhs.astype(jnp.float32) + second_order[None, :, None] * tangent
        paired = jnp.concatenate([tangent, adjoint])
        sources = jnp.concatenate([force, adjoint_source])
        for sweep in range(FSWEEP):
            paired = paired + SIGMA * (
                sources - operator(paired, (forward_kind, backward_kind), penalty)
            )
        tangent = paired[:1]
        adjoint = paired[1:]
        adjoint_values = adjoint.astype(jnp.bfloat16).reshape(variables * points, elements)
        gathered = adjoint_values[:, elem_index]
        loads = jnp.dot(coupling, gathered, preferred_element_type=jnp.float32) * weights[None, :]
        panels = received.shape[1]
        partial_loads = jnp.zeros((panels * SDOF * PN,), jnp.float32).at[columns].add(loads)
        partial_loads = partial_loads.reshape(1, panels, SDOF * PN)
        summed = lax.psum(partial_loads, ("fx", "fy"))
        owned = lax.all_to_all(summed, "st", split_axis=1, concat_axis=0, tiled=True)
        shell_adjoint = shell_solve(shell_adjoint_rhs - owned)
        shell_tangent = shell_solve(shell_load + shell_adjoint)
    return (
        tangent.astype(jnp.bfloat16),
        adjoint.astype(jnp.bfloat16),
        shell_tangent,
        shell_adjoint,
    )


def _iota(shape, dim):
    return lax.broadcasted_iota(jnp.int32, shape, dim)


def _flag(cond):
    return jnp.where(cond, 1.0, 0.0)


def _nt(a, b):
    return lax.dot_general(a, b, (((1,), (1,)), ((), ())), preferred_element_type=F32)


def _nn(a, b):
    return lax.dot_general(a, b, (((1,), (0,)), ((), ())), preferred_element_type=F32)


def _tn(a, b):
    return lax.dot_general(a, b, (((0,), (0,)), ((), ())), preferred_element_type=F32)


def _split(x):
    high = x.astype(BF16)
    low = (x - high.astype(F32)).astype(BF16)
    return jnp.concatenate([high, low], axis=0)


def _fold(x):
    half = x.shape[0] // 2
    return x[:half] + x[half:]


def _roll(x, shift):
    shift = shift % LANES
    return x if shift == 0 else pltpu.roll(x, shift, 1)


def swap_masks(count):
    group = _iota((16, LANES), 1) // (LANES // count)
    masks, step = [], 1
    while step < count:
        has = (group // step) % 2
        masks.append((_flag(has == 0).astype(BF16), _flag(has == 1).astype(BF16)))
        step *= 2
    return masks


def swap_groups(parts, masks):
    width = LANES // len(parts)
    for bit, (without, having) in enumerate(masks):
        step = 1 << bit
        swapped = list(parts)
        for a in range(len(parts)):
            if not a & step:
                x, y = parts[a], parts[a | step]
                swapped[a] = x * without + _roll(y, width * step) * having
                swapped[a | step] = y * having + _roll(x, -width * step) * without
        parts = swapped
    return parts


class Plan:
    def __init__(self, nx, ny, ns, nv, span, panels, width):
        self.nx, self.ny, self.ns, self.nv = nx, ny, ns, nv
        self.span, self.panels, self.width = span, panels, width
        self.groups = nx * ny
        self.own = span // self.groups
        self.window = LANES // ny
        self.halo = (self.window - self.own) // 2
        self.held = panels // ns
        self.nodes = panels * PN
        self.tiles = width // LANES
        self.deps = 3 * nv * nv
        self.granules = 3 * nv + 1
        self.per = -(-self.granules // 4)
        self.field_rows = nv * 16
        self.rows = 2 * self.field_rows + self.per * 8
        self.depth = 7 * NP + 32
        self.slots = ny * LANES
        self.shell_rows = -(-ns * self.tiles // 8) * 8

    def rank(self):
        return lax.axis_index("fy") * self.nx + lax.axis_index("fx")


def fits(nx, ny, ns, local_shape, slots, panels, width):
    members, nv, points, size_x, size_y, span = local_shape
    groups = nx * ny
    if members != 1 or (size_x, size_y) != (1, 1) or points != NP or nv > 6 or nv % 2:
        return False
    if span != LANES or slots != LANES or span % groups or LANES % ny or LANES % groups:
        return False
    own, window = span // groups, LANES // ny
    if window * 4 != LANES or (window - own) % 2 or (window - own) // 2 < ROUNDS * FSWEEP - 1:
        return False
    if own * 8 != LANES or width != SDOF * PN or width % LANES or SDOF > 8:
        return False
    held = panels // ns
    if panels % ns or panels != 16 or 8 % held or groups % held or groups < 2 * held:
        return False
    return ns <= 4 and 2 * (width // LANES) <= 8


def solve_steps(plan, received, load, shell_rhs, inverse, mine, result):
    def first():
        rows = member_rows(plan, shell_rhs, mine) - read_own_loads(plan, received)
        result.append(_nt(rows.astype(BF16), inverse[mine]))

    def second():
        rows = member_rows(plan, load, mine) + result[0]
        result.append(_nt(rows.astype(BF16), inverse[mine]))

    return [first, second]


def member_rows(plan, ref, panel):
    rows = [ref[d, pl.ds(panel, 1), :] for d in range(plan.ns)]
    rows.append(jnp.zeros((8 - plan.ns, plan.width), F32))
    return jnp.concatenate(rows, axis=0)


def fetch(pairs, sems):
    copies = [
        pltpu.make_async_copy(source, target, sems.at[i])
        for i, (source, target) in enumerate(pairs)
    ]
    for copy in copies:
        copy.start()
    return copies


def pack_kernel(
    plan, trhs_hbm, arhs_hbm, jac_hbm, second_hbm, elem_hbm, node_hbm, weight_hbm, count_hbm,
    out_hbm, trhs, arhs, jac, second, elem, node, weight, count, scr, out, sems,
):
    nv, window = plan.nv, plan.window
    copies = fetch(
        (
            (trhs_hbm, trhs), (arhs_hbm, arhs), (jac_hbm, jac), (second_hbm, second),
            (elem_hbm, elem), (node_hbm, node), (weight_hbm, weight),
            (count_hbm, count),
        ),
        sems,
    )
    lane = _iota((1, LANES), 1)
    masks = []
    for dest in range(plan.groups):
        start = plan.own * dest - plan.halo
        row = []
        for k in range(4):
            z = start + lane % window
            row.append(_flag((lane // window == k) & (z >= 0) & (z < plan.span)))
        masks.append(row)

    def window_of(parts, dest, dtype):
        start = plan.own * dest - plan.halo
        total = None
        for k in range(4):
            term = _roll(parts[k], window * k - start) * masks[dest][k].astype(dtype)
            total = term if total is None else total + term
        return total

    sent = []

    def send(first, count):
        part = pl.ds(first, count)
        sem = sems.at[len(copies) + len(sent)]
        sent.append(pltpu.make_async_copy(out.at[:, part], out_hbm.at[:, part], sem))
        sent[-1].start()

    for f, ref in enumerate((trhs, arhs)):
        copies[f].wait()
        for a in range(nv):
            parts = [ref[a, pl.ds(16 * k, 16), :] for k in range(4)]
            for dest in range(plan.groups):
                out[dest, pl.ds((f * nv + a) * 16, 16), :] = window_of(parts, dest, BF16)
        send(f * plan.field_rows, plan.field_rows)

    for copy in copies[2:]:
        copy.wait()
    scr[...] = jnp.zeros(scr.shape, F32)
    for k in range(3):
        for a in range(nv):
            scr[k * nv + a, 0:nv, :] = jac[k, a].astype(F32)
    for a in range(nv):
        scr[3 * nv, a : a + 1, :] = second[a]
    quarter = [
        scr[pl.ds(plan.per * k, plan.per)].reshape(plan.per * 8, LANES) for k in range(4)
    ]
    live = _flag(lane < jnp.broadcast_to(count[...], (1, LANES)))
    scaled = weight[...] * live
    coarse = scaled.astype(BF16).astype(F32)
    panel = node[...] // PN
    upper = jnp.where(panel >= 8, 1, 0)
    table = [
        elem[...].astype(F32),
        (panel - 8 * upper).astype(F32),
        (node[...] - panel * PN + PN * upper).astype(F32),
        coarse,
        scaled - coarse,
    ]
    row = _iota((8, LANES), 0)
    zero = jnp.zeros((8, LANES), F32)
    table = [jnp.where(row == 6, line, 0.0) for line in table] + [zero] * (plan.per - len(table))
    table = jnp.concatenate(table, axis=0)
    for dest in range(plan.groups):
        block = window_of(quarter, dest, F32) + table
        first = 2 * plan.field_rows
        out[dest, pl.ds(first, plan.rows - first), :] = block.astype(BF16)
    send(2 * plan.field_rows, plan.rows - 2 * plan.field_rows)
    for copy in sent:
        copy.wait()


def coefficients(plan, penalty, coef, strength):
    point = _iota((NP, LANES), 0)
    ends = [point // 16, (point // 4) % 4, point % 4]
    faces = sum(_flag((e == 0) | (e == 3)) for e in ends)
    lane = _iota((16, LANES), 1)
    z = plan.own * plan.rank() - plan.halo + lane % plan.window
    inside = _flag((z >= 0) & (z < plan.span))
    for a in range(plan.nv):
        coef[a] = 0.5 - (0.5 * penalty[a]) * faces
        strength[a] = penalty[a] * inside


def sweeps(plan, states, source, table, matrix, transposed, coef, strength, steps=()):
    nv, nx, window = plan.nv, plan.nx, plan.window
    lane = _iota((16, LANES), 1)
    not_last = _flag(lane < LANES - window).astype(BF16)
    not_first = _flag(lane >= window).astype(BF16)
    none = jnp.zeros((16, LANES), BF16)
    rows = [strength[a].astype(BF16) for a in range(nv)]

    def plane(state, h, a, i):
        return state[h, a, pl.ds(16 * i, 16), :].astype(BF16)

    def flux(h, k, a, b):
        index, row = (k * nv + b, a) if transposed else (k * nv + a, b)
        line = table[h, index, pl.ds(row, 1), :]
        return jnp.broadcast_to(line, (16, LANES)).astype(BF16)

    for now, later in zip(states[:-1], states[1:]):
        for h in range(nx):
            if steps:
                steps.pop(0)()
            own = [[plane(now, h, b, i) for i in range(4)] for b in range(nv)]
            for a0 in range(0, nv, 2):
                stacks = []
                for a in (a0, a0 + 1):
                    parts = []
                    for k in range(3):
                        total = [None] * 4
                        for b in range(nv):
                            factor = flux(h, k, a, b)
                            for i in range(4):
                                term = own[b][i] * factor
                                total[i] = term if b == 0 else total[i] + term
                        parts += total
                    scaled = [own[a][i] * rows[a] for i in range(4)]
                    parts += [_roll(x, -window) * not_last for x in scaled]
                    parts += [_roll(x, window) * not_first for x in scaled]
                    parts += [_roll(x, -1) for x in scaled]
                    parts += [_roll(x, 1) for x in scaled]
                    parts.append(plane(now, h + 1, a, 0) * rows[a] if h + 1 < nx else none)
                    parts.append(plane(now, h - 1, a, 3) * rows[a] if h > 0 else none)
                    stacks.append(jnp.concatenate(parts, axis=0))
                product = _nn(matrix, jnp.concatenate(stacks, axis=1))
                for i, a in enumerate((a0, a0 + 1)):
                    value = coef[a] * now[h, a] + source[h, a]
                    later[h, a] = value + product[:, LANES * i : LANES * (i + 1)]


def chain(start, refs, count):
    return [start] + [refs[(i - count) % len(refs)] for i in range(count)]


def couple_rows(coupling):
    wide = coupling[...].astype(F32)
    pad = jnp.zeros((8 - SDOF, wide.shape[1]), F32)
    return jnp.concatenate([wide, pad], axis=0).astype(BF16)


def node_loads(plan, couple, values, hot, tile_hot, places, weights):
    lane = _iota((1, LANES), 1)
    place = lane % plan.window
    owned = _flag((place >= plan.halo) & (place < plan.halo + plan.own))
    picked = []
    for h in range(plan.nx):
        flow = _nn(couple, values[h]) * owned
        picked.append(_fold(_nn(_split(flow), places[h])))
    picked = jnp.concatenate(picked, axis=1) * weights[...]
    spread = [picked[c : c + 1] * tile_hot[...] for c in range(SDOF)]
    nodal = _fold(_nt(_split(jnp.concatenate(spread, axis=0)), hot[...]))
    left = _iota((8, LANES), 1) < PN
    low, high = [], []
    for t in range(plan.tiles):
        even, odd = nodal[16 * t : 16 * t + 8], nodal[16 * t + 8 : 16 * t + 16]
        low.append(jnp.where(left, even, _roll(odd, PN)))
        high.append(jnp.where(left, _roll(even, PN), odd))
    return low, high


def write_exchange(plan, low, high, solved, out):
    share, tiles = plan.groups // plan.held, plan.tiles
    row = _iota((8, LANES), 0)
    for dest in range(plan.ns):
        tail = jnp.zeros((8, LANES), F32)
        for t in range(tiles):
            part = pltpu.roll(solved[:, LANES * t : LANES * (t + 1)], (tiles + t - dest) % 8, 0)
            tail = jnp.where(row == tiles + t, part, tail)
        for panel in range(plan.held):
            q = dest * plan.held + panel
            block = tail
            for t in range(tiles):
                part = pltpu.roll(low[t] if q < 8 else high[t], (t - q) % 8, 0)
                block = jnp.where(row == t, part, block)
            block = block.astype(BF16)
            for g in range(panel * share, (panel + 1) * share):
                out[g * plan.ns + dest] = block


def summed(plan, received):
    totals = []
    for d in range(plan.ns):
        total = received[d].astype(F32)
        for g in range(1, plan.groups):
            total = total + received[g * plan.ns + d].astype(F32)
        totals.append(total)
    return totals


def read_own_loads(plan, received):
    totals = summed(plan, received)
    tiles = []
    for t in range(plan.tiles):
        rows = [x[t : t + 1] for x in totals] + [jnp.zeros((8 - plan.ns, LANES), F32)]
        tiles.append(jnp.concatenate(rows, axis=0))
    return jnp.concatenate(tiles, axis=1)


def push_force(
    plan, received, first, hot, tile_hot, places, weights, couple, rhs, shell_scr, scr, source
):
    span = plan.groups // plan.held
    for s in range(plan.ns):
        for panel in range(plan.held):
            block = received[panel * span * plan.ns + s].astype(F32)
            q = s * plan.held + panel
            for t in range(plan.tiles):
                line = block[first + t : first + t + 1]
                shell_scr[q : q + 1, LANES * t : LANES * (t + 1)] = line
    left = _iota((8, LANES), 1) < PN
    for t in range(plan.tiles):
        upper = shell_scr[0:8, LANES * t : LANES * (t + 1)]
        lower = shell_scr[8:16, LANES * t : LANES * (t + 1)]
        scr[2 * t] = jnp.where(left, upper, _roll(lower, PN))
        scr[2 * t + 1] = jnp.where(left, _roll(upper, PN), lower)
    for c in range(2 * plan.tiles, 8):
        scr[c] = jnp.zeros((8, LANES), F32)
    nodal = jnp.concatenate([scr[:, j, :] for j in range(8)], axis=0).astype(BF16)
    spread = _nn(nodal, hot[...])
    picked = sum(spread[8 * j : 8 * (j + 1)] * tile_hot[j : j + 1, :] for j in range(8))
    picked = picked * weights[...]
    twice = jnp.concatenate([couple, couple], axis=0)
    for h in range(plan.nx):
        part = picked[:, plan.slots * h : plan.slots * (h + 1)]
        dofs = _fold(_nt(_split(part), places[h]))
        push = _tn(twice, _split(dofs))
        for a in range(plan.nv):
            value = rhs[0, h, a].astype(F32) - push[NP * a : NP * (a + 1)]
            source[h, a] = 0.5 * value


def prepare_kernel(
    plan, deriv, load, inverse, penalty, forward, backward, solved, coef, strength
):
    coefficients(plan, penalty, coef, strength)
    mine = plan.rank() // (plan.groups // plan.held)
    p, c = _iota((NP, plan.depth), 0), _iota((NP, plan.depth), 1)
    j, l = (p // 4) % 4, p % 4

    def block(n, ok, shift):
        return ok & (c - (3 + n) * NP == p + shift)

    links = block(0, j == 3, -12) | block(1, j == 0, 12)
    links = links | block(2, l == 3, -3) | block(3, l == 0, 3)
    links = links | ((p >= 48) & (c - 7 * NP == p - 48))
    links = links | ((p < 16) & (c - 7 * NP - 16 == p))
    base = (0.5 * _flag(links)).astype(BF16)
    forward[...] = base
    backward[...] = base
    for k in range(3):
        part = -0.5 * deriv[k].astype(F32)
        forward[:, NP * k : NP * (k + 1)] = part.astype(BF16)
        backward[:, NP * k : NP * (k + 1)] = part.T.astype(BF16)
    solved[...] = _nt(member_rows(plan, load, mine).astype(BF16), inverse[mine])


def first_kernel(
    plan, received, backward, solved, coupling, coef, strength,
    adjoint, rhs, table, hot, tile_hot, places, weights, out,
    middle, source,
):
    nv, window, nx, ny = plan.nv, plan.window, plan.nx, plan.ny
    rank = plan.rank()
    masks = swap_masks(ny)
    for h in range(nx):
        for f in range(2):
            for a in range(nv):
                first = (f * nv + a) * 16
                parts = [received[y * nx + h, pl.ds(first, 16), :] for y in range(ny)]
                for k, part in enumerate(swap_groups(parts, masks)):
                    rhs[f, h, a, pl.ds(16 * k, 16), :] = part
        first = 2 * plan.field_rows
        count = plan.rows - first
        tails = [received[y * nx + h, pl.ds(first, count), :] for y in range(ny)]
        info = [x.astype(F32).reshape(plan.per, 8, LANES) for x in tails]
        pieces = [[] for _ in range(ny)]
        for r in range(0, count, 16):
            size = min(16, count - r)
            parts = [received[y * nx + h, pl.ds(first + r, size), :] for y in range(ny)]
            short = [(a[:size], b[:size]) for a, b in masks]
            for k, part in enumerate(swap_groups(parts, short)):
                pieces[k] += [part.astype(F32)[i : i + 8] for i in range(0, size, 8)]
        for k in range(ny):
            for i in range(plan.per):
                table[h, k * plan.per + i] = pieces[k][i]
        place = _iota((LANES, LANES), 0)
        row = _iota((8, LANES), 0)
        for y in range(ny):
            elem, tile, spot, coarse, fine = [info[y][i, 6:7, :] for i in range(5)]
            where = (elem - (plan.own * rank - plan.halo).astype(F32)).astype(jnp.int32)
            within = (where >= 0) & (where < window)
            target = jnp.where(within, where + y * window, -1)
            columns = pl.ds(LANES * y, LANES)
            places[h, :, columns] = _flag(place == target).astype(BF16)
            columns = pl.ds(plan.slots * h + LANES * y, LANES)
            weights[:, columns] = coarse + fine
            tile_hot[:, columns] = _flag(row == tile.astype(jnp.int32))
            hot[:, columns] = _flag(place == spot.astype(jnp.int32)).astype(BF16)

    for h in range(nx):
        for a in range(nv):
            source[h, a] = 0.5 * rhs[1, h, a].astype(F32)
    states = chain(source, [middle, adjoint], FSWEEP - 1)
    sweeps(plan, states, source, table, backward[...], True, coef, strength)
    values = [adjoint[h].reshape(nv * NP, LANES).astype(BF16) for h in range(nx)]
    low, high = node_loads(plan, couple_rows(coupling), values, hot, tile_hot, places, weights)
    write_exchange(plan, low, high, solved[...], out)


def second_kernel(
    plan, received, adjoint_in, rhs, table, hot, tile_hot, places, weights, forward, backward,
    coef, strength, coupling, load, shell_rhs, inverse,
    tangent, adjoint_last, out,
    first, second, source, scr, shell_scr,
):
    nv, nx = plan.nv, plan.nx
    rank = plan.rank()
    mine = rank // (plan.groups // plan.held)
    result = []
    steps = solve_steps(plan, received, load, shell_rhs, inverse, mine, result)
    couple = couple_rows(coupling)
    push_force(
        plan, received, plan.tiles, hot, tile_hot, places, weights, couple, rhs, shell_scr, scr,
        source,
    )
    states = chain(source, [first, tangent], FSWEEP - 1)
    sweeps(plan, states, source, table, forward[...], False, coef, strength, steps)
    for h in range(nx):
        for a in range(nv):
            extra = table[h, 3 * nv, a : a + 1, :] * tangent[h, a]
            source[h, a] = 0.5 * (rhs[1, h, a].astype(F32) + extra)
    states = chain(adjoint_in, [second, first], FSWEEP)
    sweeps(plan, states, source, table, backward[...], True, coef, strength)
    adjoint = states[-1]
    values = []
    for h in range(nx):
        value = adjoint[h].reshape(nv * NP, LANES).astype(BF16)
        adjoint_last[h] = value
        values.append(value)
    low, high = node_loads(plan, couple, values, hot, tile_hot, places, weights)
    write_exchange(plan, low, high, result[1], out)


def third_kernel(
    plan, received, tangent_in, adjoint_last, rhs, table, hot, tile_hot, places, weights, forward,
    coef, strength, coupling, load, shell_rhs, inverse,
    out,
    first, second, source, scr, shell_scr,
):
    nv, nx, ny, ns = plan.nv, plan.nx, plan.ny, plan.ns
    rank, share = plan.rank(), plan.groups // plan.held
    result = []
    steps = solve_steps(plan, received, load, shell_rhs, inverse, rank // share, result)
    push_force(
        plan, received, plan.tiles, hot, tile_hot, places, weights,
        couple_rows(coupling), rhs, shell_scr, scr, source,
    )
    states = chain(tangent_in, [first, second], FSWEEP)
    sweeps(plan, states, source, table, forward[...], False, coef, strength, steps)
    tangent = states[-1]
    shell = jnp.where(lax.rem(rank, share) == 0, result[0], result[1])
    tiles = [shell[:ns, LANES * t : LANES * (t + 1)] for t in range(plan.tiles)]
    tiles.append(jnp.zeros((plan.shell_rows - ns * plan.tiles, LANES), F32))
    shell = jnp.concatenate(tiles, axis=0).astype(BF16)
    for dest in range(plan.groups):
        out[dest, pl.ds(plan.field_rows, shell.shape[0]), :] = shell
    lane = _iota((16, LANES), 1)
    group = [_flag(lane // plan.own == n).astype(BF16) for n in range(plan.groups)]
    for h in range(nx):
        for a in range(nv):
            parts = [tangent[h, a, pl.ds(16 * i, 16), :].astype(BF16) for i in range(4)]
            parts += [adjoint_last[h, pl.ds(a * NP + 16 * i, 16), :] for i in range(4)]
            for y in range(ny):
                total = None
                for n in range(plan.groups):
                    shift = plan.own * n - plan.window * y - plan.halo
                    term = _roll(parts[n], shift) * group[n]
                    total = term if total is None else total + term
                out[y * nx + h, pl.ds(16 * a, 16), :] = total


def last_kernel(plan, received, tangent, adjoint, shell_tangent, shell_adjoint):
    share, ns = plan.groups // plan.held, plan.ns
    for panel in range(plan.held):
        for i, ref in enumerate((shell_adjoint, shell_tangent)):
            block = received[panel * share + i, pl.ds(plan.field_rows, plan.shell_rows), :]
            block = block.astype(F32)
            for t in range(plan.tiles):
                columns = pl.ds(LANES * t, LANES)
                ref[:, panel, columns] = block[ns * t : ns * (t + 1)]
    masks = swap_masks(plan.groups)
    for a in range(plan.nv):
        parts = [received[g, pl.ds(16 * a, 16), :] for g in range(plan.groups)]
        for n, part in enumerate(swap_groups(parts, masks)):
            (tangent, adjoint)[n // 4][a, pl.ds(16 * (n % 4), 16), :] = part


def call(kernel, plan, out_shape, scratch, copies, on_chip, in_hbm, scalars, limit=KERNEL_VMEM,
         out_space=pltpu.VMEM):
    vmem = pl.BlockSpec(memory_space=pltpu.VMEM)
    hbm = pl.BlockSpec(memory_space=pltpu.HBM)
    smem = pl.BlockSpec(memory_space=pltpu.SMEM)
    specs = [vmem] * len(on_chip) + [hbm] * len(in_hbm) + [smem] * len(scalars)
    scratch_shapes = [pltpu.VMEM(s, d) for s, d in scratch]
    if copies:
        scratch_shapes.append(pltpu.SemaphoreType.DMA((copies,)))
    return pl.pallas_call(
        functools.partial(kernel, plan),
        out_shape=[jax.ShapeDtypeStruct(s, d) for s, d in out_shape],
        in_specs=specs,
        out_specs=[pl.BlockSpec(memory_space=out_space)] * len(out_shape),
        scratch_shapes=scratch_shapes,
        compiler_params=pltpu.CompilerParams(vmem_limit_bytes=limit),
    )(*on_chip, *in_hbm, *scalars)


def slab_body(
    plan, tangent_rhs, adjoint_rhs, jacobians, deriv, penalty, second_order, coupling,
    shell_inverse, shell_load, shell_adjoint_rhs, iface_elem, iface_node, iface_weight,
    iface_count,
):
    nv, nx, ns, groups = plan.nv, plan.nx, plan.ns, plan.groups
    flow, everyone = ("fy", "fx"), ("fy", "fx", "st")
    state = ((nx, nv, NP, LANES), F32)
    coef = ((nv, NP, LANES), F32)
    scr = ((8, 8, LANES), F32)
    shell_rows = ((plan.panels, plan.width), F32)
    matrix = ((NP, plan.depth), BF16)

    def like(*arrays):
        return [(x.shape, x.dtype) for x in arrays]

    inputs = (
        tangent_rhs.reshape(nv, NP, LANES), adjoint_rhs.reshape(nv, NP, LANES),
        jacobians.reshape(3, nv, nv, LANES), second_order.reshape(nv, 1, LANES),
        iface_elem, iface_node, iface_weight, iface_count.reshape(1, 1),
    )
    (packed,) = call(
        pack_kernel, plan, [((groups, plan.rows, LANES), BF16)],
        like(*inputs)
        + [((4 * plan.per, 8, LANES), F32), ((groups, plan.rows, LANES), BF16)],
        len(inputs) + 3, (), inputs, (), None, pltpu.HBM,
    )
    slab = lax.all_to_all(packed, flow, split_axis=0, concat_axis=0, tiled=True)
    forward, backward, solved, coef, strength = call(
        prepare_kernel, plan,
        [matrix, matrix, ((8, plan.width), F32), coef, ((nv, 16, LANES), F32)],
        [], 0, (deriv, shell_load, shell_inverse), (), (penalty,),
    )
    adjoint, rhs, table, hot, tile_hot, places, weights, sent = call(
        first_kernel, plan,
        [
            state, ((2,) + state[0], BF16), ((nx, 4 * plan.per, 8, LANES), F32),
            ((LANES, nx * plan.slots), BF16), ((8, nx * plan.slots), F32),
            ((nx, LANES, plan.slots), BF16), ((1, nx * plan.slots), F32),
            ((groups * ns, 8, LANES), BF16),
        ],
        [state, state], 0, (slab, backward, solved, coupling, coef, strength), (), (),
    )
    received = lax.all_to_all(sent, everyone, split_axis=0, concat_axis=0, tiled=True)
    tangent, adjoint_last, sent = call(
        second_kernel, plan,
        [state, ((nx, nv * NP, LANES), BF16), ((groups * ns, 8, LANES), BF16)],
        [state, state, state, scr, shell_rows], 0,
        (
            received, adjoint, rhs, table, hot, tile_hot, places, weights, forward, backward,
            coef, strength, coupling, shell_load, shell_adjoint_rhs, shell_inverse,
        ),
        (), (),
    )
    received = lax.all_to_all(sent, everyone, split_axis=0, concat_axis=0, tiled=True)
    (sent,) = call(
        third_kernel, plan,
        [((groups, plan.field_rows + plan.shell_rows, LANES), BF16)],
        [state, state, state, scr, shell_rows], 0,
        (
            received, tangent, adjoint_last, rhs, table, hot, tile_hot, places, weights,
            forward, coef, strength, coupling, shell_load, shell_adjoint_rhs, shell_inverse,
        ),
        (), (),
    )
    received = lax.all_to_all(sent, flow, split_axis=0, concat_axis=0, tiled=True)
    shell_shape = (shell_load.shape, F32)
    tangent, adjoint, shell_tangent, shell_adjoint = call(
        last_kernel, plan, [((nv, NP, LANES), BF16)] * 2 + [shell_shape] * 2, [], 0,
        (received,), (), (),
    )
    return (
        tangent.reshape(tangent_rhs.shape), adjoint.reshape(adjoint_rhs.shape),
        shell_tangent, shell_adjoint,
    )


def body(*args):
    tangent_rhs, shell_inverse, shell_load, iface_elem = args[0], args[7], args[8], args[10]
    nx, ny, ns = (lax.axis_size(name) for name in ("fx", "fy", "st"))
    panels, width = shell_inverse.shape[0] * ns, shell_load.shape[2]
    if fits(nx, ny, ns, tangent_rhs.shape, iface_elem.shape[1], panels, width):
        plan = Plan(nx, ny, ns, tangent_rhs.shape[1], tangent_rhs.shape[5], panels, width)
        return slab_body(plan, *args)
    return halo_body(*args)


def solution(mesh):
    in_specs = (
        P("st", None, None, "fx", "fy", None),
        P("st", None, None, "fx", "fy", None),
        P(None, None, None, "fx", "fy", None),
        P(),
        P(),
        P(None, "fx", "fy", None),
        P(),
        P("st", None, None),
        P(None, "st", None),
        P(None, "st", None),
        P(("fx", "fy"), None),
        P(("fx", "fy"), None),
        P(("fx", "fy"), None),
        P(("fx", "fy")),
    )
    out_specs = (
        P("st", None, None, "fx", "fy", None),
        P("st", None, None, "fx", "fy", None),
        P(None, "st", None),
        P(None, "st", None),
    )
    return jax.shard_map(body, mesh=mesh, in_specs=in_specs, out_specs=out_specs, check_vma=False)
```
